128 devices in a mesh: qx: 16 (over z_hi, x, core), qy: 8 (over y, z_lo).
Axes of the slice: x: 4, y: 4, z: 4 (z_hi: 2, z_lo: 2; z = z_hi * 2 + z_lo), core: 2. Of those that a mesh axis runs over, the one named last changes fastest.
Arguments:
- image_tiles: bfloat16 [16, 8, 256, 64, 128], P('qx', 'qy'), may hold values from -6 to 6
- observed: bfloat16 [16, 8, 256, 64, 128], P('qx', 'qy'), may hold values from -6 to 6
- phases: float32 [16, 8, 256, 64, 128], P('qx', 'qy'), may hold values from -3.140625 to 3.140625
- interpolate: bfloat16 [64, 64], replicated, may hold values from -0.75 to 0.75
- local_weights: bfloat16 [16, 8, 2, 4, 4, 64, 64], P('qx', 'qy'), may hold values from -0.375 to 0.375
- merge_weights: bfloat16 [16, 8, 2, 4, 4, 64, 64], P('qx', 'qy'), may hold values from -0.375 to 0.375
- output_weight: bfloat16 [64, 64], replicated, may hold values from -0.75 to 0.75
Outputs:
- gradient: bfloat16 [16, 8, 256, 64, 128], P('qx', 'qy')
The draws below stay inside these ranges and needn't reach their ends.
All inputs are finite; a program needn't handle non-finite values.
Results may differ from the reference program's by a relative error of at most 0.02.
Values may be sent and summed in bfloat16 or wider, within the bound.
A program may use at most 128 MiB of HBM per device.

```python
import jax
import jax.numpy as jnp
from jax import lax

R = 64
L = 128
GROUPS = 256
LOCAL = 2
DIST = 2
N_QX = 16
N_QY = 8


def block_scale(stream_key, extent, shards, smallest, largest):
    gain = 1.0
    for dim, shards_of in shards:
        heights = jax.random.uniform(jax.random.fold_in(jax.random.fold_in(stream_key, 6), dim), (shards_of,), jnp.float32, smallest / len(shards), largest / len(shards))
        gain = gain * jnp.repeat(jnp.exp(heights), extent[dim] // shards_of).reshape((-1,) + (1,) * (len(extent) - 1 - dim))
    return gain


def normal_values(rng, shape, deviation, bound, cuts=(), kind=jnp.bfloat16):
    level = block_scale(rng, shape, cuts, -0.22, 0.18) if cuts else 1.0
    values = jax.random.normal(rng, shape, jnp.float32) * deviation * level
    return jnp.minimum(jnp.maximum(values, -bound), bound).astype(kind)


def setup_inputs(seed: int = 0) -> dict:
    streams_of = jax.random.split(jax.random.key(seed), 8)
    image_tiles = normal_values(streams_of[0], (N_QX, N_QY, GROUPS, R, L), 1.0, 6.0, ((0, 16), (1, 8)))
    observed = normal_values(streams_of[1], (N_QX, N_QY, GROUPS, R, L), 1.0, 6.0, ((0, 16), (1, 8)))
    phases = jnp.clip(jax.random.uniform(streams_of[2], (N_QX, N_QY, GROUPS, R, L), jnp.float32, -3.140625, 3.140625), -3.140625, 3.140625)
    interpolate = normal_values(streams_of[3], (R, R), R ** -0.5, 0.75)
    local_weights = normal_values(streams_of[4], (N_QX, N_QY, LOCAL, 4, 4, R, R), (4 * R) ** -0.5, 0.375, ((0, 16), (1, 8)))
    merge_weights = normal_values(streams_of[5], (N_QX, N_QY, DIST, 4, 4, R, R), (4 * R) ** -0.5, 0.375, ((0, 16), (1, 8)))
    output_weight = normal_values(streams_of[6], (R, R), R ** -0.5, 0.75)
    return dict(image_tiles=image_tiles, observed=observed, phases=phases, interpolate=interpolate, local_weights=local_weights, merge_weights=merge_weights, output_weight=output_weight)


def mixing(weight, data, form):
    return jnp.einsum(form, weight.astype(jnp.float32), data.astype(jnp.float32)).astype(jnp.bfloat16)


def level_bit(axis_count, level_index, depth):
    total_bits = axis_count.bit_length() - 1
    return (level_index * (total_bits - 1)) // max(depth - 1, 1)


def route_all(field, level_index):
    stride_x = 2 ** level_bit(N_QX, level_index, DIST)
    stride_y = 2 ** level_bit(N_QY, level_index, DIST)
    outer_x = N_QX // (2 * stride_x)
    outer_y = N_QY // (2 * stride_y)
    quarter_size = GROUPS // 4
    split_field = field.reshape(outer_x, 2, stride_x, outer_y, 2, stride_y, 2, 2, quarter_size, R, L)
    moved = jnp.transpose(split_field, (0, 6, 2, 3, 7, 5, 1, 4, 8, 9, 10))
    return moved.reshape(N_QX * N_QY, 4, quarter_size, R, L)


def reference(image_tiles, observed, phases, interpolate, local_weights, merge_weights, output_weight):
    device_count = N_QX * N_QY
    quarter_size = GROUPS // 4
    blocks = image_tiles.reshape(device_count, GROUPS, R, L)
    levels = local_weights.reshape(device_count, LOCAL, 4, 4, R, R)
    merges = merge_weights.reshape(device_count, DIST, 4, 4, R, R)

    def forward_local(packed):
        tiles, weights = packed
        current = mixing(interpolate, tiles, "op,gpl->gol")
        for section_index in range(LOCAL):
            stride_size = 4 ** section_index
            blocked = current.reshape(GROUPS // (4 * stride_size), 4, stride_size, R, L)
            current = mixing(weights[section_index], blocked, "kcor,acbrl->akbol").reshape(GROUPS, R, L)
        return current

    def merge_forward(packed):
        weight, pieces = packed
        return mixing(weight, pieces, "scor,chrl->shol")

    def merge_adjoint(packed):
        weight, pieces = packed
        return mixing(weight, pieces, "scor,shol->chrl")

    current = lax.map(forward_local, (blocks, levels)).reshape(N_QX, N_QY, GROUPS, R, L)
    for level_index in range(DIST):
        pieces = route_all(current, level_index)
        current = lax.map(merge_forward, (merges[:, level_index], pieces))
        current = current.reshape(N_QX, N_QY, GROUPS, R, L)
    merged_y = current

    cas_wave = jnp.cos(phases) + jnp.sin(phases)
    predicted = jnp.einsum("or,tvgrl->tvgol", output_weight.astype(jnp.float32), merged_y.astype(jnp.float32))
    residual = (cas_wave * predicted - observed.astype(jnp.float32)).astype(jnp.bfloat16)
    weighted = (cas_wave * residual.astype(jnp.float32)).astype(jnp.bfloat16)
    back = mixing(output_weight, weighted, "or,tvgol->tvgrl")

    for level_index in reversed(range(DIST)):
        pieces = back.reshape(device_count, 4, quarter_size, R, L)
        terms = lax.map(merge_adjoint, (merges[:, level_index], pieces))
        terms = terms.reshape(N_QX, N_QY, GROUPS, R, L)
        back = route_all(terms, level_index).reshape(N_QX, N_QY, GROUPS, R, L)

    def adjoint_local(packed):
        current, weights = packed
        for section_index in reversed(range(LOCAL)):
            stride_size = 4 ** section_index
            blocked = current.reshape(GROUPS // (4 * stride_size), 4, stride_size, R, L)
            current = mixing(weights[section_index], blocked, "kcor,akbol->acbrl").reshape(GROUPS, R, L)
        return mixing(interpolate, current, "op,gol->gpl")

    gradient = lax.map(adjoint_local, (back.reshape(device_count, GROUPS, R, L), levels))
    return gradient.reshape(N_QX, N_QY, GROUPS, R, L)
```

```python
import math

import jax
import jax.numpy as jnp
from jax import lax
from jax.sharding import PartitionSpec as P

CHUNKS = 2


def mixing(weight, data, form):
    return jnp.einsum(form, weight, data, preferred_element_type=jnp.float32).astype(jnp.bfloat16)


def level_bit(axis_count, level_index, depth):
    total_bits = axis_count.bit_length() - 1
    return level_index * (total_bits - 1) // max(depth - 1, 1)


def xor_order(x, axis, x_bit, y_bit):
    moved = jnp.moveaxis(x, axis, 0)
    shape = moved.shape
    pairs = moved.reshape((2, 2) + shape[1:])
    pairs = jnp.where(y_bit == 1, jnp.flip(pairs, 1), pairs)
    pairs = jnp.where(x_bit == 1, jnp.flip(pairs, 0), pairs)
    return jnp.moveaxis(pairs.reshape(shape), 0, axis)


def flip_send(value, flip, x_shift, y_shift):
    n_x = lax.axis_size("qx")
    n_y = lax.axis_size("qy")
    if flip == 2:
        pairs = [(i, i ^ (1 << x_shift)) for i in range(n_x)]
        return lax.ppermute(value, "qx", pairs)
    if flip == 1:
        pairs = [(i, i ^ (1 << y_shift)) for i in range(n_y)]
        return lax.ppermute(value, "qy", pairs)
    pairs = [
        (t * n_y + u, (t ^ (1 << x_shift)) * n_y + (u ^ (1 << y_shift)))
        for t in range(n_x)
        for u in range(n_y)
    ]
    return lax.ppermute(value, ("qx", "qy"), pairs)


def exchange(relative, x_shift, y_shift):
    got = [relative[0]] + [flip_send(relative[f], f, x_shift, y_shift) for f in (1, 2, 3)]
    return jnp.stack(got)


def local(image_tiles, observed, phases, interpolate, local_weights, merge_weights, output_weight):
    groups = image_tiles.shape[2]
    rank_size = image_tiles.shape[3]
    inner_boxes = image_tiles.shape[4]
    local_depth = local_weights.shape[2]
    quarter = groups // 4
    part = quarter // CHUNKS
    levels = local_weights[0, 0]
    merges = merge_weights[0, 0]
    n_x = lax.axis_size("qx")
    n_y = lax.axis_size("qy")
    t = lax.axis_index("qx")
    u = lax.axis_index("qy")
    shifts = [(level_bit(n_x, j, 2), level_bit(n_y, j, 2)) for j in range(2)]
    bits = [
        (jnp.right_shift(t, xs) & 1, jnp.right_shift(u, ys) & 1) for xs, ys in shifts
    ]

    w0 = xor_order(xor_order(merges[0], 1, *bits[0]), 0, *bits[1])
    w1 = xor_order(merges[1], 1, *bits[1])

    shape5 = (4, CHUNKS, part, rank_size, inner_boxes)
    image = xor_order(image_tiles[0, 0].reshape(shape5), 0, *bits[0])
    obs = observed[0, 0].reshape(shape5)
    cas_all = jnp.float32(math.sqrt(2.0)) * jnp.sin(
        phases[0, 0].reshape(shape5) + jnp.float32(math.pi / 4)
    )

    results = []
    for m in range(CHUNKS):
        cur = mixing(interpolate, image[:, m], "op,qjpl->qjol")
        for i in range(local_depth):
            b = 4**i
            blk = cur.reshape(4, part // (4 * b), 4, b, rank_size, inner_boxes)
            cur = mixing(levels[i], blk, "kcor,qacerl->qakeol").reshape(
                4, part, rank_size, inner_boxes
            )
        pieces = exchange(cur, *shifts[0])
        cur = mixing(w0, pieces, "scor,cjrl->sjol")
        pieces = exchange(cur, *shifts[1])
        merged_y = mixing(w1, pieces, "scor,cjrl->sjol")
        cas_wave = cas_all[:, m]
        predicted = jnp.einsum(
            "or,sjrl->sjol", output_weight, merged_y, preferred_element_type=jnp.float32
        )
        residual = (cas_wave * predicted - obs[:, m].astype(jnp.float32)).astype(jnp.bfloat16)
        weighted = (cas_wave * residual.astype(jnp.float32)).astype(jnp.bfloat16)
        back = mixing(output_weight, weighted, "or,sjol->sjrl")
        terms = mixing(w1, back, "scor,sjol->cjrl")
        back = exchange(terms, *shifts[1])
        terms = mixing(w0, back, "scor,sjol->cjrl")
        cur = exchange(terms, *shifts[0])
        for i in reversed(range(local_depth)):
            b = 4**i
            blk = cur.reshape(4, part // (4 * b), 4, b, rank_size, inner_boxes)
            cur = mixing(levels[i], blk, "kcor,qakeol->qacerl").reshape(
                4, part, rank_size, inner_boxes
            )
        results.append(mixing(interpolate, cur, "op,qjol->qjpl"))
    gradient = xor_order(jnp.stack(results, 1), 0, *bits[0])
    return gradient.reshape(groups, rank_size, inner_boxes)[None, None]


def solution(mesh):
    placed = (
        P("qx", "qy", None, None, None),
        P("qx", "qy", None, None, None),
        P("qx", "qy", None, None, None),
        P(),
        P("qx", "qy", None, None, None, None, None),
        P("qx", "qy", None, None, None, None, None),
        P(),
    )
    return jax.shard_map(
        local,
        mesh=mesh,
        in_specs=placed,
        out_specs=P("qx", "qy", None, None, None),
        check_vma=False,
    )
```

```python
import math

import jax
import jax.numpy as jnp
from jax import lax
from jax.sharding import PartitionSpec as P

CHUNKS = 2


def mixing(weight, data, form):
    return jnp.einsum(form, weight, data, preferred_element_type=jnp.float32).astype(jnp.bfloat16)


def level_bit(axis_count, level_index, depth):
    total_bits = axis_count.bit_length() - 1
    return level_index * (total_bits - 1) // max(depth - 1, 1)


def xor_order(x, axis, x_bit, y_bit):
    moved = jnp.moveaxis(x, axis, 0)
    shape = moved.shape
    pairs = moved.reshape((2, 2) + shape[1:])
    pairs = jnp.where(y_bit == 1, jnp.flip(pairs, 1), pairs)
    pairs = jnp.where(x_bit == 1, jnp.flip(pairs, 0), pairs)
    return jnp.moveaxis(pairs.reshape(shape), 0, axis)


def flip_send(value, flip, x_shift, y_shift):
    n_x = lax.axis_size("qx")
    n_y = lax.axis_size("qy")
    if flip == 2:
        pairs = [(i, i ^ (1 << x_shift)) for i in range(n_x)]
        return lax.ppermute(value, "qx", pairs)
    if flip == 1:
        pairs = [(i, i ^ (1 << y_shift)) for i in range(n_y)]
        return lax.ppermute(value, "qy", pairs)
    pairs = [
        (t * n_y + u, (t ^ (1 << x_shift)) * n_y + (u ^ (1 << y_shift)))
        for t in range(n_x)
        for u in range(n_y)
    ]
    return lax.ppermute(value, ("qx", "qy"), pairs)


def exchange(relative, x_shift, y_shift):
    got = [relative[0]] + [flip_send(relative[f], f, x_shift, y_shift) for f in (1, 2, 3)]
    return jnp.stack(got)


def local(image_tiles, observed, phases, interpolate, local_weights, merge_weights, output_weight):
    groups = image_tiles.shape[2]
    rank_size = image_tiles.shape[3]
    inner_boxes = image_tiles.shape[4]
    local_depth = local_weights.shape[2]
    quarter = groups // 4
    part = quarter // CHUNKS
    levels = local_weights[0, 0]
    merges = merge_weights[0, 0]
    n_x = lax.axis_size("qx")
    n_y = lax.axis_size("qy")
    t = lax.axis_index("qx")
    u = lax.axis_index("qy")
    shifts = [(level_bit(n_x, j, 2), level_bit(n_y, j, 2)) for j in range(2)]
    bits = [
        (jnp.right_shift(t, xs) & 1, jnp.right_shift(u, ys) & 1) for xs, ys in shifts
    ]

    w0 = xor_order(xor_order(merges[0], 1, *bits[0]), 0, *bits[1])
    w1 = xor_order(merges[1], 1, *bits[1])

    shape5 = (4, CHUNKS, part, rank_size, inner_boxes)
    image = image_tiles[0, 0].reshape(shape5)
    obs = observed[0, 0].reshape(shape5)
    cas_all = jnp.float32(math.sqrt(2.0)) * jnp.sin(
        phases[0, 0].reshape(shape5) + jnp.float32(math.pi / 4)
    )
    k0 = 2 * bits[0][0] + bits[0][1]

    def local_forward(tiles):
        cur = mixing(interpolate, tiles, "op,jpl->jol")
        for i in range(local_depth):
            b = 4**i
            blk = cur.reshape(part // (4 * b), 4, b, rank_size, inner_boxes)
            cur = mixing(levels[i], blk, "kcor,acerl->akeol").reshape(
                part, rank_size, inner_boxes
            )
        return cur

    def local_adjoint(cur):
        for i in reversed(range(local_depth)):
            b = 4**i
            blk = cur.reshape(part // (4 * b), 4, b, rank_size, inner_boxes)
            cur = mixing(levels[i], blk, "kcor,akeol->acerl").reshape(
                part, rank_size, inner_boxes
            )
        return mixing(interpolate, cur, "op,jol->jpl")

    gradient = jnp.zeros(shape5, jnp.bfloat16)
    for m in range(CHUNKS):
        chunk = image[:, m]
        coef = [
            local_forward(lax.dynamic_index_in_dim(chunk, k0 ^ f, 0, keepdims=False))
            for f in range(4)
        ]
        pieces = exchange(jnp.stack(coef), *shifts[0])
        cur = mixing(w0, pieces, "scor,cjrl->sjol")
        pieces = exchange(cur, *shifts[1])
        merged_y = mixing(w1, pieces, "scor,cjrl->sjol")
        cas_wave = cas_all[:, m]
        predicted = jnp.einsum(
            "or,sjrl->sjol", output_weight, merged_y, preferred_element_type=jnp.float32
        )
        residual = (cas_wave * predicted - obs[:, m].astype(jnp.float32)).astype(jnp.bfloat16)
        weighted = (cas_wave * residual.astype(jnp.float32)).astype(jnp.bfloat16)
        back = mixing(output_weight, weighted, "or,sjol->sjrl")
        terms = mixing(w1, back, "scor,sjol->cjrl")
        back = exchange(terms, *shifts[1])
        terms = mixing(w0, back, "scor,sjol->cjrl")
        back = exchange(terms, *shifts[0])
        for f in range(4):
            piece = local_adjoint(back[f])
            gradient = lax.dynamic_update_slice(
                gradient, piece[None, None], (k0 ^ f, m, 0, 0, 0)
            )
    return gradient.reshape(groups, rank_size, inner_boxes)[None, None]


def solution(mesh):
    placed = (
        P("qx", "qy", None, None, None),
        P("qx", "qy", None, None, None),
        P("qx", "qy", None, None, None),
        P(),
        P("qx", "qy", None, None, None, None, None),
        P("qx", "qy", None, None, None, None, None),
        P(),
    )
    return jax.shard_map(
        local,
        mesh=mesh,
        in_specs=placed,
        out_specs=P("qx", "qy", None, None, None),
        check_vma=False,
    )
```

```python
import math

import jax
import jax.numpy as jnp
from jax import lax
from jax.sharding import PartitionSpec as P

CHUNKS = 2


def mixing(weight, data, form):
    return jnp.einsum(form, weight, data, preferred_element_type=jnp.float32).astype(jnp.bfloat16)


def level_bit(axis_count, level_index, depth):
    total_bits = axis_count.bit_length() - 1
    return level_index * (total_bits - 1) // max(depth - 1, 1)


def xor_order(x, axis, x_bit, y_bit):
    moved = jnp.moveaxis(x, axis, 0)
    shape = moved.shape
    pairs = moved.reshape((2, 2) + shape[1:])
    pairs = jnp.where(y_bit == 1, jnp.flip(pairs, 1), pairs)
    pairs = jnp.where(x_bit == 1, jnp.flip(pairs, 0), pairs)
    return jnp.moveaxis(pairs.reshape(shape), 0, axis)


PI_HI = 3.140625
PI_LO = math.pi - 3.140625


def cas(phase):
    x = phase + jnp.float32(math.pi / 4)
    n = jnp.round(x * jnp.float32(1 / math.pi))
    y = (x - n * jnp.float32(PI_HI)) - n * jnp.float32(PI_LO)
    y2 = y * y
    poly = jnp.float32(-1 / 39916800)
    for k in (9, 7, 5, 3):
        poly = poly * y2 + jnp.float32((-1) ** ((k - 1) // 2) / math.factorial(k))
    sine = y + y * y2 * poly
    odd = jnp.abs(n) == 1
    scale = jnp.where(odd, jnp.float32(-math.sqrt(2.0)), jnp.float32(math.sqrt(2.0)))
    return scale * sine


def flip_send(value, flip, x_shift, y_shift):
    n_x = lax.axis_size("qx")
    n_y = lax.axis_size("qy")
    if flip == 2:
        pairs = [(i, i ^ (1 << x_shift)) for i in range(n_x)]
        return lax.ppermute(value, "qx", pairs)
    if flip == 1:
        pairs = [(i, i ^ (1 << y_shift)) for i in range(n_y)]
        return lax.ppermute(value, "qy", pairs)
    pairs = [
        (t * n_y + u, (t ^ (1 << x_shift)) * n_y + (u ^ (1 << y_shift)))
        for t in range(n_x)
        for u in range(n_y)
    ]
    return lax.ppermute(value, ("qx", "qy"), pairs)


def exchange(relative, x_shift, y_shift):
    got = [relative[0]] + [flip_send(relative[f], f, x_shift, y_shift) for f in (1, 2, 3)]
    return jnp.stack(got)


def local(image_tiles, observed, phases, interpolate, local_weights, merge_weights, output_weight):
    groups = image_tiles.shape[2]
    rank_size = image_tiles.shape[3]
    inner_boxes = image_tiles.shape[4]
    local_depth = local_weights.shape[2]
    quarter = groups // 4
    part = quarter // CHUNKS
    levels = local_weights[0, 0]
    merges = merge_weights[0, 0]
    n_x = lax.axis_size("qx")
    n_y = lax.axis_size("qy")
    t = lax.axis_index("qx")
    u = lax.axis_index("qy")
    shifts = [(level_bit(n_x, j, 2), level_bit(n_y, j, 2)) for j in range(2)]
    bits = [
        (jnp.right_shift(t, xs) & 1, jnp.right_shift(u, ys) & 1) for xs, ys in shifts
    ]

    w0 = xor_order(xor_order(merges[0], 1, *bits[0]), 0, *bits[1])
    w1 = xor_order(merges[1], 1, *bits[1])

    shape5 = (4, CHUNKS, part, rank_size, inner_boxes)
    image = image_tiles[0, 0].reshape(shape5)
    obs = observed[0, 0].reshape(shape5)
    wave = phases[0, 0].reshape(shape5)
    k0 = 2 * bits[0][0] + bits[0][1]

    def local_forward(tiles):
        cur = mixing(interpolate, tiles, "op,jpl->jol")
        for i in range(local_depth):
            b = 4**i
            blk = cur.reshape(part // (4 * b), 4, b, rank_size, inner_boxes)
            cur = mixing(levels[i], blk, "kcor,acerl->akeol").reshape(
                part, rank_size, inner_boxes
            )
        return cur

    def local_adjoint(cur):
        for i in reversed(range(local_depth)):
            b = 4**i
            blk = cur.reshape(part // (4 * b), 4, b, rank_size, inner_boxes)
            cur = mixing(levels[i], blk, "kcor,akeol->acerl").reshape(
                part, rank_size, inner_boxes
            )
        return mixing(interpolate, cur, "op,jol->jpl")

    gradient = jnp.zeros(shape5, jnp.bfloat16)
    for m in range(CHUNKS):
        chunk = image[:, m]
        coef = [
            local_forward(lax.dynamic_index_in_dim(chunk, k0 ^ f, 0, keepdims=False))
            for f in range(4)
        ]
        pieces = exchange(jnp.stack(coef), *shifts[0])
        cur = mixing(w0, pieces, "scor,cjrl->sjol")
        pieces = exchange(cur, *shifts[1])
        merged_y = mixing(w1, pieces, "scor,cjrl->sjol")
        cas_wave = cas(wave[:, m])
        predicted = jnp.einsum(
            "or,sjrl->sjol", output_weight, merged_y, preferred_element_type=jnp.float32
        )
        residual = (cas_wave * predicted - obs[:, m].astype(jnp.float32)).astype(jnp.bfloat16)
        weighted = (cas_wave * residual.astype(jnp.float32)).astype(jnp.bfloat16)
        back = mixing(output_weight, weighted, "or,sjol->sjrl")
        terms = mixing(w1, back, "scor,sjol->cjrl")
        back = exchange(terms, *shifts[1])
        terms = mixing(w0, back, "scor,sjol->cjrl")
        back = exchange(terms, *shifts[0])
        for f in range(4):
            piece = local_adjoint(back[f])
            gradient = lax.dynamic_update_slice(
                gradient, piece[None, None], (k0 ^ f, m, 0, 0, 0)
            )
    return gradient.reshape(groups, rank_size, inner_boxes)[None, None]


def solution(mesh):
    placed = (
        P("qx", "qy", None, None, None),
        P("qx", "qy", None, None, None),
        P("qx", "qy", None, None, None),
        P(),
        P("qx", "qy", None, None, None, None, None),
        P("qx", "qy", None, None, None, None, None),
        P(),
    )
    return jax.shard_map(
        local,
        mesh=mesh,
        in_specs=placed,
        out_specs=P("qx", "qy", None, None, None),
        check_vma=False,
    )
```

```python
import math

import jax
import jax.numpy as jnp
from jax import lax
from jax.sharding import PartitionSpec as P

CHUNKS = 4


def mixing(weight, data, form):
    return jnp.einsum(form, weight, data, preferred_element_type=jnp.float32).astype(jnp.bfloat16)


def level_bit(axis_count, level_index, depth):
    total_bits = axis_count.bit_length() - 1
    return level_index * (total_bits - 1) // max(depth - 1, 1)


def xor_order(x, axis, x_bit, y_bit):
    moved = jnp.moveaxis(x, axis, 0)
    shape = moved.shape
    pairs = moved.reshape((2, 2) + shape[1:])
    pairs = jnp.where(y_bit == 1, jnp.flip(pairs, 1), pairs)
    pairs = jnp.where(x_bit == 1, jnp.flip(pairs, 0), pairs)
    return jnp.moveaxis(pairs.reshape(shape), 0, axis)


PI_HI = 3.140625
PI_LO = math.pi - 3.140625


def cas(phase):
    x = phase + jnp.float32(math.pi / 4)
    n = jnp.round(x * jnp.float32(1 / math.pi))
    y = (x - n * jnp.float32(PI_HI)) - n * jnp.float32(PI_LO)
    y2 = y * y
    poly = jnp.float32(-1 / 39916800)
    for k in (9, 7, 5, 3):
        poly = poly * y2 + jnp.float32((-1) ** ((k - 1) // 2) / math.factorial(k))
    sine = y + y * y2 * poly
    odd = jnp.abs(n) == 1
    scale = jnp.where(odd, jnp.float32(-math.sqrt(2.0)), jnp.float32(math.sqrt(2.0)))
    return scale * sine


def flip_send(value, flip, x_shift, y_shift):
    n_x = lax.axis_size("qx")
    n_y = lax.axis_size("qy")
    if flip == 2:
        pairs = [(i, i ^ (1 << x_shift)) for i in range(n_x)]
        return lax.ppermute(value, "qx", pairs)
    if flip == 1:
        pairs = [(i, i ^ (1 << y_shift)) for i in range(n_y)]
        return lax.ppermute(value, "qy", pairs)
    pairs = [
        (t * n_y + u, (t ^ (1 << x_shift)) * n_y + (u ^ (1 << y_shift)))
        for t in range(n_x)
        for u in range(n_y)
    ]
    return lax.ppermute(value, ("qx", "qy"), pairs)


def exchange(relative, x_shift, y_shift):
    got = [relative[0]] + [flip_send(relative[f], f, x_shift, y_shift) for f in (1, 2, 3)]
    return jnp.stack(got)


def local(image_tiles, observed, phases, interpolate, local_weights, merge_weights, output_weight):
    groups = image_tiles.shape[2]
    rank_size = image_tiles.shape[3]
    inner_boxes = image_tiles.shape[4]
    local_depth = local_weights.shape[2]
    quarter = groups // 4
    part = quarter // CHUNKS
    levels = local_weights[0, 0]
    merges = merge_weights[0, 0]
    n_x = lax.axis_size("qx")
    n_y = lax.axis_size("qy")
    t = lax.axis_index("qx")
    u = lax.axis_index("qy")
    shifts = [(level_bit(n_x, j, 2), level_bit(n_y, j, 2)) for j in range(2)]
    bits = [
        (jnp.right_shift(t, xs) & 1, jnp.right_shift(u, ys) & 1) for xs, ys in shifts
    ]

    w0 = xor_order(xor_order(merges[0], 1, *bits[0]), 0, *bits[1])
    w1 = xor_order(merges[1], 1, *bits[1])

    shape5 = (4, CHUNKS, part, rank_size, inner_boxes)
    image = image_tiles[0, 0].reshape(shape5)
    obs = observed[0, 0].reshape(shape5)
    wave = phases[0, 0].reshape(shape5)
    k0 = 2 * bits[0][0] + bits[0][1]

    def local_forward(tiles):
        cur = mixing(interpolate, tiles, "op,jpl->jol")
        for i in range(local_depth):
            b = 4**i
            blk = cur.reshape(part // (4 * b), 4, b, rank_size, inner_boxes)
            cur = mixing(levels[i], blk, "kcor,acerl->akeol").reshape(
                part, rank_size, inner_boxes
            )
        return cur

    def local_adjoint(cur):
        for i in reversed(range(local_depth)):
            b = 4**i
            blk = cur.reshape(part // (4 * b), 4, b, rank_size, inner_boxes)
            cur = mixing(levels[i], blk, "kcor,akeol->acerl").reshape(
                part, rank_size, inner_boxes
            )
        return mixing(interpolate, cur, "op,jol->jpl")

    gradient = jnp.zeros(shape5, jnp.bfloat16)
    for m in range(CHUNKS):
        chunk = image[:, m]
        coef = [
            local_forward(lax.dynamic_index_in_dim(chunk, k0 ^ f, 0, keepdims=False))
            for f in range(4)
        ]
        pieces = exchange(jnp.stack(coef), *shifts[0])
        cur = mixing(w0, pieces, "scor,cjrl->sjol")
        pieces = exchange(cur, *shifts[1])
        merged_y = mixing(w1, pieces, "scor,cjrl->sjol")
        cas_wave = cas(wave[:, m])
        predicted = jnp.einsum(
            "or,sjrl->sjol", output_weight, merged_y, preferred_element_type=jnp.float32
        )
        residual = (cas_wave * predicted - obs[:, m].astype(jnp.float32)).astype(jnp.bfloat16)
        weighted = (cas_wave * residual.astype(jnp.float32)).astype(jnp.bfloat16)
        back = mixing(output_weight, weighted, "or,sjol->sjrl")
        terms = mixing(w1, back, "scor,sjol->cjrl")
        back = exchange(terms, *shifts[1])
        terms = mixing(w0, back, "scor,sjol->cjrl")
        back = exchange(terms, *shifts[0])
        for f in range(4):
            piece = local_adjoint(back[f])
            gradient = lax.dynamic_update_slice(
                gradient, piece[None, None], (k0 ^ f, m, 0, 0, 0)
            )
    return gradient.reshape(groups, rank_size, inner_boxes)[None, None]


def solution(mesh):
    placed = (
        P("qx", "qy", None, None, None),
        P("qx", "qy", None, None, None),
        P("qx", "qy", None, None, None),
        P(),
        P("qx", "qy", None, None, None, None, None),
        P("qx", "qy", None, None, None, None, None),
        P(),
    )
    return jax.shard_map(
        local,
        mesh=mesh,
        in_specs=placed,
        out_specs=P("qx", "qy", None, None, None),
        check_vma=False,
    )
```

```python
import math

import jax
import jax.numpy as jnp
from jax import lax
from jax.experimental import pallas as pl
from jax.experimental.pallas import tpu as pltpu
from jax.sharding import PartitionSpec as P

CHUNKS = 2


def mixing(weight, data, form):
    return jnp.einsum(form, weight, data, preferred_element_type=jnp.float32).astype(jnp.bfloat16)


def level_bit(axis_count, level_index, depth):
    total_bits = axis_count.bit_length() - 1
    return level_index * (total_bits - 1) // max(depth - 1, 1)


def xor_order(x, axis, x_bit, y_bit):
    moved = jnp.moveaxis(x, axis, 0)
    shape = moved.shape
    pairs = moved.reshape((2, 2) + shape[1:])
    pairs = jnp.where(y_bit == 1, jnp.flip(pairs, 1), pairs)
    pairs = jnp.where(x_bit == 1, jnp.flip(pairs, 0), pairs)
    return jnp.moveaxis(pairs.reshape(shape), 0, axis)


PI_HI = 3.140625
PI_LO = math.pi - 3.140625


def cas(phase):
    x = phase + jnp.float32(math.pi / 4)
    n = jnp.round(x * jnp.float32(1 / math.pi))
    y = (x - n * jnp.float32(PI_HI)) - n * jnp.float32(PI_LO)
    y2 = y * y
    poly = jnp.float32(-1 / 39916800)
    for k in (9, 7, 5, 3):
        poly = poly * y2 + jnp.float32((-1) ** ((k - 1) // 2) / math.factorial(k))
    sine = y + y * y2 * poly
    odd = jnp.abs(n) == 1
    scale = jnp.where(odd, jnp.float32(-math.sqrt(2.0)), jnp.float32(math.sqrt(2.0)))
    return scale * sine


def flip_send(value, flip, x_shift, y_shift):
    n_x = lax.axis_size("qx")
    n_y = lax.axis_size("qy")
    if flip == 2:
        pairs = [(i, i ^ (1 << x_shift)) for i in range(n_x)]
        return lax.ppermute(value, "qx", pairs)
    if flip == 1:
        pairs = [(i, i ^ (1 << y_shift)) for i in range(n_y)]
        return lax.ppermute(value, "qy", pairs)
    pairs = [
        (t * n_y + u, (t ^ (1 << x_shift)) * n_y + (u ^ (1 << y_shift)))
        for t in range(n_x)
        for u in range(n_y)
    ]
    return lax.ppermute(value, ("qx", "qy"), pairs)


def exchange(relative, x_shift, y_shift):
    return [relative[0]] + [flip_send(relative[f], f, x_shift, y_shift) for f in (1, 2, 3)]


def cas_kernel(phase):
    x = phase + jnp.float32(math.pi / 4)
    n = jnp.floor(x * jnp.float32(1 / math.pi) + jnp.float32(0.5))
    y = (x - n * jnp.float32(PI_HI)) - n * jnp.float32(PI_LO)
    y2 = y * y
    poly = jnp.float32(-1 / 39916800)
    for k in (9, 7, 5, 3):
        poly = poly * y2 + jnp.float32((-1) ** ((k - 1) // 2) / math.factorial(k))
    sine = y + y * y2 * poly
    half = n * jnp.float32(0.5)
    odd = half != jnp.floor(half)
    scale = jnp.where(odd, jnp.float32(-math.sqrt(2.0)), jnp.float32(math.sqrt(2.0)))
    return scale * sine


def output_stage_kernel(p0, p1, p2, p3, ph_ref, obs_ref, w_ref, wt_ref, o_ref, ot_ref,
                        t0, t1, t2, t3):
    rows = 4 * p0.shape[1]
    pieces = (p0, p1, p2, p3)
    terms = (t0, t1, t2, t3)

    def body(j, carry):
        stacked = jnp.concatenate([p[j] for p in pieces], axis=0)
        merged = jnp.dot(w_ref[...], stacked, preferred_element_type=jnp.float32)
        merged = merged.astype(jnp.bfloat16)
        predicted = jnp.dot(o_ref[...], merged, preferred_element_type=jnp.float32)
        wave = cas_kernel(ph_ref[:, j].reshape(rows, -1))
        seen = obs_ref[:, j].reshape(rows, -1).astype(jnp.float32)
        residual = (wave * predicted - seen).astype(jnp.bfloat16)
        weighted = (wave * residual.astype(jnp.float32)).astype(jnp.bfloat16)
        back = jnp.dot(ot_ref[...], weighted, preferred_element_type=jnp.float32)
        back = back.astype(jnp.bfloat16)
        out = jnp.dot(wt_ref[...], back, preferred_element_type=jnp.float32)
        out = out.astype(jnp.bfloat16)
        size = p0.shape[1]
        for f in range(4):
            terms[f][j] = out[f * size:(f + 1) * size]
        return carry

    lax.fori_loop(0, p0.shape[0], body, 0)


def output_stage(pieces, wave, obs, chunk, w_mat, w_t, o_mat, o_t, step=8):
    part, rank_size, inner_boxes = pieces[0].shape
    piece_spec = pl.BlockSpec((step, rank_size, inner_boxes), lambda i: (i, 0, 0))
    field_spec = pl.BlockSpec(
        (4, None, step, rank_size, inner_boxes), lambda i: (0, chunk, i, 0, 0)
    )
    square = pl.BlockSpec(w_mat.shape, lambda i: (0, 0))
    flops = 4 * 2 * part * inner_boxes * w_mat.shape[0] * w_mat.shape[1]
    moved = part * rank_size * inner_boxes * 4 * (2 + 4 + 2 + 2)
    return pl.pallas_call(
        output_stage_kernel,
        grid=(part // step,),
        in_specs=[piece_spec] * 4 + [field_spec, field_spec] + [square] * 4,
        out_specs=[piece_spec] * 4,
        out_shape=[jax.ShapeDtypeStruct(pieces[0].shape, jnp.bfloat16)] * 4,
        cost_estimate=pl.CostEstimate(
            flops=flops, bytes_accessed=moved, transcendentals=0
        ),
    )(*pieces, wave, obs, w_mat, w_t, o_mat, o_t)


def local(image_tiles, observed, phases, interpolate, local_weights, merge_weights, output_weight):
    groups = image_tiles.shape[2]
    rank_size = image_tiles.shape[3]
    inner_boxes = image_tiles.shape[4]
    local_depth = local_weights.shape[2]
    quarter = groups // 4
    part = quarter // CHUNKS
    levels = local_weights[0, 0]
    merges = merge_weights[0, 0]
    n_x = lax.axis_size("qx")
    n_y = lax.axis_size("qy")
    t = lax.axis_index("qx")
    u = lax.axis_index("qy")
    shifts = [(level_bit(n_x, j, 2), level_bit(n_y, j, 2)) for j in range(2)]
    bits = [
        (jnp.right_shift(t, xs) & 1, jnp.right_shift(u, ys) & 1) for xs, ys in shifts
    ]

    w0 = xor_order(xor_order(merges[0], 1, *bits[0]), 0, *bits[1])
    w1 = xor_order(merges[1], 1, *bits[1])
    w1_mat = jnp.transpose(w1, (0, 2, 1, 3)).reshape(4 * rank_size, 4 * rank_size)
    w1_t = w1_mat.T
    eye = jnp.eye(4, dtype=output_weight.dtype)
    ow_mat = jnp.einsum("st,or->sotr", eye, output_weight).reshape(4 * rank_size, 4 * rank_size)
    ow_t = ow_mat.T

    shape5 = (4, CHUNKS, part, rank_size, inner_boxes)
    image = image_tiles[0, 0].reshape(shape5)
    obs = observed[0, 0].reshape(shape5)
    wave = phases[0, 0].reshape(shape5)
    k0 = 2 * bits[0][0] + bits[0][1]

    def local_forward(tiles):
        cur = mixing(interpolate, tiles, "op,jpl->jol")
        for i in range(local_depth):
            b = 4**i
            blk = cur.reshape(part // (4 * b), 4, b, rank_size, inner_boxes)
            cur = mixing(levels[i], blk, "kcor,acerl->akeol").reshape(
                part, rank_size, inner_boxes
            )
        return cur

    def local_adjoint(cur):
        for i in reversed(range(local_depth)):
            b = 4**i
            blk = cur.reshape(part // (4 * b), 4, b, rank_size, inner_boxes)
            cur = mixing(levels[i], blk, "kcor,akeol->acerl").reshape(
                part, rank_size, inner_boxes
            )
        return mixing(interpolate, cur, "op,jol->jpl")

    gradient = jnp.zeros(shape5, jnp.bfloat16)
    for m in range(CHUNKS):
        chunk = image[:, m]
        coef = [
            local_forward(lax.dynamic_index_in_dim(chunk, k0 ^ f, 0, keepdims=False))
            for f in range(4)
        ]
        pieces = exchange(coef, *shifts[0])
        cur = mixing(w0, jnp.stack(pieces), "scor,cjrl->sjol")
        pieces = exchange(cur, *shifts[1])
        terms = output_stage(pieces, wave, obs, m, w1_mat, w1_t, ow_mat, ow_t)
        back = exchange(terms, *shifts[1])
        terms = mixing(w0, jnp.stack(back), "scor,sjol->cjrl")
        back = exchange(terms, *shifts[0])
        for f in range(4):
            piece = local_adjoint(back[f])
            gradient = lax.dynamic_update_slice(
                gradient, piece[None, None], (k0 ^ f, m, 0, 0, 0)
            )
    return gradient.reshape(groups, rank_size, inner_boxes)[None, None]


def solution(mesh):
    placed = (
        P("qx", "qy", None, None, None),
        P("qx", "qy", None, None, None),
        P("qx", "qy", None, None, None),
        P(),
        P("qx", "qy", None, None, None, None, None),
        P("qx", "qy", None, None, None, None, None),
        P(),
    )
    return jax.shard_map(
        local,
        mesh=mesh,
        in_specs=placed,
        out_specs=P("qx", "qy", None, None, None),
        check_vma=False,
    )
```

```python
import math

import jax
import jax.numpy as jnp
from jax import lax
from jax.experimental import pallas as pl
from jax.experimental.pallas import tpu as pltpu
from jax.sharding import PartitionSpec as P

CHUNKS = 2


def mixing(weight, data, form):
    return jnp.einsum(form, weight, data, preferred_element_type=jnp.float32).astype(jnp.bfloat16)


def level_bit(axis_count, level_index, depth):
    total_bits = axis_count.bit_length() - 1
    return level_index * (total_bits - 1) // max(depth - 1, 1)


def xor_order(x, axis, x_bit, y_bit):
    moved = jnp.moveaxis(x, axis, 0)
    shape = moved.shape
    pairs = moved.reshape((2, 2) + shape[1:])
    pairs = jnp.where(y_bit == 1, jnp.flip(pairs, 1), pairs)
    pairs = jnp.where(x_bit == 1, jnp.flip(pairs, 0), pairs)
    return jnp.moveaxis(pairs.reshape(shape), 0, axis)


PI_HI = 3.140625
PI_LO = math.pi - 3.140625


def cas(phase):
    x = phase + jnp.float32(math.pi / 4)
    n = jnp.round(x * jnp.float32(1 / math.pi))
    y = (x - n * jnp.float32(PI_HI)) - n * jnp.float32(PI_LO)
    y2 = y * y
    poly = jnp.float32(-1 / 39916800)
    for k in (9, 7, 5, 3):
        poly = poly * y2 + jnp.float32((-1) ** ((k - 1) // 2) / math.factorial(k))
    sine = y + y * y2 * poly
    odd = jnp.abs(n) == 1
    scale = jnp.where(odd, jnp.float32(-math.sqrt(2.0)), jnp.float32(math.sqrt(2.0)))
    return scale * sine


def flip_send(value, flip, x_shift, y_shift):
    n_x = lax.axis_size("qx")
    n_y = lax.axis_size("qy")
    if flip == 2:
        pairs = [(i, i ^ (1 << x_shift)) for i in range(n_x)]
        return lax.ppermute(value, "qx", pairs)
    if flip == 1:
        pairs = [(i, i ^ (1 << y_shift)) for i in range(n_y)]
        return lax.ppermute(value, "qy", pairs)
    pairs = [
        (t * n_y + u, (t ^ (1 << x_shift)) * n_y + (u ^ (1 << y_shift)))
        for t in range(n_x)
        for u in range(n_y)
    ]
    return lax.ppermute(value, ("qx", "qy"), pairs)


def exchange(relative, x_shift, y_shift):
    return [relative[0]] + [flip_send(relative[f], f, x_shift, y_shift) for f in (1, 2, 3)]


def cas_kernel(phase):
    x = phase + jnp.float32(math.pi / 4)
    n = jnp.floor(x * jnp.float32(1 / math.pi) + jnp.float32(0.5))
    y = (x - n * jnp.float32(PI_HI)) - n * jnp.float32(PI_LO)
    y2 = y * y
    poly = jnp.float32(-1 / 39916800)
    for k in (9, 7, 5, 3):
        poly = poly * y2 + jnp.float32((-1) ** ((k - 1) // 2) / math.factorial(k))
    sine = y + y * y2 * poly
    half = n * jnp.float32(0.5)
    odd = half != jnp.floor(half)
    scale = jnp.where(odd, jnp.float32(-math.sqrt(2.0)), jnp.float32(math.sqrt(2.0)))
    return scale * sine


def output_stage_kernel(p0, p1, p2, p3, ph_ref, obs_ref, w_ref, wt_ref, o_ref, ot_ref,
                        t0, t1, t2, t3):
    size = p0.shape[1]
    rows = 4 * size
    step = p0.shape[0]
    pieces = (p0, p1, p2, p3)
    terms = (t0, t1, t2, t3)

    def wide(parts):
        return jnp.concatenate(parts, axis=1)

    stacked = wide([jnp.concatenate([p[j] for p in pieces], axis=0) for j in range(step)])
    merged = jnp.dot(w_ref[...], stacked, preferred_element_type=jnp.float32)
    merged = merged.astype(jnp.bfloat16)
    predicted = jnp.dot(o_ref[...], merged, preferred_element_type=jnp.float32)
    wave = cas_kernel(wide([ph_ref[:, j].reshape(rows, -1) for j in range(step)]))
    seen = wide([obs_ref[:, j].reshape(rows, -1) for j in range(step)]).astype(jnp.float32)
    residual = (wave * predicted - seen).astype(jnp.bfloat16)
    weighted = (wave * residual.astype(jnp.float32)).astype(jnp.bfloat16)
    back = jnp.dot(ot_ref[...], weighted, preferred_element_type=jnp.float32)
    back = back.astype(jnp.bfloat16)
    out = jnp.dot(wt_ref[...], back, preferred_element_type=jnp.float32)
    out = out.astype(jnp.bfloat16)
    lanes = p0.shape[2]
    for f in range(4):
        for j in range(step):
            terms[f][j] = out[f * size:(f + 1) * size, j * lanes:(j + 1) * lanes]


def output_stage(pieces, wave, obs, chunk, w_mat, w_t, o_mat, o_t, step=8):
    part, rank_size, inner_boxes = pieces[0].shape
    piece_spec = pl.BlockSpec((step, rank_size, inner_boxes), lambda i: (i, 0, 0))
    field_spec = pl.BlockSpec(
        (4, None, step, rank_size, inner_boxes), lambda i: (0, chunk, i, 0, 0)
    )
    square = pl.BlockSpec(w_mat.shape, lambda i: (0, 0))
    flops = 4 * 2 * part * inner_boxes * w_mat.shape[0] * w_mat.shape[1]
    moved = part * rank_size * inner_boxes * 4 * (2 + 4 + 2 + 2)
    return pl.pallas_call(
        output_stage_kernel,
        grid=(part // step,),
        in_specs=[piece_spec] * 4 + [field_spec, field_spec] + [square] * 4,
        out_specs=[piece_spec] * 4,
        out_shape=[jax.ShapeDtypeStruct(pieces[0].shape, jnp.bfloat16)] * 4,
        cost_estimate=pl.CostEstimate(
            flops=flops, bytes_accessed=moved, transcendentals=0
        ),
    )(*pieces, wave, obs, w_mat, w_t, o_mat, o_t)


def local(image_tiles, observed, phases, interpolate, local_weights, merge_weights, output_weight):
    groups = image_tiles.shape[2]
    rank_size = image_tiles.shape[3]
    inner_boxes = image_tiles.shape[4]
    local_depth = local_weights.shape[2]
    quarter = groups // 4
    part = quarter // CHUNKS
    levels = local_weights[0, 0]
    merges = merge_weights[0, 0]
    n_x = lax.axis_size("qx")
    n_y = lax.axis_size("qy")
    t = lax.axis_index("qx")
    u = lax.axis_index("qy")
    shifts = [(level_bit(n_x, j, 2), level_bit(n_y, j, 2)) for j in range(2)]
    bits = [
        (jnp.right_shift(t, xs) & 1, jnp.right_shift(u, ys) & 1) for xs, ys in shifts
    ]

    w0 = xor_order(xor_order(merges[0], 1, *bits[0]), 0, *bits[1])
    w1 = xor_order(merges[1], 1, *bits[1])
    w1_mat = jnp.transpose(w1, (0, 2, 1, 3)).reshape(4 * rank_size, 4 * rank_size)
    w1_t = w1_mat.T
    eye = jnp.eye(4, dtype=output_weight.dtype)
    ow_mat = jnp.einsum("st,or->sotr", eye, output_weight).reshape(4 * rank_size, 4 * rank_size)
    ow_t = ow_mat.T

    shape5 = (4, CHUNKS, part, rank_size, inner_boxes)
    image = image_tiles[0, 0].reshape(shape5)
    obs = observed[0, 0].reshape(shape5)
    wave = phases[0, 0].reshape(shape5)
    k0 = 2 * bits[0][0] + bits[0][1]

    def local_forward(tiles):
        cur = mixing(interpolate, tiles, "op,jpl->jol")
        for i in range(local_depth):
            b = 4**i
            blk = cur.reshape(part // (4 * b), 4, b, rank_size, inner_boxes)
            cur = mixing(levels[i], blk, "kcor,acerl->akeol").reshape(
                part, rank_size, inner_boxes
            )
        return cur

    def local_adjoint(cur):
        for i in reversed(range(local_depth)):
            b = 4**i
            blk = cur.reshape(part // (4 * b), 4, b, rank_size, inner_boxes)
            cur = mixing(levels[i], blk, "kcor,akeol->acerl").reshape(
                part, rank_size, inner_boxes
            )
        return mixing(interpolate, cur, "op,jol->jpl")

    gradient = jnp.zeros(shape5, jnp.bfloat16)
    for m in range(CHUNKS):
        chunk = image[:, m]
        coef = [
            local_forward(lax.dynamic_index_in_dim(chunk, k0 ^ f, 0, keepdims=False))
            for f in range(4)
        ]
        pieces = exchange(coef, *shifts[0])
        cur = mixing(w0, jnp.stack(pieces), "scor,cjrl->sjol")
        pieces = exchange(cur, *shifts[1])
        terms = output_stage(pieces, wave, obs, m, w1_mat, w1_t, ow_mat, ow_t)
        back = exchange(terms, *shifts[1])
        terms = mixing(w0, jnp.stack(back), "scor,sjol->cjrl")
        back = exchange(terms, *shifts[0])
        for f in range(4):
            piece = local_adjoint(back[f])
            gradient = lax.dynamic_update_slice(
                gradient, piece[None, None], (k0 ^ f, m, 0, 0, 0)
            )
    return gradient.reshape(groups, rank_size, inner_boxes)[None, None]


def solution(mesh):
    placed = (
        P("qx", "qy", None, None, None),
        P("qx", "qy", None, None, None),
        P("qx", "qy", None, None, None),
        P(),
        P("qx", "qy", None, None, None, None, None),
        P("qx", "qy", None, None, None, None, None),
        P(),
    )
    return jax.shard_map(
        local,
        mesh=mesh,
        in_specs=placed,
        out_specs=P("qx", "qy", None, None, None),
        check_vma=False,
    )
```

```python
import functools
import math

import jax
import jax.numpy as jnp
from jax import lax
from jax.experimental import pallas as pl
from jax.experimental.pallas import tpu as pltpu
from jax.sharding import PartitionSpec as P

CHUNKS = 2


def mixing(weight, data, form):
    return jnp.einsum(form, weight, data, preferred_element_type=jnp.float32).astype(jnp.bfloat16)


def level_bit(axis_count, level_index, depth):
    total_bits = axis_count.bit_length() - 1
    return level_index * (total_bits - 1) // max(depth - 1, 1)


def xor_order(x, axis, x_bit, y_bit):
    moved = jnp.moveaxis(x, axis, 0)
    shape = moved.shape
    pairs = moved.reshape((2, 2) + shape[1:])
    pairs = jnp.where(y_bit == 1, jnp.flip(pairs, 1), pairs)
    pairs = jnp.where(x_bit == 1, jnp.flip(pairs, 0), pairs)
    return jnp.moveaxis(pairs.reshape(shape), 0, axis)


PI_HI = 3.140625
PI_LO = math.pi - 3.140625


def cas(phase):
    x = phase + jnp.float32(math.pi / 4)
    n = jnp.round(x * jnp.float32(1 / math.pi))
    y = (x - n * jnp.float32(PI_HI)) - n * jnp.float32(PI_LO)
    y2 = y * y
    poly = jnp.float32(-1 / 39916800)
    for k in (9, 7, 5, 3):
        poly = poly * y2 + jnp.float32((-1) ** ((k - 1) // 2) / math.factorial(k))
    sine = y + y * y2 * poly
    odd = jnp.abs(n) == 1
    scale = jnp.where(odd, jnp.float32(-math.sqrt(2.0)), jnp.float32(math.sqrt(2.0)))
    return scale * sine


def flip_send(value, flip, x_shift, y_shift):
    n_x = lax.axis_size("qx")
    n_y = lax.axis_size("qy")
    if flip == 2:
        pairs = [(i, i ^ (1 << x_shift)) for i in range(n_x)]
        return lax.ppermute(value, "qx", pairs)
    if flip == 1:
        pairs = [(i, i ^ (1 << y_shift)) for i in range(n_y)]
        return lax.ppermute(value, "qy", pairs)
    pairs = [
        (t * n_y + u, (t ^ (1 << x_shift)) * n_y + (u ^ (1 << y_shift)))
        for t in range(n_x)
        for u in range(n_y)
    ]
    return lax.ppermute(value, ("qx", "qy"), pairs)


def exchange(relative, x_shift, y_shift):
    return [relative[0]] + [flip_send(relative[f], f, x_shift, y_shift) for f in (1, 2, 3)]


def cas_kernel(phase):
    x = phase + jnp.float32(math.pi / 4)
    n = jnp.floor(x * jnp.float32(1 / math.pi) + jnp.float32(0.5))
    y = (x - n * jnp.float32(PI_HI)) - n * jnp.float32(PI_LO)
    y2 = y * y
    poly = jnp.float32(-1 / 39916800)
    for k in (9, 7, 5, 3):
        poly = poly * y2 + jnp.float32((-1) ** ((k - 1) // 2) / math.factorial(k))
    sine = y + y * y2 * poly
    half = n * jnp.float32(0.5)
    odd = half != jnp.floor(half)
    scale = jnp.where(odd, jnp.float32(-math.sqrt(2.0)), jnp.float32(math.sqrt(2.0)))
    return scale * sine


def output_stage_kernel(p0, p1, p2, p3, ph_ref, obs_ref, w_ref, wt_ref, o_ref, ot_ref,
                        t0, t1, t2, t3):
    size = p0.shape[1]
    rows = 4 * size
    step = p0.shape[0]
    pieces = (p0, p1, p2, p3)
    terms = (t0, t1, t2, t3)

    def wide(parts):
        return jnp.concatenate(parts, axis=1)

    stacked = wide([jnp.concatenate([p[j] for p in pieces], axis=0) for j in range(step)])
    merged = jnp.dot(w_ref[...], stacked, preferred_element_type=jnp.float32)
    merged = merged.astype(jnp.bfloat16)
    predicted = jnp.dot(o_ref[...], merged, preferred_element_type=jnp.float32)
    wave = cas_kernel(wide([ph_ref[:, j].reshape(rows, -1) for j in range(step)]))
    seen = wide([obs_ref[:, j].reshape(rows, -1) for j in range(step)]).astype(jnp.float32)
    residual = (wave * predicted - seen).astype(jnp.bfloat16)
    weighted = (wave * residual.astype(jnp.float32)).astype(jnp.bfloat16)
    back = jnp.dot(ot_ref[...], weighted, preferred_element_type=jnp.float32)
    back = back.astype(jnp.bfloat16)
    out = jnp.dot(wt_ref[...], back, preferred_element_type=jnp.float32)
    out = out.astype(jnp.bfloat16)
    lanes = p0.shape[2]
    for f in range(4):
        for j in range(step):
            terms[f][j] = out[f * size:(f + 1) * size, j * lanes:(j + 1) * lanes]


def chain_stage(cur, matrix, sets):
    size = cur[0].shape[0]
    lanes = cur[0].shape[1]
    wide = jnp.concatenate(
        [jnp.concatenate([cur[g] for g in group], axis=0) for group in sets], axis=1
    )
    mixed = jnp.dot(matrix, wide, preferred_element_type=jnp.float32).astype(jnp.bfloat16)
    out = list(cur)
    for b, group in enumerate(sets):
        for c, g in enumerate(group):
            out[g] = mixed[c * size:(c + 1) * size, b * lanes:(b + 1) * lanes]
    return out


def chain_sets(count, stride):
    return [
        [a * 4 * stride + c * stride + e for c in range(4)]
        for a in range(count // (4 * stride))
        for e in range(stride)
    ]


def chain_kernel(plan, k_ref, x_ref, m_ref, *rest):
    o_ref = rest[-1]
    cur = [x_ref[g] for g in range(x_ref.shape[0])]
    for index, sets in enumerate(plan):
        cur = chain_stage(cur, m_ref[index], sets)
    for g in range(len(cur)):
        o_ref[g] = cur[g]


def chain_call(plan, k0, data, mats, data_spec, out_shape, out_spec, target=None):
    in_specs = [data_spec, pl.BlockSpec(mats.shape, lambda i, k: (0, 0, 0))]
    operands = [k0, data, mats]
    aliases = {}
    if target is not None:
        in_specs.append(pl.BlockSpec(memory_space=pl.ANY))
        operands.append(target)
        aliases = {3: 0}
    return pl.pallas_call(
        functools.partial(chain_kernel, plan),
        grid_spec=pltpu.PrefetchScalarGridSpec(
            num_scalar_prefetch=1, grid=(1,), in_specs=in_specs, out_specs=out_spec
        ),
        out_shape=out_shape,
        input_output_aliases=aliases,
    )(*operands)


def output_stage(pieces, wave, obs, chunk, w_mat, w_t, o_mat, o_t, step=8):
    part, rank_size, inner_boxes = pieces[0].shape
    piece_spec = pl.BlockSpec((step, rank_size, inner_boxes), lambda i: (i, 0, 0))
    field_spec = pl.BlockSpec(
        (4, None, step, rank_size, inner_boxes), lambda i: (0, chunk, i, 0, 0)
    )
    square = pl.BlockSpec(w_mat.shape, lambda i: (0, 0))
    flops = 4 * 2 * part * inner_boxes * w_mat.shape[0] * w_mat.shape[1]
    moved = part * rank_size * inner_boxes * 4 * (2 + 4 + 2 + 2)
    return pl.pallas_call(
        output_stage_kernel,
        grid=(part // step,),
        in_specs=[piece_spec] * 4 + [field_spec, field_spec] + [square] * 4,
        out_specs=[piece_spec] * 4,
        out_shape=[jax.ShapeDtypeStruct(pieces[0].shape, jnp.bfloat16)] * 4,
        cost_estimate=pl.CostEstimate(
            flops=flops, bytes_accessed=moved, transcendentals=0
        ),
    )(*pieces, wave, obs, w_mat, w_t, o_mat, o_t)


def local(image_tiles, observed, phases, interpolate, local_weights, merge_weights, output_weight):
    groups = image_tiles.shape[2]
    rank_size = image_tiles.shape[3]
    inner_boxes = image_tiles.shape[4]
    local_depth = local_weights.shape[2]
    quarter = groups // 4
    part = quarter // CHUNKS
    levels = local_weights[0, 0]
    merges = merge_weights[0, 0]
    n_x = lax.axis_size("qx")
    n_y = lax.axis_size("qy")
    t = lax.axis_index("qx")
    u = lax.axis_index("qy")
    shifts = [(level_bit(n_x, j, 2), level_bit(n_y, j, 2)) for j in range(2)]
    bits = [
        (jnp.right_shift(t, xs) & 1, jnp.right_shift(u, ys) & 1) for xs, ys in shifts
    ]

    w0 = xor_order(xor_order(merges[0], 1, *bits[0]), 0, *bits[1])
    w1 = xor_order(merges[1], 1, *bits[1])
    w1_mat = jnp.transpose(w1, (0, 2, 1, 3)).reshape(4 * rank_size, 4 * rank_size)
    w1_t = w1_mat.T
    ow_mat = jnp.einsum("st,or->sotr", jnp.eye(4, dtype=output_weight.dtype), output_weight).reshape(4 * rank_size, 4 * rank_size)
    ow_t = ow_mat.T

    shape5 = (4, CHUNKS, part, rank_size, inner_boxes)
    image = image_tiles[0, 0].reshape(shape5)
    obs = observed[0, 0].reshape(shape5)
    wave = phases[0, 0].reshape(shape5)
    k0 = 2 * bits[0][0] + bits[0][1]

    eye = jnp.eye(4, dtype=interpolate.dtype)
    spread = jnp.einsum("st,op->sotp", eye, interpolate).reshape(4 * rank_size, 4 * rank_size)
    forward_levels = [
        jnp.transpose(levels[i], (0, 2, 1, 3)).reshape(4 * rank_size, 4 * rank_size)
        for i in range(local_depth)
    ]
    forward_mats = jnp.stack([spread] + forward_levels)
    adjoint_mats = jnp.stack([w.T for w in reversed(forward_levels)] + [spread.T])
    forward_plan = [chain_sets(part, 1)] + [chain_sets(part, 4**i) for i in range(local_depth)]
    adjoint_plan = [chain_sets(part, 4**i) for i in reversed(range(local_depth))] + [
        chain_sets(part, 1)
    ]
    k0_ref = jnp.reshape(k0, (1,)).astype(jnp.int32)
    piece_shape = jax.ShapeDtypeStruct((part, rank_size, inner_boxes), jnp.bfloat16)
    whole_piece = pl.BlockSpec((part, rank_size, inner_boxes), lambda i, k: (0, 0, 0))

    def in_place(m, f):
        return pl.BlockSpec(
            (None, None, part, rank_size, inner_boxes),
            lambda i, k: (jnp.bitwise_xor(k[0], f), m, 0, 0, 0),
        )

    def local_forward(m, f):
        return chain_call(
            forward_plan, k0_ref, image, forward_mats, in_place(m, f), piece_shape, whole_piece
        )

    def local_adjoint(gradient, piece, m, f):
        return chain_call(
            adjoint_plan,
            k0_ref,
            piece,
            adjoint_mats,
            whole_piece,
            jax.ShapeDtypeStruct(shape5, jnp.bfloat16),
            in_place(m, f),
            target=gradient,
        )

    gradient = jnp.zeros(shape5, jnp.bfloat16)
    for m in range(CHUNKS):
        coef = [local_forward(m, f) for f in range(4)]
        pieces = exchange(coef, *shifts[0])
        cur = mixing(w0, jnp.stack(pieces), "scor,cjrl->sjol")
        pieces = exchange(cur, *shifts[1])
        terms = output_stage(pieces, wave, obs, m, w1_mat, w1_t, ow_mat, ow_t)
        back = exchange(terms, *shifts[1])
        terms = mixing(w0, jnp.stack(back), "scor,sjol->cjrl")
        back = exchange(terms, *shifts[0])
        for f in range(4):
            gradient = local_adjoint(gradient, back[f], m, f)
    return gradient.reshape(groups, rank_size, inner_boxes)[None, None]


def solution(mesh):
    placed = (
        P("qx", "qy", None, None, None),
        P("qx", "qy", None, None, None),
        P("qx", "qy", None, None, None),
        P(),
        P("qx", "qy", None, None, None, None, None),
        P("qx", "qy", None, None, None, None, None),
        P(),
    )
    return jax.shard_map(
        local,
        mesh=mesh,
        in_specs=placed,
        out_specs=P("qx", "qy", None, None, None),
        check_vma=False,
    )
```

```python
import functools
import math

import jax
import jax.numpy as jnp
from jax import lax
from jax.experimental import pallas as pl
from jax.experimental.pallas import tpu as pltpu
from jax.sharding import PartitionSpec as P

CHUNKS = 2


def mixing(weight, data, form):
    return jnp.einsum(form, weight, data, preferred_element_type=jnp.float32).astype(jnp.bfloat16)


def level_bit(axis_count, level_index, depth):
    total_bits = axis_count.bit_length() - 1
    return level_index * (total_bits - 1) // max(depth - 1, 1)


def xor_order(x, axis, x_bit, y_bit):
    moved = jnp.moveaxis(x, axis, 0)
    shape = moved.shape
    pairs = moved.reshape((2, 2) + shape[1:])
    pairs = jnp.where(y_bit == 1, jnp.flip(pairs, 1), pairs)
    pairs = jnp.where(x_bit == 1, jnp.flip(pairs, 0), pairs)
    return jnp.moveaxis(pairs.reshape(shape), 0, axis)


PI_HI = 3.140625
PI_LO = math.pi - 3.140625


def cas(phase):
    x = phase + jnp.float32(math.pi / 4)
    n = jnp.round(x * jnp.float32(1 / math.pi))
    y = (x - n * jnp.float32(PI_HI)) - n * jnp.float32(PI_LO)
    y2 = y * y
    poly = jnp.float32(-1 / 39916800)
    for k in (9, 7, 5, 3):
        poly = poly * y2 + jnp.float32((-1) ** ((k - 1) // 2) / math.factorial(k))
    sine = y + y * y2 * poly
    odd = jnp.abs(n) == 1
    scale = jnp.where(odd, jnp.float32(-math.sqrt(2.0)), jnp.float32(math.sqrt(2.0)))
    return scale * sine


def flip_send(value, flip, x_shift, y_shift):
    n_x = lax.axis_size("qx")
    n_y = lax.axis_size("qy")
    if flip == 2:
        pairs = [(i, i ^ (1 << x_shift)) for i in range(n_x)]
        return lax.ppermute(value, "qx", pairs)
    if flip == 1:
        pairs = [(i, i ^ (1 << y_shift)) for i in range(n_y)]
        return lax.ppermute(value, "qy", pairs)
    pairs = [
        (t * n_y + u, (t ^ (1 << x_shift)) * n_y + (u ^ (1 << y_shift)))
        for t in range(n_x)
        for u in range(n_y)
    ]
    return lax.ppermute(value, ("qx", "qy"), pairs)


def exchange(relative, x_shift, y_shift):
    return [relative[0]] + [flip_send(relative[f], f, x_shift, y_shift) for f in (1, 2, 3)]


def cas_kernel(phase):
    x = phase + jnp.float32(math.pi / 4)
    n = jnp.floor(x * jnp.float32(1 / math.pi) + jnp.float32(0.5))
    y = (x - n * jnp.float32(PI_HI)) - n * jnp.float32(PI_LO)
    y2 = y * y
    poly = jnp.float32(-1 / 39916800)
    for k in (9, 7, 5, 3):
        poly = poly * y2 + jnp.float32((-1) ** ((k - 1) // 2) / math.factorial(k))
    sine = y + y * y2 * poly
    half = n * jnp.float32(0.5)
    odd = half != jnp.floor(half)
    scale = jnp.where(odd, jnp.float32(-math.sqrt(2.0)), jnp.float32(math.sqrt(2.0)))
    return scale * sine


def output_stage_kernel(p0, p1, p2, p3, ph_ref, obs_ref, w_ref, wt_ref, o_ref, ot_ref,
                        t0, t1, t2, t3):
    size = p0.shape[1]
    rows = 4 * size
    step = p0.shape[0]
    pieces = (p0, p1, p2, p3)
    terms = (t0, t1, t2, t3)

    def wide(parts):
        return jnp.concatenate(parts, axis=1)

    stacked = wide([jnp.concatenate([p[j] for p in pieces], axis=0) for j in range(step)])
    merged = jnp.dot(w_ref[...], stacked, preferred_element_type=jnp.float32)
    merged = merged.astype(jnp.bfloat16)
    predicted = jnp.dot(o_ref[...], merged, preferred_element_type=jnp.float32)
    wave = cas_kernel(wide([ph_ref[:, j].reshape(rows, -1) for j in range(step)]))
    seen = wide([obs_ref[:, j].reshape(rows, -1) for j in range(step)]).astype(jnp.float32)
    residual = (wave * predicted - seen).astype(jnp.bfloat16)
    weighted = (wave * residual.astype(jnp.float32)).astype(jnp.bfloat16)
    back = jnp.dot(ot_ref[...], weighted, preferred_element_type=jnp.float32)
    back = back.astype(jnp.bfloat16)
    out = jnp.dot(wt_ref[...], back, preferred_element_type=jnp.float32)
    out = out.astype(jnp.bfloat16)
    lanes = p0.shape[2]
    for f in range(4):
        for j in range(step):
            terms[f][j] = out[f * size:(f + 1) * size, j * lanes:(j + 1) * lanes]


def chain_stage(cur, matrix, sets):
    size = cur[0].shape[0]
    lanes = cur[0].shape[1]
    wide = jnp.concatenate(
        [jnp.concatenate([cur[g] for g in group], axis=0) for group in sets], axis=1
    )
    mixed = jnp.dot(matrix, wide, preferred_element_type=jnp.float32).astype(jnp.bfloat16)
    out = list(cur)
    for b, group in enumerate(sets):
        for c, g in enumerate(group):
            out[g] = mixed[c * size:(c + 1) * size, b * lanes:(b + 1) * lanes]
    return out


def chain_sets(count, stride):
    return [
        [a * 4 * stride + c * stride + e for c in range(4)]
        for a in range(count // (4 * stride))
        for e in range(stride)
    ]


def chain_kernel(plan, k_ref, x_ref, m_ref, *rest):
    o_ref = rest[-1]
    cur = [x_ref[g] for g in range(x_ref.shape[0])]
    for index, sets in enumerate(plan):
        cur = chain_stage(cur, m_ref[index], sets)
    for g in range(len(cur)):
        o_ref[g] = cur[g]


def chain_call(plan, k0, data, mats, data_spec, out_shape, out_spec, steps, target=None):
    in_specs = [data_spec, pl.BlockSpec(mats.shape, lambda i, k: (0, 0, 0))]
    operands = [k0, data, mats]
    aliases = {}
    if target is not None:
        in_specs.append(pl.BlockSpec(memory_space=pl.ANY))
        operands.append(target)
        aliases = {3: 0}
    return pl.pallas_call(
        functools.partial(chain_kernel, plan),
        grid_spec=pltpu.PrefetchScalarGridSpec(
            num_scalar_prefetch=1, grid=(steps,), in_specs=in_specs, out_specs=out_spec
        ),
        out_shape=out_shape,
        input_output_aliases=aliases,
    )(*operands)


def output_stage(pieces, wave, obs, chunk, w_mat, w_t, o_mat, o_t, step=8):
    part, rank_size, inner_boxes = pieces[0].shape
    piece_spec = pl.BlockSpec((step, rank_size, inner_boxes), lambda i: (i, 0, 0))
    field_spec = pl.BlockSpec(
        (4, None, step, rank_size, inner_boxes), lambda i: (0, chunk, i, 0, 0)
    )
    square = pl.BlockSpec(w_mat.shape, lambda i: (0, 0))
    flops = 4 * 2 * part * inner_boxes * w_mat.shape[0] * w_mat.shape[1]
    moved = part * rank_size * inner_boxes * 4 * (2 + 4 + 2 + 2)
    return pl.pallas_call(
        output_stage_kernel,
        grid=(part // step,),
        in_specs=[piece_spec] * 4 + [field_spec, field_spec] + [square] * 4,
        out_specs=[piece_spec] * 4,
        out_shape=[jax.ShapeDtypeStruct(pieces[0].shape, jnp.bfloat16)] * 4,
        cost_estimate=pl.CostEstimate(
            flops=flops, bytes_accessed=moved, transcendentals=0
        ),
    )(*pieces, wave, obs, w_mat, w_t, o_mat, o_t)


def local(image_tiles, observed, phases, interpolate, local_weights, merge_weights, output_weight):
    groups = image_tiles.shape[2]
    rank_size = image_tiles.shape[3]
    inner_boxes = image_tiles.shape[4]
    local_depth = local_weights.shape[2]
    quarter = groups // 4
    part = quarter // CHUNKS
    levels = local_weights[0, 0]
    merges = merge_weights[0, 0]
    n_x = lax.axis_size("qx")
    n_y = lax.axis_size("qy")
    t = lax.axis_index("qx")
    u = lax.axis_index("qy")
    shifts = [(level_bit(n_x, j, 2), level_bit(n_y, j, 2)) for j in range(2)]
    bits = [
        (jnp.right_shift(t, xs) & 1, jnp.right_shift(u, ys) & 1) for xs, ys in shifts
    ]

    w0 = xor_order(xor_order(merges[0], 1, *bits[0]), 0, *bits[1])
    w1 = xor_order(merges[1], 1, *bits[1])
    w1_mat = jnp.transpose(w1, (0, 2, 1, 3)).reshape(4 * rank_size, 4 * rank_size)
    w1_t = w1_mat.T
    ow_mat = jnp.einsum("st,or->sotr", jnp.eye(4, dtype=output_weight.dtype), output_weight).reshape(4 * rank_size, 4 * rank_size)
    ow_t = ow_mat.T

    shape5 = (4, CHUNKS, part, rank_size, inner_boxes)
    image = image_tiles[0, 0].reshape(shape5)
    obs = observed[0, 0].reshape(shape5)
    wave = phases[0, 0].reshape(shape5)
    k0 = 2 * bits[0][0] + bits[0][1]

    eye = jnp.eye(4, dtype=interpolate.dtype)
    spread = jnp.einsum("st,op->sotp", eye, interpolate).reshape(4 * rank_size, 4 * rank_size)
    forward_levels = [
        jnp.transpose(levels[i], (0, 2, 1, 3)).reshape(4 * rank_size, 4 * rank_size)
        for i in range(local_depth)
    ]
    forward_mats = jnp.stack([spread] + forward_levels)
    adjoint_mats = jnp.stack([w.T for w in reversed(forward_levels)] + [spread.T])
    steps = 2
    block = part // steps
    forward_plan = [chain_sets(block, 1)] + [chain_sets(block, 4**i) for i in range(local_depth)]
    adjoint_plan = [chain_sets(block, 4**i) for i in reversed(range(local_depth))] + [
        chain_sets(block, 1)
    ]
    k0_ref = jnp.reshape(k0, (1,)).astype(jnp.int32)
    piece_shape = jax.ShapeDtypeStruct((part, rank_size, inner_boxes), jnp.bfloat16)
    whole_piece = pl.BlockSpec((block, rank_size, inner_boxes), lambda i, k: (i, 0, 0))

    def in_place(m, f):
        return pl.BlockSpec(
            (None, None, block, rank_size, inner_boxes),
            lambda i, k: (jnp.bitwise_xor(k[0], f), m, i, 0, 0),
        )

    def local_forward(m, f):
        return chain_call(
            forward_plan, k0_ref, image, forward_mats, in_place(m, f), piece_shape, whole_piece,
            steps,
        )

    def local_adjoint(gradient, piece, m, f):
        return chain_call(
            adjoint_plan,
            k0_ref,
            piece,
            adjoint_mats,
            whole_piece,
            jax.ShapeDtypeStruct(shape5, jnp.bfloat16),
            in_place(m, f),
            steps,
            target=gradient,
        )

    gradient = None
    for m in range(CHUNKS):
        coef = [local_forward(m, f) for f in range(4)]
        pieces = exchange(coef, *shifts[0])
        cur = mixing(w0, jnp.stack(pieces), "scor,cjrl->sjol")
        pieces = exchange(cur, *shifts[1])
        terms = output_stage(pieces, wave, obs, m, w1_mat, w1_t, ow_mat, ow_t)
        back = exchange(terms, *shifts[1])
        terms = mixing(w0, jnp.stack(back), "scor,sjol->cjrl")
        back = exchange(terms, *shifts[0])
        for f in range(4):
            gradient = local_adjoint(gradient, back[f], m, f)
    return gradient.reshape(groups, rank_size, inner_boxes)[None, None]


def solution(mesh):
    placed = (
        P("qx", "qy", None, None, None),
        P("qx", "qy", None, None, None),
        P("qx", "qy", None, None, None),
        P(),
        P("qx", "qy", None, None, None, None, None),
        P("qx", "qy", None, None, None, None, None),
        P(),
    )
    return jax.shard_map(
        local,
        mesh=mesh,
        in_specs=placed,
        out_specs=P("qx", "qy", None, None, None),
        check_vma=False,
    )
```

```python
import functools
import math

import jax
import jax.numpy as jnp
from jax import lax
from jax.experimental import pallas as pl
from jax.experimental.pallas import tpu as pltpu
from jax.sharding import PartitionSpec as P

CHUNKS = 2


def mixing(weight, data, form):
    return jnp.einsum(form, weight, data, preferred_element_type=jnp.float32).astype(jnp.bfloat16)


def level_bit(axis_count, level_index, depth):
    total_bits = axis_count.bit_length() - 1
    return level_index * (total_bits - 1) // max(depth - 1, 1)


def xor_order(x, axis, x_bit, y_bit):
    moved = jnp.moveaxis(x, axis, 0)
    shape = moved.shape
    pairs = moved.reshape((2, 2) + shape[1:])
    pairs = jnp.where(y_bit == 1, jnp.flip(pairs, 1), pairs)
    pairs = jnp.where(x_bit == 1, jnp.flip(pairs, 0), pairs)
    return jnp.moveaxis(pairs.reshape(shape), 0, axis)


PI_HI = 3.140625
PI_LO = math.pi - 3.140625


def cas(phase):
    x = phase + jnp.float32(math.pi / 4)
    n = jnp.round(x * jnp.float32(1 / math.pi))
    y = (x - n * jnp.float32(PI_HI)) - n * jnp.float32(PI_LO)
    y2 = y * y
    poly = jnp.float32(-1 / 39916800)
    for k in (9, 7, 5, 3):
        poly = poly * y2 + jnp.float32((-1) ** ((k - 1) // 2) / math.factorial(k))
    sine = y + y * y2 * poly
    odd = jnp.abs(n) == 1
    scale = jnp.where(odd, jnp.float32(-math.sqrt(2.0)), jnp.float32(math.sqrt(2.0)))
    return scale * sine


def flip_send(value, flip, x_shift, y_shift):
    n_x = lax.axis_size("qx")
    n_y = lax.axis_size("qy")
    if flip == 2:
        pairs = [(i, i ^ (1 << x_shift)) for i in range(n_x)]
        return lax.ppermute(value, "qx", pairs)
    if flip == 1:
        pairs = [(i, i ^ (1 << y_shift)) for i in range(n_y)]
        return lax.ppermute(value, "qy", pairs)
    pairs = [
        (t * n_y + u, (t ^ (1 << x_shift)) * n_y + (u ^ (1 << y_shift)))
        for t in range(n_x)
        for u in range(n_y)
    ]
    return lax.ppermute(value, ("qx", "qy"), pairs)


def exchange(relative, x_shift, y_shift):
    return [relative[0]] + [flip_send(relative[f], f, x_shift, y_shift) for f in (1, 2, 3)]


def cas_kernel(phase):
    x = phase + jnp.float32(math.pi / 4)
    n = jnp.floor(x * jnp.float32(1 / math.pi) + jnp.float32(0.5))
    y = (x - n * jnp.float32(PI_HI)) - n * jnp.float32(PI_LO)
    y2 = y * y
    poly = jnp.float32(-1 / 39916800)
    for k in (9, 7, 5, 3):
        poly = poly * y2 + jnp.float32((-1) ** ((k - 1) // 2) / math.factorial(k))
    sine = y + y * y2 * poly
    half = n * jnp.float32(0.5)
    odd = half != jnp.floor(half)
    scale = jnp.where(odd, jnp.float32(-math.sqrt(2.0)), jnp.float32(math.sqrt(2.0)))
    return scale * sine


def output_stage_kernel(p0, p1, p2, p3, ph_ref, obs_ref, w_ref, wt_ref, o_ref, ot_ref,
                        t0, t1, t2, t3):
    size = p0.shape[1]
    rows = 4 * size
    step = p0.shape[0]
    pieces = (p0, p1, p2, p3)
    terms = (t0, t1, t2, t3)

    def wide(parts):
        return jnp.concatenate(parts, axis=1)

    stacked = wide([jnp.concatenate([p[j] for p in pieces], axis=0) for j in range(step)])
    merged = jnp.dot(w_ref[...], stacked, preferred_element_type=jnp.float32)
    merged = merged.astype(jnp.bfloat16)
    predicted = jnp.dot(o_ref[...], merged, preferred_element_type=jnp.float32)
    wave = cas_kernel(wide([ph_ref[:, j].reshape(rows, -1) for j in range(step)]))
    seen = wide([obs_ref[:, j].reshape(rows, -1) for j in range(step)]).astype(jnp.float32)
    residual = (wave * predicted - seen).astype(jnp.bfloat16)
    weighted = (wave * residual.astype(jnp.float32)).astype(jnp.bfloat16)
    back = jnp.dot(ot_ref[...], weighted, preferred_element_type=jnp.float32)
    back = back.astype(jnp.bfloat16)
    out = jnp.dot(wt_ref[...], back, preferred_element_type=jnp.float32)
    out = out.astype(jnp.bfloat16)
    lanes = p0.shape[2]
    for f in range(4):
        for j in range(step):
            terms[f][j] = out[f * size:(f + 1) * size, j * lanes:(j + 1) * lanes]


def chain_stage(cur, matrix, sets):
    size = cur[0].shape[0]
    lanes = cur[0].shape[1]
    wide = jnp.concatenate(
        [jnp.concatenate([cur[g] for g in group], axis=0) for group in sets], axis=1
    )
    mixed = jnp.dot(matrix, wide, preferred_element_type=jnp.float32).astype(jnp.bfloat16)
    out = list(cur)
    for b, group in enumerate(sets):
        for c, g in enumerate(group):
            out[g] = mixed[c * size:(c + 1) * size, b * lanes:(b + 1) * lanes]
    return out


def chain_sets(count, stride):
    return [
        [a * 4 * stride + c * stride + e for c in range(4)]
        for a in range(count // (4 * stride))
        for e in range(stride)
    ]


def chain_kernel(plan, k_ref, x_ref, m_ref, *rest):
    o_ref = rest[-1]
    cur = [x_ref[g] for g in range(x_ref.shape[0])]
    for index, sets in enumerate(plan):
        cur = chain_stage(cur, m_ref[index], sets)
    for g in range(len(cur)):
        o_ref[g] = cur[g]


def chain_call(plan, k0, data, mats, data_spec, out_shape, out_spec, target=None):
    in_specs = [data_spec, pl.BlockSpec(mats.shape, lambda i, k: (0, 0, 0))]
    operands = [k0, data, mats]
    aliases = {}
    if target is not None:
        in_specs.append(pl.BlockSpec(memory_space=pl.ANY))
        operands.append(target)
        aliases = {3: 0}
    return pl.pallas_call(
        functools.partial(chain_kernel, plan),
        grid_spec=pltpu.PrefetchScalarGridSpec(
            num_scalar_prefetch=1, grid=(1,), in_specs=in_specs, out_specs=out_spec
        ),
        out_shape=out_shape,
        input_output_aliases=aliases,
    )(*operands)


def output_stage(pieces, wave, obs, chunk, w_mat, w_t, o_mat, o_t, step=8):
    part, rank_size, inner_boxes = pieces[0].shape
    piece_spec = pl.BlockSpec((step, rank_size, inner_boxes), lambda i: (i, 0, 0))
    field_spec = pl.BlockSpec(
        (4, None, step, rank_size, inner_boxes), lambda i: (0, chunk, i, 0, 0)
    )
    square = pl.BlockSpec(w_mat.shape, lambda i: (0, 0))
    flops = 4 * 2 * part * inner_boxes * w_mat.shape[0] * w_mat.shape[1]
    moved = part * rank_size * inner_boxes * 4 * (2 + 4 + 2 + 2)
    return pl.pallas_call(
        output_stage_kernel,
        grid=(part // step,),
        in_specs=[piece_spec] * 4 + [field_spec, field_spec] + [square] * 4,
        out_specs=[piece_spec] * 4,
        out_shape=[jax.ShapeDtypeStruct(pieces[0].shape, jnp.bfloat16)] * 4,
        cost_estimate=pl.CostEstimate(
            flops=flops, bytes_accessed=moved, transcendentals=0
        ),
    )(*pieces, wave, obs, w_mat, w_t, o_mat, o_t)


def local(image_tiles, observed, phases, interpolate, local_weights, merge_weights, output_weight):
    groups = image_tiles.shape[2]
    rank_size = image_tiles.shape[3]
    inner_boxes = image_tiles.shape[4]
    local_depth = local_weights.shape[2]
    quarter = groups // 4
    part = quarter // CHUNKS
    levels = local_weights[0, 0]
    merges = merge_weights[0, 0]
    n_x = lax.axis_size("qx")
    n_y = lax.axis_size("qy")
    t = lax.axis_index("qx")
    u = lax.axis_index("qy")
    shifts = [(level_bit(n_x, j, 2), level_bit(n_y, j, 2)) for j in range(2)]
    bits = [
        (jnp.right_shift(t, xs) & 1, jnp.right_shift(u, ys) & 1) for xs, ys in shifts
    ]

    w0 = xor_order(xor_order(merges[0], 1, *bits[0]), 0, *bits[1])
    w1 = xor_order(merges[1], 1, *bits[1])
    w1_mat = jnp.transpose(w1, (0, 2, 1, 3)).reshape(4 * rank_size, 4 * rank_size)
    w1_t = w1_mat.T
    ow_mat = jnp.einsum("st,or->sotr", jnp.eye(4, dtype=output_weight.dtype), output_weight).reshape(4 * rank_size, 4 * rank_size)
    ow_t = ow_mat.T

    shape5 = (4, CHUNKS, part, rank_size, inner_boxes)
    image = image_tiles[0, 0].reshape(shape5)
    obs = observed[0, 0].reshape(shape5)
    wave = phases[0, 0].reshape(shape5)
    k0 = 2 * bits[0][0] + bits[0][1]

    eye = jnp.eye(4, dtype=interpolate.dtype)
    spread = jnp.einsum("st,op->sotp", eye, interpolate).reshape(4 * rank_size, 4 * rank_size)
    forward_levels = [
        jnp.transpose(levels[i], (0, 2, 1, 3)).reshape(4 * rank_size, 4 * rank_size)
        for i in range(local_depth)
    ]
    forward_mats = jnp.stack([spread] + forward_levels)
    adjoint_mats = jnp.stack([w.T for w in reversed(forward_levels)] + [spread.T])
    forward_plan = [chain_sets(part, 1)] + [chain_sets(part, 4**i) for i in range(local_depth)]
    adjoint_plan = [chain_sets(part, 4**i) for i in reversed(range(local_depth))] + [
        chain_sets(part, 1)
    ]
    k0_ref = jnp.reshape(k0, (1,)).astype(jnp.int32)
    piece_shape = jax.ShapeDtypeStruct((part, rank_size, inner_boxes), jnp.bfloat16)
    whole_piece = pl.BlockSpec((part, rank_size, inner_boxes), lambda i, k: (0, 0, 0))

    def in_place(m, f):
        return pl.BlockSpec(
            (None, None, part, rank_size, inner_boxes),
            lambda i, k: (jnp.bitwise_xor(k[0], f), m, 0, 0, 0),
        )

    def local_forward(m, f):
        return chain_call(
            forward_plan, k0_ref, image, forward_mats, in_place(m, f), piece_shape, whole_piece
        )

    def local_adjoint(gradient, piece, m, f):
        return chain_call(
            adjoint_plan,
            k0_ref,
            piece,
            adjoint_mats,
            whole_piece,
            jax.ShapeDtypeStruct(shape5, jnp.bfloat16),
            in_place(m, f),
            target=gradient,
        )

    gradient = None
    for m in range(CHUNKS):
        coef = [local_forward(m, f) for f in range(4)]
        pieces = exchange(coef, *shifts[0])
        cur = mixing(w0, jnp.stack(pieces), "scor,cjrl->sjol")
        pieces = exchange(cur, *shifts[1])
        terms = output_stage(pieces, wave, obs, m, w1_mat, w1_t, ow_mat, ow_t)
        back = exchange(terms, *shifts[1])
        terms = mixing(w0, jnp.stack(back), "scor,sjol->cjrl")
        back = exchange(terms, *shifts[0])
        for f in range(4):
            gradient = local_adjoint(gradient, back[f], m, f)
    return gradient.reshape(groups, rank_size, inner_boxes)[None, None]


def solution(mesh):
    placed = (
        P("qx", "qy", None, None, None),
        P("qx", "qy", None, None, None),
        P("qx", "qy", None, None, None),
        P(),
        P("qx", "qy", None, None, None, None, None),
        P("qx", "qy", None, None, None, None, None),
        P(),
    )
    return jax.shard_map(
        local,
        mesh=mesh,
        in_specs=placed,
        out_specs=P("qx", "qy", None, None, None),
        check_vma=False,
    )
```

```python
import functools
import math

import jax
import jax.numpy as jnp
from jax import lax
from jax.experimental import pallas as pl
from jax.experimental.pallas import tpu as pltpu
from jax.sharding import PartitionSpec as P

CHUNKS = 2


def mixing(weight, data, form):
    return jnp.einsum(form, weight, data, preferred_element_type=jnp.float32).astype(jnp.bfloat16)


def level_bit(axis_count, level_index, depth):
    total_bits = axis_count.bit_length() - 1
    return level_index * (total_bits - 1) // max(depth - 1, 1)


def xor_order(x, axis, x_bit, y_bit):
    moved = jnp.moveaxis(x, axis, 0)
    shape = moved.shape
    pairs = moved.reshape((2, 2) + shape[1:])
    pairs = jnp.where(y_bit == 1, jnp.flip(pairs, 1), pairs)
    pairs = jnp.where(x_bit == 1, jnp.flip(pairs, 0), pairs)
    return jnp.moveaxis(pairs.reshape(shape), 0, axis)


PI_HI = 3.140625
PI_LO = math.pi - 3.140625


def cas(phase):
    x = phase + jnp.float32(math.pi / 4)
    n = jnp.round(x * jnp.float32(1 / math.pi))
    y = (x - n * jnp.float32(PI_HI)) - n * jnp.float32(PI_LO)
    y2 = y * y
    poly = jnp.float32(-1 / 39916800)
    for k in (9, 7, 5, 3):
        poly = poly * y2 + jnp.float32((-1) ** ((k - 1) // 2) / math.factorial(k))
    sine = y + y * y2 * poly
    odd = jnp.abs(n) == 1
    scale = jnp.where(odd, jnp.float32(-math.sqrt(2.0)), jnp.float32(math.sqrt(2.0)))
    return scale * sine


def flip_send(value, flip, x_shift, y_shift):
    n_x = lax.axis_size("qx")
    n_y = lax.axis_size("qy")
    if flip == 2:
        pairs = [(i, i ^ (1 << x_shift)) for i in range(n_x)]
        return lax.ppermute(value, "qx", pairs)
    if flip == 1:
        pairs = [(i, i ^ (1 << y_shift)) for i in range(n_y)]
        return lax.ppermute(value, "qy", pairs)
    pairs = [
        (t * n_y + u, (t ^ (1 << x_shift)) * n_y + (u ^ (1 << y_shift)))
        for t in range(n_x)
        for u in range(n_y)
    ]
    return lax.ppermute(value, ("qx", "qy"), pairs)


def exchange(relative, x_shift, y_shift):
    return [relative[0]] + [flip_send(relative[f], f, x_shift, y_shift) for f in (1, 2, 3)]


def cas_kernel(phase):
    x = phase + jnp.float32(math.pi / 4)
    n = jnp.floor(x * jnp.float32(1 / math.pi) + jnp.float32(0.5))
    y = (x - n * jnp.float32(PI_HI)) - n * jnp.float32(PI_LO)
    y2 = y * y
    poly = jnp.float32(-1 / 39916800)
    for k in (9, 7, 5, 3):
        poly = poly * y2 + jnp.float32((-1) ** ((k - 1) // 2) / math.factorial(k))
    sine = y + y * y2 * poly
    half = n * jnp.float32(0.5)
    odd = half != jnp.floor(half)
    scale = jnp.where(odd, jnp.float32(-math.sqrt(2.0)), jnp.float32(math.sqrt(2.0)))
    return scale * sine


def output_stage_kernel(p0, p1, p2, p3, ph_ref, obs_ref, w_ref, wt_ref, o_ref, ot_ref,
                        t0, t1, t2, t3):
    size = p0.shape[1]
    rows = 4 * size
    step = p0.shape[0]
    pieces = (p0, p1, p2, p3)
    terms = (t0, t1, t2, t3)

    def wide(parts):
        return jnp.concatenate(parts, axis=1)

    stacked = wide([jnp.concatenate([p[j] for p in pieces], axis=0) for j in range(step)])
    merged = jnp.dot(w_ref[...], stacked, preferred_element_type=jnp.float32)
    merged = merged.astype(jnp.bfloat16)
    predicted = jnp.dot(o_ref[...], merged, preferred_element_type=jnp.float32)
    wave = cas_kernel(wide([ph_ref[:, j].reshape(rows, -1) for j in range(step)]))
    seen = wide([obs_ref[:, j].reshape(rows, -1) for j in range(step)]).astype(jnp.float32)
    residual = (wave * predicted - seen).astype(jnp.bfloat16)
    weighted = (wave * residual.astype(jnp.float32)).astype(jnp.bfloat16)
    back = jnp.dot(ot_ref[...], weighted, preferred_element_type=jnp.float32)
    back = back.astype(jnp.bfloat16)
    out = jnp.dot(wt_ref[...], back, preferred_element_type=jnp.float32)
    out = out.astype(jnp.bfloat16)
    lanes = p0.shape[2]
    for f in range(4):
        for j in range(step):
            terms[f][j] = out[f * size:(f + 1) * size, j * lanes:(j + 1) * lanes]


def chain_stage(cur, matrix, sets):
    size = cur[0].shape[0]
    lanes = cur[0].shape[1]
    wide = jnp.concatenate(
        [jnp.concatenate([cur[g] for g in group], axis=0) for group in sets], axis=1
    )
    mixed = jnp.dot(matrix, wide, preferred_element_type=jnp.float32).astype(jnp.bfloat16)
    out = list(cur)
    for b, group in enumerate(sets):
        for c, g in enumerate(group):
            out[g] = mixed[c * size:(c + 1) * size, b * lanes:(b + 1) * lanes]
    return out


def chain_sets(count, stride):
    return [
        [a * 4 * stride + c * stride + e for c in range(4)]
        for a in range(count // (4 * stride))
        for e in range(stride)
    ]


def chain_kernel(plan, k_ref, x_ref, m_ref, *rest):
    o_ref = rest[-1]
    cur = [x_ref[g] for g in range(x_ref.shape[0])]
    for index, sets in enumerate(plan):
        cur = chain_stage(cur, m_ref[index], sets)
    for g in range(len(cur)):
        o_ref[g] = cur[g]


def chain_call(plan, k0, data, mats, data_spec, out_shape, out_spec, target=None):
    in_specs = [data_spec, pl.BlockSpec(mats.shape, lambda i, k: (0, 0, 0))]
    operands = [k0, data, mats]
    aliases = {}
    if target is not None:
        in_specs.append(pl.BlockSpec(memory_space=pl.ANY))
        operands.append(target)
        aliases = {3: 0}
    return pl.pallas_call(
        functools.partial(chain_kernel, plan),
        grid_spec=pltpu.PrefetchScalarGridSpec(
            num_scalar_prefetch=1, grid=(1,), in_specs=in_specs, out_specs=out_spec
        ),
        out_shape=out_shape,
        input_output_aliases=aliases,
    )(*operands)


def level0_kernel(plan, x_shift, y_shift, img_ref, mat_ref, out_ref, send_buf, send_sem,
                  recv_sem):
    t = lax.axis_index("qx")
    u = lax.axis_index("qy")
    k0 = 2 * (jnp.right_shift(t, x_shift) & 1) + (jnp.right_shift(u, y_shift) & 1)

    def partner(f):
        tt = jnp.bitwise_xor(t, 1 << x_shift) if f & 2 else t
        uu = jnp.bitwise_xor(u, 1 << y_shift) if f & 1 else u
        return (tt, uu)

    barrier = pltpu.get_barrier_semaphore()
    for f in (1, 2, 3):
        pl.semaphore_signal(
            barrier, inc=1, device_id=partner(f), device_id_type=pl.DeviceIdType.MESH
        )
    pl.semaphore_wait(barrier, 3)
    chunks = img_ref.shape[1]
    count = img_ref.shape[2]
    copies = []
    for m in range(chunks):
        for f in (1, 2, 3, 0):
            q = jnp.bitwise_xor(k0, f)
            cur = [img_ref[q, m, g] for g in range(count)]
            for index, sets in enumerate(plan):
                cur = chain_stage(cur, mat_ref[index], sets)
            if f == 0:
                for g in range(count):
                    out_ref[m, 0, g] = cur[g]
                continue
            for g in range(count):
                send_buf[m, f - 1, g] = cur[g]
            copy = pltpu.make_async_remote_copy(
                src_ref=send_buf.at[m, f - 1],
                dst_ref=out_ref.at[m, f],
                send_sem=send_sem.at[m, f - 1],
                recv_sem=recv_sem.at[m, f - 1],
                device_id=partner(f),
                device_id_type=pl.DeviceIdType.MESH,
            )
            copy.start()
            copies.append(copy)
    for copy in copies:
        copy.wait()


def level0_forward(plan, shifts, image, mats):
    _, chunks, count, rank_size, inner_boxes = image.shape
    vmem = pltpu.MemorySpace.VMEM if hasattr(pltpu, "MemorySpace") else pltpu.VMEM
    return pl.pallas_call(
        functools.partial(level0_kernel, plan, *shifts),
        out_shape=jax.ShapeDtypeStruct(
            (chunks, 4, count, rank_size, inner_boxes), jnp.bfloat16
        ),
        in_specs=[pl.BlockSpec(memory_space=vmem)] * 2,
        out_specs=pl.BlockSpec(memory_space=vmem),
        scratch_shapes=[
            pltpu.VMEM((chunks, 3, count, rank_size, inner_boxes), jnp.bfloat16),
            pltpu.SemaphoreType.DMA((chunks, 3)),
            pltpu.SemaphoreType.DMA((chunks, 3)),
        ],
        compiler_params=pltpu.CompilerParams(
            collective_id=0, has_side_effects=True, vmem_limit_bytes=48 * 1024 * 1024
        ),
    )(image, mats)


def output_stage(pieces, wave, obs, chunk, w_mat, w_t, o_mat, o_t, step=8):
    part, rank_size, inner_boxes = pieces[0].shape
    piece_spec = pl.BlockSpec((step, rank_size, inner_boxes), lambda i: (i, 0, 0))
    field_spec = pl.BlockSpec(
        (4, None, step, rank_size, inner_boxes), lambda i: (0, chunk, i, 0, 0)
    )
    square = pl.BlockSpec(w_mat.shape, lambda i: (0, 0))
    flops = 4 * 2 * part * inner_boxes * w_mat.shape[0] * w_mat.shape[1]
    moved = part * rank_size * inner_boxes * 4 * (2 + 4 + 2 + 2)
    return pl.pallas_call(
        output_stage_kernel,
        grid=(part // step,),
        in_specs=[piece_spec] * 4 + [field_spec, field_spec] + [square] * 4,
        out_specs=[piece_spec] * 4,
        out_shape=[jax.ShapeDtypeStruct(pieces[0].shape, jnp.bfloat16)] * 4,
        cost_estimate=pl.CostEstimate(
            flops=flops, bytes_accessed=moved, transcendentals=0
        ),
    )(*pieces, wave, obs, w_mat, w_t, o_mat, o_t)


def local(image_tiles, observed, phases, interpolate, local_weights, merge_weights, output_weight):
    groups = image_tiles.shape[2]
    rank_size = image_tiles.shape[3]
    inner_boxes = image_tiles.shape[4]
    local_depth = local_weights.shape[2]
    quarter = groups // 4
    part = quarter // CHUNKS
    levels = local_weights[0, 0]
    merges = merge_weights[0, 0]
    n_x = lax.axis_size("qx")
    n_y = lax.axis_size("qy")
    t = lax.axis_index("qx")
    u = lax.axis_index("qy")
    shifts = [(level_bit(n_x, j, 2), level_bit(n_y, j, 2)) for j in range(2)]
    bits = [
        (jnp.right_shift(t, xs) & 1, jnp.right_shift(u, ys) & 1) for xs, ys in shifts
    ]

    w0 = xor_order(xor_order(merges[0], 1, *bits[0]), 0, *bits[1])
    w1 = xor_order(merges[1], 1, *bits[1])
    w1_mat = jnp.transpose(w1, (0, 2, 1, 3)).reshape(4 * rank_size, 4 * rank_size)
    w1_t = w1_mat.T
    ow_mat = jnp.einsum("st,or->sotr", jnp.eye(4, dtype=output_weight.dtype), output_weight).reshape(4 * rank_size, 4 * rank_size)
    ow_t = ow_mat.T

    shape5 = (4, CHUNKS, part, rank_size, inner_boxes)
    image = image_tiles[0, 0].reshape(shape5)
    obs = observed[0, 0].reshape(shape5)
    wave = phases[0, 0].reshape(shape5)
    k0 = 2 * bits[0][0] + bits[0][1]

    eye = jnp.eye(4, dtype=interpolate.dtype)
    spread = jnp.einsum("st,op->sotp", eye, interpolate).reshape(4 * rank_size, 4 * rank_size)
    forward_levels = [
        jnp.transpose(levels[i], (0, 2, 1, 3)).reshape(4 * rank_size, 4 * rank_size)
        for i in range(local_depth)
    ]
    forward_mats = jnp.stack([spread] + forward_levels)
    adjoint_mats = jnp.stack([w.T for w in reversed(forward_levels)] + [spread.T])
    forward_plan = [chain_sets(part, 1)] + [chain_sets(part, 4**i) for i in range(local_depth)]
    adjoint_plan = [chain_sets(part, 4**i) for i in reversed(range(local_depth))] + [
        chain_sets(part, 1)
    ]
    k0_ref = jnp.reshape(k0, (1,)).astype(jnp.int32)
    piece_shape = jax.ShapeDtypeStruct((part, rank_size, inner_boxes), jnp.bfloat16)
    whole_piece = pl.BlockSpec((part, rank_size, inner_boxes), lambda i, k: (0, 0, 0))

    def in_place(m, f):
        return pl.BlockSpec(
            (None, None, part, rank_size, inner_boxes),
            lambda i, k: (jnp.bitwise_xor(k[0], f), m, 0, 0, 0),
        )

    def local_forward(m, f):
        return chain_call(
            forward_plan, k0_ref, image, forward_mats, in_place(m, f), piece_shape, whole_piece
        )

    def local_adjoint(gradient, piece, m, f):
        return chain_call(
            adjoint_plan,
            k0_ref,
            piece,
            adjoint_mats,
            whole_piece,
            jax.ShapeDtypeStruct(shape5, jnp.bfloat16),
            in_place(m, f),
            target=gradient,
        )

    gradient = None
    level0 = level0_forward(forward_plan, shifts[0], image, forward_mats)
    for m in range(CHUNKS):
        cur = mixing(w0, level0[m], "scor,cjrl->sjol")
        pieces = exchange(cur, *shifts[1])
        terms = output_stage(pieces, wave, obs, m, w1_mat, w1_t, ow_mat, ow_t)
        back = exchange(terms, *shifts[1])
        terms = mixing(w0, jnp.stack(back), "scor,sjol->cjrl")
        back = exchange(terms, *shifts[0])
        for f in range(4):
            gradient = local_adjoint(gradient, back[f], m, f)
    return gradient.reshape(groups, rank_size, inner_boxes)[None, None]


def solution(mesh):
    placed = (
        P("qx", "qy", None, None, None),
        P("qx", "qy", None, None, None),
        P("qx", "qy", None, None, None),
        P(),
        P("qx", "qy", None, None, None, None, None),
        P("qx", "qy", None, None, None, None, None),
        P(),
    )
    return jax.shard_map(
        local,
        mesh=mesh,
        in_specs=placed,
        out_specs=P("qx", "qy", None, None, None),
        check_vma=False,
    )
```

```python
import functools
import math

import jax
import jax.numpy as jnp
from jax import lax
from jax.experimental import pallas as pl
from jax.experimental.pallas import tpu as pltpu
from jax.sharding import PartitionSpec as P

CHUNKS = 2


def mixing(weight, data, form):
    return jnp.einsum(form, weight, data, preferred_element_type=jnp.float32).astype(jnp.bfloat16)


def level_bit(axis_count, level_index, depth):
    total_bits = axis_count.bit_length() - 1
    return level_index * (total_bits - 1) // max(depth - 1, 1)


def xor_order(x, axis, x_bit, y_bit):
    moved = jnp.moveaxis(x, axis, 0)
    shape = moved.shape
    pairs = moved.reshape((2, 2) + shape[1:])
    pairs = jnp.where(y_bit == 1, jnp.flip(pairs, 1), pairs)
    pairs = jnp.where(x_bit == 1, jnp.flip(pairs, 0), pairs)
    return jnp.moveaxis(pairs.reshape(shape), 0, axis)


PI_HI = 3.140625
PI_LO = math.pi - 3.140625


def cas(phase):
    x = phase + jnp.float32(math.pi / 4)
    n = jnp.round(x * jnp.float32(1 / math.pi))
    y = (x - n * jnp.float32(PI_HI)) - n * jnp.float32(PI_LO)
    y2 = y * y
    poly = jnp.float32(-1 / 39916800)
    for k in (9, 7, 5, 3):
        poly = poly * y2 + jnp.float32((-1) ** ((k - 1) // 2) / math.factorial(k))
    sine = y + y * y2 * poly
    odd = jnp.abs(n) == 1
    scale = jnp.where(odd, jnp.float32(-math.sqrt(2.0)), jnp.float32(math.sqrt(2.0)))
    return scale * sine


def flip_send(value, flip, x_shift, y_shift):
    n_x = lax.axis_size("qx")
    n_y = lax.axis_size("qy")
    if flip == 2:
        pairs = [(i, i ^ (1 << x_shift)) for i in range(n_x)]
        return lax.ppermute(value, "qx", pairs)
    if flip == 1:
        pairs = [(i, i ^ (1 << y_shift)) for i in range(n_y)]
        return lax.ppermute(value, "qy", pairs)
    pairs = [
        (t * n_y + u, (t ^ (1 << x_shift)) * n_y + (u ^ (1 << y_shift)))
        for t in range(n_x)
        for u in range(n_y)
    ]
    return lax.ppermute(value, ("qx", "qy"), pairs)


def exchange(relative, x_shift, y_shift):
    return [relative[0]] + [flip_send(relative[f], f, x_shift, y_shift) for f in (1, 2, 3)]


def cas_kernel(phase):
    x = phase + jnp.float32(math.pi / 4)
    n = jnp.floor(x * jnp.float32(1 / math.pi) + jnp.float32(0.5))
    y = (x - n * jnp.float32(PI_HI)) - n * jnp.float32(PI_LO)
    y2 = y * y
    poly = jnp.float32(-1 / 39916800)
    for k in (9, 7, 5, 3):
        poly = poly * y2 + jnp.float32((-1) ** ((k - 1) // 2) / math.factorial(k))
    sine = y + y * y2 * poly
    half = n * jnp.float32(0.5)
    odd = half != jnp.floor(half)
    scale = jnp.where(odd, jnp.float32(-math.sqrt(2.0)), jnp.float32(math.sqrt(2.0)))
    return scale * sine


def output_stage_kernel(p0, p1, p2, p3, ph_ref, obs_ref, w_ref, wt_ref, o_ref, ot_ref,
                        t0, t1, t2, t3):
    size = p0.shape[1]
    rows = 4 * size
    step = p0.shape[0]
    pieces = (p0, p1, p2, p3)
    terms = (t0, t1, t2, t3)

    def wide(parts):
        return jnp.concatenate(parts, axis=1)

    stacked = wide([jnp.concatenate([p[j] for p in pieces], axis=0) for j in range(step)])
    merged = jnp.dot(w_ref[...], stacked, preferred_element_type=jnp.float32)
    merged = merged.astype(jnp.bfloat16)
    predicted = jnp.dot(o_ref[...], merged, preferred_element_type=jnp.float32)
    wave = cas_kernel(wide([ph_ref[:, j].reshape(rows, -1) for j in range(step)]))
    seen = wide([obs_ref[:, j].reshape(rows, -1) for j in range(step)]).astype(jnp.float32)
    residual = (wave * predicted - seen).astype(jnp.bfloat16)
    weighted = (wave * residual.astype(jnp.float32)).astype(jnp.bfloat16)
    back = jnp.dot(ot_ref[...], weighted, preferred_element_type=jnp.float32)
    back = back.astype(jnp.bfloat16)
    out = jnp.dot(wt_ref[...], back, preferred_element_type=jnp.float32)
    out = out.astype(jnp.bfloat16)
    lanes = p0.shape[2]
    for f in range(4):
        for j in range(step):
            terms[f][j] = out[f * size:(f + 1) * size, j * lanes:(j + 1) * lanes]


def chain_stage(cur, matrix, sets):
    size = cur[0].shape[0]
    lanes = cur[0].shape[1]
    wide = jnp.concatenate(
        [jnp.concatenate([cur[g] for g in group], axis=0) for group in sets], axis=1
    )
    mixed = jnp.dot(matrix, wide, preferred_element_type=jnp.float32).astype(jnp.bfloat16)
    out = list(cur)
    for b, group in enumerate(sets):
        for c, g in enumerate(group):
            out[g] = mixed[c * size:(c + 1) * size, b * lanes:(b + 1) * lanes]
    return out


def chain_sets(count, stride):
    return [
        [a * 4 * stride + c * stride + e for c in range(4)]
        for a in range(count // (4 * stride))
        for e in range(stride)
    ]


def chain_kernel(plan, k_ref, x_ref, m_ref, *rest):
    o_ref = rest[-1]
    cur = [x_ref[g] for g in range(x_ref.shape[0])]
    for index, sets in enumerate(plan):
        cur = chain_stage(cur, m_ref[index], sets)
    for g in range(len(cur)):
        o_ref[g] = cur[g]


def chain_call(plan, k0, data, mats, data_spec, out_shape, out_spec, target=None):
    in_specs = [data_spec, pl.BlockSpec(mats.shape, lambda i, k: (0, 0, 0))]
    operands = [k0, data, mats]
    aliases = {}
    if target is not None:
        in_specs.append(pl.BlockSpec(memory_space=pl.ANY))
        operands.append(target)
        aliases = {3: 0}
    return pl.pallas_call(
        functools.partial(chain_kernel, plan),
        grid_spec=pltpu.PrefetchScalarGridSpec(
            num_scalar_prefetch=1, grid=(1,), in_specs=in_specs, out_specs=out_spec
        ),
        out_shape=out_shape,
        input_output_aliases=aliases,
    )(*operands)


def output_stage(pieces, wave, obs, chunk, w_mat, w_t, o_mat, o_t, step=8):
    part, rank_size, inner_boxes = pieces[0].shape
    piece_spec = pl.BlockSpec((step, rank_size, inner_boxes), lambda i: (i, 0, 0))
    field_spec = pl.BlockSpec(
        (4, None, step, rank_size, inner_boxes), lambda i: (0, chunk, i, 0, 0)
    )
    square = pl.BlockSpec(w_mat.shape, lambda i: (0, 0))
    flops = 4 * 2 * part * inner_boxes * w_mat.shape[0] * w_mat.shape[1]
    moved = part * rank_size * inner_boxes * 4 * (2 + 4 + 2 + 2)
    return pl.pallas_call(
        output_stage_kernel,
        grid=(part // step,),
        in_specs=[piece_spec] * 4 + [field_spec, field_spec] + [square] * 4,
        out_specs=[piece_spec] * 4,
        out_shape=[jax.ShapeDtypeStruct(pieces[0].shape, jnp.bfloat16)] * 4,
        cost_estimate=pl.CostEstimate(
            flops=flops, bytes_accessed=moved, transcendentals=0
        ),
    )(*pieces, wave, obs, w_mat, w_t, o_mat, o_t)


def local(image_tiles, observed, phases, interpolate, local_weights, merge_weights, output_weight):
    groups = image_tiles.shape[2]
    rank_size = image_tiles.shape[3]
    inner_boxes = image_tiles.shape[4]
    local_depth = local_weights.shape[2]
    quarter = groups // 4
    part = quarter // CHUNKS
    levels = local_weights[0, 0]
    merges = merge_weights[0, 0]
    n_x = lax.axis_size("qx")
    n_y = lax.axis_size("qy")
    t = lax.axis_index("qx")
    u = lax.axis_index("qy")
    shifts = [(level_bit(n_x, j, 2), level_bit(n_y, j, 2)) for j in range(2)]
    bits = [
        (jnp.right_shift(t, xs) & 1, jnp.right_shift(u, ys) & 1) for xs, ys in shifts
    ]


    shape5 = (4, CHUNKS, part, rank_size, inner_boxes)
    image = image_tiles[0, 0].reshape(shape5)
    obs = observed[0, 0].reshape(shape5)
    wave = phases[0, 0].reshape(shape5)
    k0 = 2 * bits[0][0] + bits[0][1]

    eye = jnp.eye(4, dtype=interpolate.dtype)
    spread = jnp.einsum("st,op->sotp", eye, interpolate).reshape(4 * rank_size, 4 * rank_size)
    forward_levels = [
        jnp.transpose(levels[i], (0, 2, 1, 3)).reshape(4 * rank_size, 4 * rank_size)
        for i in range(local_depth)
    ]
    forward_mats = jnp.stack([spread] + forward_levels)
    forward_plan = [chain_sets(part, 1)] + [chain_sets(part, 4**i) for i in range(local_depth)]
    adjoint_plan = [chain_sets(part, 4**i) for i in reversed(range(local_depth))] + [
        chain_sets(part, 1)
    ]
    k0_ref = jnp.reshape(k0, (1,)).astype(jnp.int32)
    piece_shape = jax.ShapeDtypeStruct((part, rank_size, inner_boxes), jnp.bfloat16)
    whole_piece = pl.BlockSpec((part, rank_size, inner_boxes), lambda i, k: (0, 0, 0))

    def in_place(m, f):
        return pl.BlockSpec(
            (None, None, part, rank_size, inner_boxes),
            lambda i, k: (jnp.bitwise_xor(k[0], f), m, 0, 0, 0),
        )

    def local_forward(m, f):
        return chain_call(
            forward_plan, k0_ref, image, forward_mats, in_place(m, f), piece_shape, whole_piece
        )

    def local_adjoint(gradient, piece, m, f):
        return chain_call(
            adjoint_plan,
            k0_ref,
            piece,
            adjoint_mats,
            whole_piece,
            jax.ShapeDtypeStruct(shape5, jnp.bfloat16),
            in_place(m, f),
            target=gradient,
        )

    first = local_forward(0, 1)
    merges, output_weight, forward_levels, spread, first = lax.optimization_barrier(
        (merges, output_weight, forward_levels, spread, first)
    )
    adjoint_mats = jnp.stack([w.T for w in reversed(forward_levels)] + [spread.T])
    w0 = xor_order(xor_order(merges[0], 1, *bits[0]), 0, *bits[1])
    w1 = xor_order(merges[1], 1, *bits[1])
    w1_mat = jnp.transpose(w1, (0, 2, 1, 3)).reshape(4 * rank_size, 4 * rank_size)
    w1_t = w1_mat.T
    ow_mat = jnp.einsum("st,or->sotr", jnp.eye(4, dtype=output_weight.dtype), output_weight).reshape(4 * rank_size, 4 * rank_size)
    ow_t = ow_mat.T

    gradient = None
    for m in range(CHUNKS):
        coef = [first if (m, f) == (0, 1) else local_forward(m, f) for f in range(4)]
        pieces = exchange(coef, *shifts[0])
        cur = mixing(w0, jnp.stack(pieces), "scor,cjrl->sjol")
        pieces = exchange(cur, *shifts[1])
        terms = output_stage(pieces, wave, obs, m, w1_mat, w1_t, ow_mat, ow_t)
        back = exchange(terms, *shifts[1])
        terms = mixing(w0, jnp.stack(back), "scor,sjol->cjrl")
        back = exchange(terms, *shifts[0])
        for f in range(4):
            gradient = local_adjoint(gradient, back[f], m, f)
    return gradient.reshape(groups, rank_size, inner_boxes)[None, None]


def solution(mesh):
    placed = (
        P("qx", "qy", None, None, None),
        P("qx", "qy", None, None, None),
        P("qx", "qy", None, None, None),
        P(),
        P("qx", "qy", None, None, None, None, None),
        P("qx", "qy", None, None, None, None, None),
        P(),
    )
    return jax.shard_map(
        local,
        mesh=mesh,
        in_specs=placed,
        out_specs=P("qx", "qy", None, None, None),
        check_vma=False,
    )
```

```python
import functools
import math

import jax
import jax.numpy as jnp
from jax import lax
from jax.experimental import pallas as pl
from jax.experimental.pallas import tpu as pltpu
from jax.sharding import PartitionSpec as P

CHUNKS = 2


def mixing(weight, data, form):
    return jnp.einsum(form, weight, data, preferred_element_type=jnp.float32).astype(jnp.bfloat16)


def level_bit(axis_count, level_index, depth):
    total_bits = axis_count.bit_length() - 1
    return level_index * (total_bits - 1) // max(depth - 1, 1)


def xor_order(x, axis, x_bit, y_bit):
    moved = jnp.moveaxis(x, axis, 0)
    shape = moved.shape
    pairs = moved.reshape((2, 2) + shape[1:])
    pairs = jnp.where(y_bit == 1, jnp.flip(pairs, 1), pairs)
    pairs = jnp.where(x_bit == 1, jnp.flip(pairs, 0), pairs)
    return jnp.moveaxis(pairs.reshape(shape), 0, axis)


PI_HI = 3.140625
PI_LO = math.pi - 3.140625


def cas(phase):
    x = phase + jnp.float32(math.pi / 4)
    n = jnp.round(x * jnp.float32(1 / math.pi))
    y = (x - n * jnp.float32(PI_HI)) - n * jnp.float32(PI_LO)
    y2 = y * y
    poly = jnp.float32(-1 / 39916800)
    for k in (9, 7, 5, 3):
        poly = poly * y2 + jnp.float32((-1) ** ((k - 1) // 2) / math.factorial(k))
    sine = y + y * y2 * poly
    odd = jnp.abs(n) == 1
    scale = jnp.where(odd, jnp.float32(-math.sqrt(2.0)), jnp.float32(math.sqrt(2.0)))
    return scale * sine


def flip_send(value, flip, x_shift, y_shift):
    n_x = lax.axis_size("qx")
    n_y = lax.axis_size("qy")
    if flip == 2:
        pairs = [(i, i ^ (1 << x_shift)) for i in range(n_x)]
        return lax.ppermute(value, "qx", pairs)
    if flip == 1:
        pairs = [(i, i ^ (1 << y_shift)) for i in range(n_y)]
        return lax.ppermute(value, "qy", pairs)
    pairs = [
        (t * n_y + u, (t ^ (1 << x_shift)) * n_y + (u ^ (1 << y_shift)))
        for t in range(n_x)
        for u in range(n_y)
    ]
    return lax.ppermute(value, ("qx", "qy"), pairs)


def exchange(relative, x_shift, y_shift):
    return [relative[0]] + [flip_send(relative[f], f, x_shift, y_shift) for f in (1, 2, 3)]


def cas_kernel(phase):
    x = phase + jnp.float32(math.pi / 4)
    n = jnp.floor(x * jnp.float32(1 / math.pi) + jnp.float32(0.5))
    y = (x - n * jnp.float32(PI_HI)) - n * jnp.float32(PI_LO)
    y2 = y * y
    poly = jnp.float32(-1 / 39916800)
    for k in (9, 7, 5, 3):
        poly = poly * y2 + jnp.float32((-1) ** ((k - 1) // 2) / math.factorial(k))
    sine = y + y * y2 * poly
    half = n * jnp.float32(0.5)
    odd = half != jnp.floor(half)
    scale = jnp.where(odd, jnp.float32(-math.sqrt(2.0)), jnp.float32(math.sqrt(2.0)))
    return scale * sine


def output_stage_kernel(p0, p1, p2, p3, ph_ref, obs_ref, w_ref, wt_ref, o_ref, ot_ref,
                        t0, t1, t2, t3):
    size = p0.shape[1]
    rows = 4 * size
    step = p0.shape[0]
    pieces = (p0, p1, p2, p3)
    terms = (t0, t1, t2, t3)

    def wide(parts):
        return jnp.concatenate(parts, axis=1)

    stacked = wide([jnp.concatenate([p[j] for p in pieces], axis=0) for j in range(step)])
    merged = jnp.dot(w_ref[...], stacked, preferred_element_type=jnp.float32)
    merged = merged.astype(jnp.bfloat16)
    predicted = jnp.dot(o_ref[...], merged, preferred_element_type=jnp.float32)
    wave = cas_kernel(wide([ph_ref[:, j].reshape(rows, -1) for j in range(step)]))
    seen = wide([obs_ref[:, j].reshape(rows, -1) for j in range(step)]).astype(jnp.float32)
    residual = (wave * predicted - seen).astype(jnp.bfloat16)
    weighted = (wave * residual.astype(jnp.float32)).astype(jnp.bfloat16)
    back = jnp.dot(ot_ref[...], weighted, preferred_element_type=jnp.float32)
    back = back.astype(jnp.bfloat16)
    out = jnp.dot(wt_ref[...], back, preferred_element_type=jnp.float32)
    out = out.astype(jnp.bfloat16)
    lanes = p0.shape[2]
    for f in range(4):
        for j in range(step):
            terms[f][j] = out[f * size:(f + 1) * size, j * lanes:(j + 1) * lanes]


def chain_stage(cur, matrix, sets):
    size = cur[0].shape[0]
    lanes = cur[0].shape[1]
    wide = jnp.concatenate(
        [jnp.concatenate([cur[g] for g in group], axis=0) for group in sets], axis=1
    )
    mixed = jnp.dot(matrix, wide, preferred_element_type=jnp.float32).astype(jnp.bfloat16)
    out = list(cur)
    for b, group in enumerate(sets):
        for c, g in enumerate(group):
            out[g] = mixed[c * size:(c + 1) * size, b * lanes:(b + 1) * lanes]
    return out


def raw_stage(cur, block_of, sets):
    size = cur[0].shape[0]
    lanes = cur[0].shape[1]
    wide = jnp.concatenate(
        [jnp.concatenate([cur[g] for g in group], axis=0) for group in sets], axis=1
    )
    rows = []
    for k in range(4):
        total = None
        for c in range(4):
            block = block_of(k, c)
            if block is None:
                continue
            term = jnp.dot(block, wide[c * size:(c + 1) * size], preferred_element_type=jnp.float32)
            total = term if total is None else total + term
        rows.append(total.astype(jnp.bfloat16))
    mixed = jnp.concatenate(rows, axis=0)
    out = list(cur)
    for b, group in enumerate(sets):
        for c, g in enumerate(group):
            out[g] = mixed[c * size:(c + 1) * size, b * lanes:(b + 1) * lanes]
    return out


def raw_chain_kernel(plan, k_ref, x_ref, lv_ref, ip_ref, o_ref):
    cur = [x_ref[g] for g in range(x_ref.shape[0])]
    cur = raw_stage(cur, lambda k, c: ip_ref[...] if k == c else None, plan[0])
    for index, sets in enumerate(plan[1:]):
        cur = raw_stage(cur, lambda k, c: lv_ref[index, k, c], sets)
    for g in range(len(cur)):
        o_ref[g] = cur[g]


def raw_chain_call(plan, k0, data, levels, interpolate, data_spec, out_shape, out_spec):
    zeros = (0,) * levels.ndim
    return pl.pallas_call(
        functools.partial(raw_chain_kernel, plan),
        grid_spec=pltpu.PrefetchScalarGridSpec(
            num_scalar_prefetch=1,
            grid=(1,),
            in_specs=[
                data_spec,
                pl.BlockSpec(levels.shape, lambda i, k: zeros),
                pl.BlockSpec(interpolate.shape, lambda i, k: (0, 0)),
            ],
            out_specs=out_spec,
        ),
        out_shape=out_shape,
    )(k0, data, levels, interpolate)


def chain_sets(count, stride):
    return [
        [a * 4 * stride + c * stride + e for c in range(4)]
        for a in range(count // (4 * stride))
        for e in range(stride)
    ]


def chain_kernel(plan, k_ref, x_ref, m_ref, *rest):
    o_ref = rest[-1]
    cur = [x_ref[g] for g in range(x_ref.shape[0])]
    for index, sets in enumerate(plan):
        cur = chain_stage(cur, m_ref[index], sets)
    for g in range(len(cur)):
        o_ref[g] = cur[g]


def chain_call(plan, k0, data, mats, data_spec, out_shape, out_spec, target=None):
    in_specs = [data_spec, pl.BlockSpec(mats.shape, lambda i, k: (0, 0, 0))]
    operands = [k0, data, mats]
    aliases = {}
    if target is not None:
        in_specs.append(pl.BlockSpec(memory_space=pl.ANY))
        operands.append(target)
        aliases = {3: 0}
    return pl.pallas_call(
        functools.partial(chain_kernel, plan),
        grid_spec=pltpu.PrefetchScalarGridSpec(
            num_scalar_prefetch=1, grid=(1,), in_specs=in_specs, out_specs=out_spec
        ),
        out_shape=out_shape,
        input_output_aliases=aliases,
    )(*operands)


def output_stage(pieces, wave, obs, chunk, w_mat, w_t, o_mat, o_t, step=8):
    part, rank_size, inner_boxes = pieces[0].shape
    piece_spec = pl.BlockSpec((step, rank_size, inner_boxes), lambda i: (i, 0, 0))
    field_spec = pl.BlockSpec(
        (4, None, step, rank_size, inner_boxes), lambda i: (0, chunk, i, 0, 0)
    )
    square = pl.BlockSpec(w_mat.shape, lambda i: (0, 0))
    flops = 4 * 2 * part * inner_boxes * w_mat.shape[0] * w_mat.shape[1]
    moved = part * rank_size * inner_boxes * 4 * (2 + 4 + 2 + 2)
    return pl.pallas_call(
        output_stage_kernel,
        grid=(part // step,),
        in_specs=[piece_spec] * 4 + [field_spec, field_spec] + [square] * 4,
        out_specs=[piece_spec] * 4,
        out_shape=[jax.ShapeDtypeStruct(pieces[0].shape, jnp.bfloat16)] * 4,
        cost_estimate=pl.CostEstimate(
            flops=flops, bytes_accessed=moved, transcendentals=0
        ),
    )(*pieces, wave, obs, w_mat, w_t, o_mat, o_t)


def local(image_tiles, observed, phases, interpolate, local_weights, merge_weights, output_weight):
    groups = image_tiles.shape[2]
    rank_size = image_tiles.shape[3]
    inner_boxes = image_tiles.shape[4]
    local_depth = local_weights.shape[2]
    quarter = groups // 4
    part = quarter // CHUNKS
    levels = local_weights[0, 0]
    merges = merge_weights[0, 0]
    n_x = lax.axis_size("qx")
    n_y = lax.axis_size("qy")
    t = lax.axis_index("qx")
    u = lax.axis_index("qy")
    shifts = [(level_bit(n_x, j, 2), level_bit(n_y, j, 2)) for j in range(2)]
    bits = [
        (jnp.right_shift(t, xs) & 1, jnp.right_shift(u, ys) & 1) for xs, ys in shifts
    ]


    shape5 = (4, CHUNKS, part, rank_size, inner_boxes)
    image = image_tiles[0, 0].reshape(shape5)
    obs = observed[0, 0].reshape(shape5)
    wave = phases[0, 0].reshape(shape5)
    k0 = 2 * bits[0][0] + bits[0][1]

    eye = jnp.eye(4, dtype=interpolate.dtype)
    spread = jnp.einsum("st,op->sotp", eye, interpolate).reshape(4 * rank_size, 4 * rank_size)
    forward_levels = [
        jnp.transpose(levels[i], (0, 2, 1, 3)).reshape(4 * rank_size, 4 * rank_size)
        for i in range(local_depth)
    ]
    forward_mats = jnp.stack([spread] + forward_levels)
    forward_plan = [chain_sets(part, 1)] + [chain_sets(part, 4**i) for i in range(local_depth)]
    adjoint_plan = [chain_sets(part, 4**i) for i in reversed(range(local_depth))] + [
        chain_sets(part, 1)
    ]
    k0_ref = jnp.reshape(k0, (1,)).astype(jnp.int32)
    piece_shape = jax.ShapeDtypeStruct((part, rank_size, inner_boxes), jnp.bfloat16)
    whole_piece = pl.BlockSpec((part, rank_size, inner_boxes), lambda i, k: (0, 0, 0))

    def in_place(m, f):
        return pl.BlockSpec(
            (None, None, part, rank_size, inner_boxes),
            lambda i, k: (jnp.bitwise_xor(k[0], f), m, 0, 0, 0),
        )

    def local_forward(m, f):
        return chain_call(
            forward_plan, k0_ref, image, forward_mats, in_place(m, f), piece_shape, whole_piece
        )

    def local_adjoint(gradient, piece, m, f):
        return chain_call(
            adjoint_plan,
            k0_ref,
            piece,
            adjoint_mats,
            whole_piece,
            jax.ShapeDtypeStruct(shape5, jnp.bfloat16),
            in_place(m, f),
            target=gradient,
        )

    first = raw_chain_call(
        forward_plan, k0_ref, image, levels, interpolate, in_place(0, 1), piece_shape, whole_piece
    )
    merges, output_weight, forward_levels, spread, first = lax.optimization_barrier(
        (merges, output_weight, forward_levels, spread, first)
    )
    adjoint_mats = jnp.stack([w.T for w in reversed(forward_levels)] + [spread.T])
    w0 = xor_order(xor_order(merges[0], 1, *bits[0]), 0, *bits[1])
    w1 = xor_order(merges[1], 1, *bits[1])
    w1_mat = jnp.transpose(w1, (0, 2, 1, 3)).reshape(4 * rank_size, 4 * rank_size)
    w1_t = w1_mat.T
    ow_mat = jnp.einsum("st,or->sotr", jnp.eye(4, dtype=output_weight.dtype), output_weight).reshape(4 * rank_size, 4 * rank_size)
    ow_t = ow_mat.T

    gradient = None
    for m in range(CHUNKS):
        coef = [first if (m, f) == (0, 1) else local_forward(m, f) for f in range(4)]
        pieces = exchange(coef, *shifts[0])
        cur = mixing(w0, jnp.stack(pieces), "scor,cjrl->sjol")
        pieces = exchange(cur, *shifts[1])
        terms = output_stage(pieces, wave, obs, m, w1_mat, w1_t, ow_mat, ow_t)
        back = exchange(terms, *shifts[1])
        terms = mixing(w0, jnp.stack(back), "scor,sjol->cjrl")
        back = exchange(terms, *shifts[0])
        for f in range(4):
            gradient = local_adjoint(gradient, back[f], m, f)
    return gradient.reshape(groups, rank_size, inner_boxes)[None, None]


def solution(mesh):
    placed = (
        P("qx", "qy", None, None, None),
        P("qx", "qy", None, None, None),
        P("qx", "qy", None, None, None),
        P(),
        P("qx", "qy", None, None, None, None, None),
        P("qx", "qy", None, None, None, None, None),
        P(),
    )
    return jax.shard_map(
        local,
        mesh=mesh,
        in_specs=placed,
        out_specs=P("qx", "qy", None, None, None),
        check_vma=False,
    )
```

```python
import functools
import math

import jax
import jax.numpy as jnp
from jax import lax
from jax.experimental import pallas as pl
from jax.experimental.pallas import tpu as pltpu
from jax.sharding import PartitionSpec as P

CHUNKS = 2


def mixing(weight, data, form):
    return jnp.einsum(form, weight, data, preferred_element_type=jnp.float32).astype(jnp.bfloat16)


def level_bit(axis_count, level_index, depth):
    total_bits = axis_count.bit_length() - 1
    return level_index * (total_bits - 1) // max(depth - 1, 1)


def xor_order(x, axis, x_bit, y_bit):
    moved = jnp.moveaxis(x, axis, 0)
    shape = moved.shape
    pairs = moved.reshape((2, 2) + shape[1:])
    pairs = jnp.where(y_bit == 1, jnp.flip(pairs, 1), pairs)
    pairs = jnp.where(x_bit == 1, jnp.flip(pairs, 0), pairs)
    return jnp.moveaxis(pairs.reshape(shape), 0, axis)


PI_HI = 3.140625
PI_LO = math.pi - 3.140625


def cas(phase):
    x = phase + jnp.float32(math.pi / 4)
    n = jnp.round(x * jnp.float32(1 / math.pi))
    y = (x - n * jnp.float32(PI_HI)) - n * jnp.float32(PI_LO)
    y2 = y * y
    poly = jnp.float32(-1 / 39916800)
    for k in (9, 7, 5, 3):
        poly = poly * y2 + jnp.float32((-1) ** ((k - 1) // 2) / math.factorial(k))
    sine = y + y * y2 * poly
    odd = jnp.abs(n) == 1
    scale = jnp.where(odd, jnp.float32(-math.sqrt(2.0)), jnp.float32(math.sqrt(2.0)))
    return scale * sine


def flip_send(value, flip, x_shift, y_shift):
    n_x = lax.axis_size("qx")
    n_y = lax.axis_size("qy")
    if flip == 2:
        pairs = [(i, i ^ (1 << x_shift)) for i in range(n_x)]
        return lax.ppermute(value, "qx", pairs)
    if flip == 1:
        pairs = [(i, i ^ (1 << y_shift)) for i in range(n_y)]
        return lax.ppermute(value, "qy", pairs)
    pairs = [
        (t * n_y + u, (t ^ (1 << x_shift)) * n_y + (u ^ (1 << y_shift)))
        for t in range(n_x)
        for u in range(n_y)
    ]
    return lax.ppermute(value, ("qx", "qy"), pairs)


def exchange(relative, x_shift, y_shift):
    return [relative[0]] + [flip_send(relative[f], f, x_shift, y_shift) for f in (1, 2, 3)]


def cas_kernel(phase):
    x = phase + jnp.float32(math.pi / 4)
    n = jnp.floor(x * jnp.float32(1 / math.pi) + jnp.float32(0.5))
    y = (x - n * jnp.float32(PI_HI)) - n * jnp.float32(PI_LO)
    y2 = y * y
    poly = jnp.float32(-1 / 39916800)
    for k in (9, 7, 5, 3):
        poly = poly * y2 + jnp.float32((-1) ** ((k - 1) // 2) / math.factorial(k))
    sine = y + y * y2 * poly
    half = n * jnp.float32(0.5)
    odd = half != jnp.floor(half)
    scale = jnp.where(odd, jnp.float32(-math.sqrt(2.0)), jnp.float32(math.sqrt(2.0)))
    return scale * sine


def output_stage_kernel(p0, p1, p2, p3, ph_ref, obs_ref, w_ref, wt_ref, o_ref, ot_ref,
                        t0, t1, t2, t3):
    size = p0.shape[1]
    rows = 4 * size
    step = p0.shape[0]
    pieces = (p0, p1, p2, p3)
    terms = (t0, t1, t2, t3)

    def wide(parts):
        return jnp.concatenate(parts, axis=1)

    stacked = wide([jnp.concatenate([p[j] for p in pieces], axis=0) for j in range(step)])
    merged = jnp.dot(w_ref[...], stacked, preferred_element_type=jnp.float32)
    merged = merged.astype(jnp.bfloat16)
    predicted = jnp.dot(o_ref[...], merged, preferred_element_type=jnp.float32)
    wave = cas_kernel(wide([ph_ref[:, j].reshape(rows, -1) for j in range(step)]))
    seen = wide([obs_ref[:, j].reshape(rows, -1) for j in range(step)]).astype(jnp.float32)
    residual = (wave * predicted - seen).astype(jnp.bfloat16)
    weighted = (wave * residual.astype(jnp.float32)).astype(jnp.bfloat16)
    back = jnp.dot(ot_ref[...], weighted, preferred_element_type=jnp.float32)
    back = back.astype(jnp.bfloat16)
    out = jnp.dot(wt_ref[...], back, preferred_element_type=jnp.float32)
    out = out.astype(jnp.bfloat16)
    lanes = p0.shape[2]
    for f in range(4):
        for j in range(step):
            terms[f][j] = out[f * size:(f + 1) * size, j * lanes:(j + 1) * lanes]


def chain_stage(cur, matrix, sets):
    size = cur[0].shape[0]
    lanes = cur[0].shape[1]
    wide = jnp.concatenate(
        [jnp.concatenate([cur[g] for g in group], axis=0) for group in sets], axis=1
    )
    mixed = jnp.dot(matrix, wide, preferred_element_type=jnp.float32).astype(jnp.bfloat16)
    out = list(cur)
    for b, group in enumerate(sets):
        for c, g in enumerate(group):
            out[g] = mixed[c * size:(c + 1) * size, b * lanes:(b + 1) * lanes]
    return out


def raw_stage(cur, block_of, sets):
    size = cur[0].shape[0]
    lanes = cur[0].shape[1]
    wide = jnp.concatenate(
        [jnp.concatenate([cur[g] for g in group], axis=0) for group in sets], axis=1
    )
    rows = []
    for k in range(4):
        total = None
        for c in range(4):
            block = block_of(k, c)
            if block is None:
                continue
            term = jnp.dot(block, wide[c * size:(c + 1) * size], preferred_element_type=jnp.float32)
            total = term if total is None else total + term
        rows.append(total.astype(jnp.bfloat16))
    mixed = jnp.concatenate(rows, axis=0)
    out = list(cur)
    for b, group in enumerate(sets):
        for c, g in enumerate(group):
            out[g] = mixed[c * size:(c + 1) * size, b * lanes:(b + 1) * lanes]
    return out


def raw_chain_kernel(plan, k_ref, x_ref, lv_ref, ip_ref, o_ref):
    cur = [x_ref[g] for g in range(x_ref.shape[0])]
    cur = raw_stage(cur, lambda k, c: ip_ref[...] if k == c else None, plan[0])
    for index, sets in enumerate(plan[1:]):
        cur = raw_stage(cur, lambda k, c: lv_ref[index, k, c], sets)
    for g in range(len(cur)):
        o_ref[g] = cur[g]


def raw_chain_call(plan, k0, data, levels, interpolate, data_spec, out_shape, out_spec):
    zeros = (0,) * levels.ndim
    return pl.pallas_call(
        functools.partial(raw_chain_kernel, plan),
        grid_spec=pltpu.PrefetchScalarGridSpec(
            num_scalar_prefetch=1,
            grid=(1,),
            in_specs=[
                data_spec,
                pl.BlockSpec(levels.shape, lambda i, k: zeros),
                pl.BlockSpec(interpolate.shape, lambda i, k: (0, 0)),
            ],
            out_specs=out_spec,
        ),
        out_shape=out_shape,
    )(k0, data, levels, interpolate)


def chain_sets(count, stride):
    return [
        [a * 4 * stride + c * stride + e for c in range(4)]
        for a in range(count // (4 * stride))
        for e in range(stride)
    ]


def chain_kernel(plan, k_ref, x_ref, m_ref, *rest):
    o_ref = rest[-1]
    cur = [x_ref[g] for g in range(x_ref.shape[0])]
    for index, sets in enumerate(plan):
        cur = chain_stage(cur, m_ref[index], sets)
    for g in range(len(cur)):
        o_ref[g] = cur[g]


def chain_call(plan, k0, data, mats, data_spec, out_shape, out_spec, target=None):
    in_specs = [data_spec, pl.BlockSpec(mats.shape, lambda i, k: (0, 0, 0))]
    operands = [k0, data, mats]
    aliases = {}
    if target is not None:
        in_specs.append(pl.BlockSpec(memory_space=pl.ANY))
        operands.append(target)
        aliases = {3: 0}
    return pl.pallas_call(
        functools.partial(chain_kernel, plan),
        grid_spec=pltpu.PrefetchScalarGridSpec(
            num_scalar_prefetch=1, grid=(1,), in_specs=in_specs, out_specs=out_spec
        ),
        out_shape=out_shape,
        input_output_aliases=aliases,
    )(*operands)


def output_stage(pieces, wave, obs, chunk, w_mat, w_t, o_mat, o_t, step=8):
    part, rank_size, inner_boxes = pieces[0].shape
    piece_spec = pl.BlockSpec((step, rank_size, inner_boxes), lambda i: (i, 0, 0))
    field_spec = pl.BlockSpec(
        (4, None, step, rank_size, inner_boxes), lambda i: (0, chunk, i, 0, 0)
    )
    square = pl.BlockSpec(w_mat.shape, lambda i: (0, 0))
    flops = 4 * 2 * part * inner_boxes * w_mat.shape[0] * w_mat.shape[1]
    moved = part * rank_size * inner_boxes * 4 * (2 + 4 + 2 + 2)
    return pl.pallas_call(
        output_stage_kernel,
        grid=(part // step,),
        in_specs=[piece_spec] * 4 + [field_spec, field_spec] + [square] * 4,
        out_specs=[piece_spec] * 4,
        out_shape=[jax.ShapeDtypeStruct(pieces[0].shape, jnp.bfloat16)] * 4,
        cost_estimate=pl.CostEstimate(
            flops=flops, bytes_accessed=moved, transcendentals=0
        ),
    )(*pieces, wave, obs, w_mat, w_t, o_mat, o_t)


def local(image_tiles, observed, phases, interpolate, local_weights, merge_weights, output_weight):
    groups = image_tiles.shape[2]
    rank_size = image_tiles.shape[3]
    inner_boxes = image_tiles.shape[4]
    local_depth = local_weights.shape[2]
    quarter = groups // 4
    part = quarter // CHUNKS
    levels = local_weights[0, 0]
    merges = merge_weights[0, 0]
    n_x = lax.axis_size("qx")
    n_y = lax.axis_size("qy")
    t = lax.axis_index("qx")
    u = lax.axis_index("qy")
    shifts = [(level_bit(n_x, j, 2), level_bit(n_y, j, 2)) for j in range(2)]
    bits = [
        (jnp.right_shift(t, xs) & 1, jnp.right_shift(u, ys) & 1) for xs, ys in shifts
    ]


    shape5 = (4, CHUNKS, part, rank_size, inner_boxes)
    image = image_tiles[0, 0].reshape(shape5)
    obs = observed[0, 0].reshape(shape5)
    wave = phases[0, 0].reshape(shape5)
    k0 = 2 * bits[0][0] + bits[0][1]

    eye = jnp.eye(4, dtype=interpolate.dtype)
    spread = jnp.einsum("st,op->sotp", eye, interpolate).reshape(4 * rank_size, 4 * rank_size)
    forward_levels = [
        jnp.transpose(levels[i], (0, 2, 1, 3)).reshape(4 * rank_size, 4 * rank_size)
        for i in range(local_depth)
    ]
    forward_mats = jnp.stack([spread] + forward_levels)
    forward_plan = [chain_sets(part, 1)] + [chain_sets(part, 4**i) for i in range(local_depth)]
    adjoint_plan = [chain_sets(part, 4**i) for i in reversed(range(local_depth))] + [
        chain_sets(part, 1)
    ]
    k0_ref = jnp.reshape(k0, (1,)).astype(jnp.int32)
    piece_shape = jax.ShapeDtypeStruct((part, rank_size, inner_boxes), jnp.bfloat16)
    whole_piece = pl.BlockSpec((part, rank_size, inner_boxes), lambda i, k: (0, 0, 0))

    def in_place(m, f):
        return pl.BlockSpec(
            (None, None, part, rank_size, inner_boxes),
            lambda i, k: (jnp.bitwise_xor(k[0], f), m, 0, 0, 0),
        )

    def local_forward(m, f):
        return chain_call(
            forward_plan, k0_ref, image, forward_mats, in_place(m, f), piece_shape, whole_piece
        )

    def local_adjoint(gradient, piece, m, f):
        return chain_call(
            adjoint_plan,
            k0_ref,
            piece,
            adjoint_mats,
            whole_piece,
            jax.ShapeDtypeStruct(shape5, jnp.bfloat16),
            in_place(m, f),
            target=gradient,
        )

    first = [
        raw_chain_call(
            forward_plan, k0_ref, image, levels, interpolate, in_place(0, f), piece_shape,
            whole_piece,
        )
        for f in (1, 2, 3)
    ]
    merges, output_weight, forward_levels, spread, first = lax.optimization_barrier(
        (merges, output_weight, forward_levels, spread, first)
    )
    adjoint_mats = jnp.stack([w.T for w in reversed(forward_levels)] + [spread.T])
    w0 = xor_order(xor_order(merges[0], 1, *bits[0]), 0, *bits[1])
    w1 = xor_order(merges[1], 1, *bits[1])
    w1_mat = jnp.transpose(w1, (0, 2, 1, 3)).reshape(4 * rank_size, 4 * rank_size)
    w1_t = w1_mat.T
    ow_mat = jnp.einsum("st,or->sotr", jnp.eye(4, dtype=output_weight.dtype), output_weight).reshape(4 * rank_size, 4 * rank_size)
    ow_t = ow_mat.T

    gradient = None
    for m in range(CHUNKS):
        coef = [first[f - 1] if m == 0 and f else local_forward(m, f) for f in range(4)]
        pieces = exchange(coef, *shifts[0])
        cur = mixing(w0, jnp.stack(pieces), "scor,cjrl->sjol")
        pieces = exchange(cur, *shifts[1])
        terms = output_stage(pieces, wave, obs, m, w1_mat, w1_t, ow_mat, ow_t)
        back = exchange(terms, *shifts[1])
        terms = mixing(w0, jnp.stack(back), "scor,sjol->cjrl")
        back = exchange(terms, *shifts[0])
        for f in range(4):
            gradient = local_adjoint(gradient, back[f], m, f)
    return gradient.reshape(groups, rank_size, inner_boxes)[None, None]


def solution(mesh):
    placed = (
        P("qx", "qy", None, None, None),
        P("qx", "qy", None, None, None),
        P("qx", "qy", None, None, None),
        P(),
        P("qx", "qy", None, None, None, None, None),
        P("qx", "qy", None, None, None, None, None),
        P(),
    )
    return jax.shard_map(
        local,
        mesh=mesh,
        in_specs=placed,
        out_specs=P("qx", "qy", None, None, None),
        check_vma=False,
    )
```

```python
import functools
import math

import jax
import jax.numpy as jnp
from jax import lax
from jax.experimental import pallas as pl
from jax.experimental.pallas import tpu as pltpu
from jax.sharding import PartitionSpec as P

CHUNKS = 2


def mixing(weight, data, form):
    return jnp.einsum(form, weight, data, preferred_element_type=jnp.float32).astype(jnp.bfloat16)


def level_bit(axis_count, level_index, depth):
    total_bits = axis_count.bit_length() - 1
    return level_index * (total_bits - 1) // max(depth - 1, 1)


def xor_order(x, axis, x_bit, y_bit):
    moved = jnp.moveaxis(x, axis, 0)
    shape = moved.shape
    pairs = moved.reshape((2, 2) + shape[1:])
    pairs = jnp.where(y_bit == 1, jnp.flip(pairs, 1), pairs)
    pairs = jnp.where(x_bit == 1, jnp.flip(pairs, 0), pairs)
    return jnp.moveaxis(pairs.reshape(shape), 0, axis)


PI_HI = 3.140625
PI_LO = math.pi - 3.140625


def cas(phase):
    x = phase + jnp.float32(math.pi / 4)
    n = jnp.round(x * jnp.float32(1 / math.pi))
    y = (x - n * jnp.float32(PI_HI)) - n * jnp.float32(PI_LO)
    y2 = y * y
    poly = jnp.float32(-1 / 39916800)
    for k in (9, 7, 5, 3):
        poly = poly * y2 + jnp.float32((-1) ** ((k - 1) // 2) / math.factorial(k))
    sine = y + y * y2 * poly
    odd = jnp.abs(n) == 1
    scale = jnp.where(odd, jnp.float32(-math.sqrt(2.0)), jnp.float32(math.sqrt(2.0)))
    return scale * sine


def flip_send(value, flip, x_shift, y_shift):
    n_x = lax.axis_size("qx")
    n_y = lax.axis_size("qy")
    if flip == 2:
        pairs = [(i, i ^ (1 << x_shift)) for i in range(n_x)]
        return lax.ppermute(value, "qx", pairs)
    if flip == 1:
        pairs = [(i, i ^ (1 << y_shift)) for i in range(n_y)]
        return lax.ppermute(value, "qy", pairs)
    pairs = [
        (t * n_y + u, (t ^ (1 << x_shift)) * n_y + (u ^ (1 << y_shift)))
        for t in range(n_x)
        for u in range(n_y)
    ]
    return lax.ppermute(value, ("qx", "qy"), pairs)


def exchange(relative, x_shift, y_shift):
    return [relative[0]] + [flip_send(relative[f], f, x_shift, y_shift) for f in (1, 2, 3)]


def cas_kernel(phase):
    x = phase + jnp.float32(math.pi / 4)
    n = jnp.floor(x * jnp.float32(1 / math.pi) + jnp.float32(0.5))
    y = (x - n * jnp.float32(PI_HI)) - n * jnp.float32(PI_LO)
    y2 = y * y
    poly = jnp.float32(-1 / 39916800)
    for k in (9, 7, 5, 3):
        poly = poly * y2 + jnp.float32((-1) ** ((k - 1) // 2) / math.factorial(k))
    sine = y + y * y2 * poly
    half = n * jnp.float32(0.5)
    odd = half != jnp.floor(half)
    scale = jnp.where(odd, jnp.float32(-math.sqrt(2.0)), jnp.float32(math.sqrt(2.0)))
    return scale * sine


def output_stage_kernel(p0, p1, p2, p3, ph_ref, obs_ref, w_ref, wt_ref, o_ref, ot_ref,
                        t0, t1, t2, t3):
    size = p0.shape[1]
    rows = 4 * size
    step = p0.shape[0]
    pieces = (p0, p1, p2, p3)
    terms = (t0, t1, t2, t3)

    def wide(parts):
        return jnp.concatenate(parts, axis=1)

    stacked = wide([jnp.concatenate([p[j] for p in pieces], axis=0) for j in range(step)])
    merged = jnp.dot(w_ref[...], stacked, preferred_element_type=jnp.float32)
    merged = merged.astype(jnp.bfloat16)
    predicted = jnp.dot(o_ref[...], merged, preferred_element_type=jnp.float32)
    wave = cas_kernel(wide([ph_ref[:, j].reshape(rows, -1) for j in range(step)]))
    seen = wide([obs_ref[:, j].reshape(rows, -1) for j in range(step)]).astype(jnp.float32)
    residual = (wave * predicted - seen).astype(jnp.bfloat16)
    weighted = (wave * residual.astype(jnp.float32)).astype(jnp.bfloat16)
    back = jnp.dot(ot_ref[...], weighted, preferred_element_type=jnp.float32)
    back = back.astype(jnp.bfloat16)
    out = jnp.dot(wt_ref[...], back, preferred_element_type=jnp.float32)
    out = out.astype(jnp.bfloat16)
    lanes = p0.shape[2]
    for f in range(4):
        for j in range(step):
            terms[f][j] = out[f * size:(f + 1) * size, j * lanes:(j + 1) * lanes]


def chain_stage(cur, matrix, sets):
    size = cur[0].shape[0]
    lanes = cur[0].shape[1]
    wide = jnp.concatenate(
        [jnp.concatenate([cur[g] for g in group], axis=0) for group in sets], axis=1
    )
    mixed = jnp.dot(matrix, wide, preferred_element_type=jnp.float32).astype(jnp.bfloat16)
    out = list(cur)
    for b, group in enumerate(sets):
        for c, g in enumerate(group):
            out[g] = mixed[c * size:(c + 1) * size, b * lanes:(b + 1) * lanes]
    return out


def chain_sets(count, stride):
    return [
        [a * 4 * stride + c * stride + e for c in range(4)]
        for a in range(count // (4 * stride))
        for e in range(stride)
    ]


def chain_kernel(plan, k_ref, x_ref, m_ref, *rest):
    o_ref = rest[-1]
    cur = [x_ref[g] for g in range(x_ref.shape[0])]
    for index, sets in enumerate(plan):
        cur = chain_stage(cur, m_ref[index], sets)
    for g in range(len(cur)):
        o_ref[g] = cur[g]


def chain_call(plan, k0, data, mats, data_spec, out_shape, out_spec, target=None):
    in_specs = [data_spec, pl.BlockSpec(mats.shape, lambda i, k: (0, 0, 0))]
    operands = [k0, data, mats]
    aliases = {}
    if target is not None:
        in_specs.append(pl.BlockSpec(memory_space=pl.ANY))
        operands.append(target)
        aliases = {3: 0}
    return pl.pallas_call(
        functools.partial(chain_kernel, plan),
        grid_spec=pltpu.PrefetchScalarGridSpec(
            num_scalar_prefetch=1, grid=(1,), in_specs=in_specs, out_specs=out_spec
        ),
        out_shape=out_shape,
        input_output_aliases=aliases,
    )(*operands)


def output_stage(pieces, wave, obs, chunk, w_mat, w_t, o_mat, o_t, step=8):
    part, rank_size, inner_boxes = pieces[0].shape
    piece_spec = pl.BlockSpec((step, rank_size, inner_boxes), lambda i: (i, 0, 0))
    field_spec = pl.BlockSpec(
        (4, None, step, rank_size, inner_boxes), lambda i: (0, chunk, i, 0, 0)
    )
    square = pl.BlockSpec(w_mat.shape, lambda i: (0, 0))
    flops = 4 * 2 * part * inner_boxes * w_mat.shape[0] * w_mat.shape[1]
    moved = part * rank_size * inner_boxes * 4 * (2 + 4 + 2 + 2)
    return pl.pallas_call(
        output_stage_kernel,
        grid=(part // step,),
        in_specs=[piece_spec] * 4 + [field_spec, field_spec] + [square] * 4,
        out_specs=[piece_spec] * 4,
        out_shape=[jax.ShapeDtypeStruct(pieces[0].shape, jnp.bfloat16)] * 4,
        cost_estimate=pl.CostEstimate(
            flops=flops, bytes_accessed=moved, transcendentals=0
        ),
    )(*pieces, wave, obs, w_mat, w_t, o_mat, o_t)


def local(image_tiles, observed, phases, interpolate, local_weights, merge_weights, output_weight):
    groups = image_tiles.shape[2]
    rank_size = image_tiles.shape[3]
    inner_boxes = image_tiles.shape[4]
    local_depth = local_weights.shape[2]
    quarter = groups // 4
    part = quarter // CHUNKS
    levels = local_weights[0, 0]
    merges = merge_weights[0, 0]
    n_x = lax.axis_size("qx")
    n_y = lax.axis_size("qy")
    t = lax.axis_index("qx")
    u = lax.axis_index("qy")
    shifts = [(level_bit(n_x, j, 2), level_bit(n_y, j, 2)) for j in range(2)]
    bits = [
        (jnp.right_shift(t, xs) & 1, jnp.right_shift(u, ys) & 1) for xs, ys in shifts
    ]

    w0 = xor_order(xor_order(merges[0], 1, *bits[0]), 0, *bits[1])
    w1 = xor_order(merges[1], 1, *bits[1])
    w1_mat = jnp.transpose(w1, (0, 2, 1, 3)).reshape(4 * rank_size, 4 * rank_size)
    w1_t = w1_mat.T
    ow_mat = jnp.einsum("st,or->sotr", jnp.eye(4, dtype=output_weight.dtype), output_weight).reshape(4 * rank_size, 4 * rank_size)
    ow_t = ow_mat.T

    shape5 = (4, CHUNKS, part, rank_size, inner_boxes)
    image = image_tiles[0, 0].reshape(shape5)
    obs = observed[0, 0].reshape(shape5)
    wave = phases[0, 0].reshape(shape5)
    k0 = 2 * bits[0][0] + bits[0][1]

    eye = jnp.eye(4, dtype=interpolate.dtype)
    spread = jnp.einsum("st,op->sotp", eye, interpolate).reshape(4 * rank_size, 4 * rank_size)
    side = 4 * rank_size
    forward_levels = jnp.transpose(levels, (0, 1, 3, 2, 4)).reshape(local_depth, side, side)
    forward_mats = jnp.concatenate([spread[None], forward_levels], axis=0)
    adjoint_mats = jnp.concatenate(
        [jnp.swapaxes(forward_levels[::-1], 1, 2), spread.T[None]], axis=0
    )
    forward_plan = [chain_sets(part, 1)] + [chain_sets(part, 4**i) for i in range(local_depth)]
    adjoint_plan = [chain_sets(part, 4**i) for i in reversed(range(local_depth))] + [
        chain_sets(part, 1)
    ]
    k0_ref = jnp.reshape(k0, (1,)).astype(jnp.int32)
    piece_shape = jax.ShapeDtypeStruct((part, rank_size, inner_boxes), jnp.bfloat16)
    whole_piece = pl.BlockSpec((part, rank_size, inner_boxes), lambda i, k: (0, 0, 0))

    def in_place(m, f):
        return pl.BlockSpec(
            (None, None, part, rank_size, inner_boxes),
            lambda i, k: (jnp.bitwise_xor(k[0], f), m, 0, 0, 0),
        )

    def local_forward(m, f):
        return chain_call(
            forward_plan, k0_ref, image, forward_mats, in_place(m, f), piece_shape, whole_piece
        )

    def local_adjoint(gradient, piece, m, f):
        return chain_call(
            adjoint_plan,
            k0_ref,
            piece,
            adjoint_mats,
            whole_piece,
            jax.ShapeDtypeStruct(shape5, jnp.bfloat16),
            in_place(m, f),
            target=gradient,
        )

    gradient = None
    for m in range(CHUNKS):
        coef = [local_forward(m, f) for f in range(4)]
        pieces = exchange(coef, *shifts[0])
        cur = mixing(w0, jnp.stack(pieces), "scor,cjrl->sjol")
        pieces = exchange(cur, *shifts[1])
        terms = output_stage(pieces, wave, obs, m, w1_mat, w1_t, ow_mat, ow_t)
        back = exchange(terms, *shifts[1])
        terms = mixing(w0, jnp.stack(back), "scor,sjol->cjrl")
        back = exchange(terms, *shifts[0])
        for f in range(4):
            gradient = local_adjoint(gradient, back[f], m, f)
    return gradient.reshape(groups, rank_size, inner_boxes)[None, None]


def solution(mesh):
    placed = (
        P("qx", "qy", None, None, None),
        P("qx", "qy", None, None, None),
        P("qx", "qy", None, None, None),
        P(),
        P("qx", "qy", None, None, None, None, None),
        P("qx", "qy", None, None, None, None, None),
        P(),
    )
    return jax.shard_map(
        local,
        mesh=mesh,
        in_specs=placed,
        out_specs=P("qx", "qy", None, None, None),
        check_vma=False,
    )
```

```python
import functools
import math

import jax
import jax.numpy as jnp
from jax import lax
from jax.experimental import pallas as pl
from jax.experimental.pallas import tpu as pltpu
from jax.sharding import PartitionSpec as P

CHUNKS = 2


def mixing(weight, data, form):
    return jnp.einsum(form, weight, data, preferred_element_type=jnp.float32).astype(jnp.bfloat16)


def level_bit(axis_count, level_index, depth):
    total_bits = axis_count.bit_length() - 1
    return level_index * (total_bits - 1) // max(depth - 1, 1)


def xor_order(x, axis, x_bit, y_bit):
    moved = jnp.moveaxis(x, axis, 0)
    shape = moved.shape
    pairs = moved.reshape((2, 2) + shape[1:])
    pairs = jnp.where(y_bit == 1, jnp.flip(pairs, 1), pairs)
    pairs = jnp.where(x_bit == 1, jnp.flip(pairs, 0), pairs)
    return jnp.moveaxis(pairs.reshape(shape), 0, axis)


PI_HI = 3.140625
PI_LO = math.pi - 3.140625


def cas(phase):
    x = phase + jnp.float32(math.pi / 4)
    n = jnp.round(x * jnp.float32(1 / math.pi))
    y = (x - n * jnp.float32(PI_HI)) - n * jnp.float32(PI_LO)
    y2 = y * y
    poly = jnp.float32(-1 / 39916800)
    for k in (9, 7, 5, 3):
        poly = poly * y2 + jnp.float32((-1) ** ((k - 1) // 2) / math.factorial(k))
    sine = y + y * y2 * poly
    odd = jnp.abs(n) == 1
    scale = jnp.where(odd, jnp.float32(-math.sqrt(2.0)), jnp.float32(math.sqrt(2.0)))
    return scale * sine


def flip_send(value, flip, x_shift, y_shift):
    n_x = lax.axis_size("qx")
    n_y = lax.axis_size("qy")
    if flip == 2:
        pairs = [(i, i ^ (1 << x_shift)) for i in range(n_x)]
        return lax.ppermute(value, "qx", pairs)
    if flip == 1:
        pairs = [(i, i ^ (1 << y_shift)) for i in range(n_y)]
        return lax.ppermute(value, "qy", pairs)
    pairs = [
        (t * n_y + u, (t ^ (1 << x_shift)) * n_y + (u ^ (1 << y_shift)))
        for t in range(n_x)
        for u in range(n_y)
    ]
    return lax.ppermute(value, ("qx", "qy"), pairs)


def exchange(relative, x_shift, y_shift):
    return [relative[0]] + [flip_send(relative[f], f, x_shift, y_shift) for f in (1, 2, 3)]


def cas_kernel(phase):
    x = phase + jnp.float32(math.pi / 4)
    n = jnp.floor(x * jnp.float32(1 / math.pi) + jnp.float32(0.5))
    y = (x - n * jnp.float32(PI_HI)) - n * jnp.float32(PI_LO)
    y2 = y * y
    poly = jnp.float32(-1 / 39916800)
    for k in (9, 7, 5, 3):
        poly = poly * y2 + jnp.float32((-1) ** ((k - 1) // 2) / math.factorial(k))
    sine = y + y * y2 * poly
    half = n * jnp.float32(0.5)
    odd = half != jnp.floor(half)
    scale = jnp.where(odd, jnp.float32(-math.sqrt(2.0)), jnp.float32(math.sqrt(2.0)))
    return scale * sine


def output_stage_kernel(p0, p1, p2, p3, ph_ref, obs_ref, w_ref, wt_ref, o_ref, ot_ref,
                        t0, t1, t2, t3):
    size = p0.shape[1]
    rows = 4 * size
    step = p0.shape[0]
    pieces = (p0, p1, p2, p3)
    terms = (t0, t1, t2, t3)

    def wide(parts):
        return jnp.concatenate(parts, axis=1)

    stacked = wide([jnp.concatenate([p[j] for p in pieces], axis=0) for j in range(step)])
    merged = jnp.dot(w_ref[...], stacked, preferred_element_type=jnp.float32)
    merged = merged.astype(jnp.bfloat16)
    predicted = jnp.dot(o_ref[...], merged, preferred_element_type=jnp.float32)
    wave = cas_kernel(wide([ph_ref[:, j].reshape(rows, -1) for j in range(step)]))
    seen = wide([obs_ref[:, j].reshape(rows, -1) for j in range(step)]).astype(jnp.float32)
    residual = (wave * predicted - seen).astype(jnp.bfloat16)
    weighted = (wave * residual.astype(jnp.float32)).astype(jnp.bfloat16)
    back = jnp.dot(ot_ref[...], weighted, preferred_element_type=jnp.float32)
    back = back.astype(jnp.bfloat16)
    out = jnp.dot(wt_ref[...], back, preferred_element_type=jnp.float32)
    out = out.astype(jnp.bfloat16)
    lanes = p0.shape[2]
    for f in range(4):
        for j in range(step):
            terms[f][j] = out[f * size:(f + 1) * size, j * lanes:(j + 1) * lanes]


def chain_stage(cur, matrix, sets):
    size = cur[0].shape[0]
    lanes = cur[0].shape[1]
    wide = jnp.concatenate(
        [jnp.concatenate([cur[g] for g in group], axis=0) for group in sets], axis=1
    )
    mixed = jnp.dot(matrix, wide, preferred_element_type=jnp.float32).astype(jnp.bfloat16)
    out = list(cur)
    for b, group in enumerate(sets):
        for c, g in enumerate(group):
            out[g] = mixed[c * size:(c + 1) * size, b * lanes:(b + 1) * lanes]
    return out


def chain_sets(count, stride):
    return [
        [a * 4 * stride + c * stride + e for c in range(4)]
        for a in range(count // (4 * stride))
        for e in range(stride)
    ]


def chain_kernel(plan, k_ref, x_ref, m_ref, *rest):
    o_ref = rest[-1]
    cur = [x_ref[g] for g in range(x_ref.shape[0])]
    for index, sets in enumerate(plan):
        cur = chain_stage(cur, m_ref[index], sets)
    for g in range(len(cur)):
        o_ref[g] = cur[g]


def chain_call(plan, k0, data, mats, data_spec, out_shape, out_spec, target=None):
    in_specs = [data_spec, pl.BlockSpec(mats.shape, lambda i, k: (0, 0, 0))]
    operands = [k0, data, mats]
    aliases = {}
    if target is not None:
        in_specs.append(pl.BlockSpec(memory_space=pl.ANY))
        operands.append(target)
        aliases = {3: 0}
    return pl.pallas_call(
        functools.partial(chain_kernel, plan),
        grid_spec=pltpu.PrefetchScalarGridSpec(
            num_scalar_prefetch=1, grid=(1,), in_specs=in_specs, out_specs=out_spec
        ),
        out_shape=out_shape,
        input_output_aliases=aliases,
        cost_estimate=pl.CostEstimate(
            flops=2 * len(plan) * mats.shape[1] * mats.shape[2] * data_spec.block_shape[-1]
            * data_spec.block_shape[-3],
            bytes_accessed=mats.size * 2 + 4 * data_spec.block_shape[-1]
            * data_spec.block_shape[-2] * data_spec.block_shape[-3],
            transcendentals=0,
        ),
    )(*operands)


def output_stage(pieces, wave, obs, chunk, w_mat, w_t, o_mat, o_t, step=8):
    part, rank_size, inner_boxes = pieces[0].shape
    piece_spec = pl.BlockSpec((step, rank_size, inner_boxes), lambda i: (i, 0, 0))
    field_spec = pl.BlockSpec(
        (4, None, step, rank_size, inner_boxes), lambda i: (0, chunk, i, 0, 0)
    )
    square = pl.BlockSpec(w_mat.shape, lambda i: (0, 0))
    flops = 4 * 2 * part * inner_boxes * w_mat.shape[0] * w_mat.shape[1]
    moved = part * rank_size * inner_boxes * 4 * (2 + 4 + 2 + 2)
    return pl.pallas_call(
        output_stage_kernel,
        grid=(part // step,),
        in_specs=[piece_spec] * 4 + [field_spec, field_spec] + [square] * 4,
        out_specs=[piece_spec] * 4,
        out_shape=[jax.ShapeDtypeStruct(pieces[0].shape, jnp.bfloat16)] * 4,
        cost_estimate=pl.CostEstimate(
            flops=flops, bytes_accessed=moved, transcendentals=0
        ),
    )(*pieces, wave, obs, w_mat, w_t, o_mat, o_t)


def local(image_tiles, observed, phases, interpolate, local_weights, merge_weights, output_weight):
    groups = image_tiles.shape[2]
    rank_size = image_tiles.shape[3]
    inner_boxes = image_tiles.shape[4]
    local_depth = local_weights.shape[2]
    quarter = groups // 4
    part = quarter // CHUNKS
    levels = local_weights[0, 0]
    merges = merge_weights[0, 0]
    n_x = lax.axis_size("qx")
    n_y = lax.axis_size("qy")
    t = lax.axis_index("qx")
    u = lax.axis_index("qy")
    shifts = [(level_bit(n_x, j, 2), level_bit(n_y, j, 2)) for j in range(2)]
    bits = [
        (jnp.right_shift(t, xs) & 1, jnp.right_shift(u, ys) & 1) for xs, ys in shifts
    ]

    w0 = xor_order(xor_order(merges[0], 1, *bits[0]), 0, *bits[1])
    w1 = xor_order(merges[1], 1, *bits[1])
    w1_mat = jnp.transpose(w1, (0, 2, 1, 3)).reshape(4 * rank_size, 4 * rank_size)
    w1_t = w1_mat.T
    ow_mat = jnp.einsum("st,or->sotr", jnp.eye(4, dtype=output_weight.dtype), output_weight).reshape(4 * rank_size, 4 * rank_size)
    ow_t = ow_mat.T

    shape5 = (4, CHUNKS, part, rank_size, inner_boxes)
    image = image_tiles[0, 0].reshape(shape5)
    obs = observed[0, 0].reshape(shape5)
    wave = phases[0, 0].reshape(shape5)
    k0 = 2 * bits[0][0] + bits[0][1]

    eye = jnp.eye(4, dtype=interpolate.dtype)
    spread = jnp.einsum("st,op->sotp", eye, interpolate).reshape(4 * rank_size, 4 * rank_size)
    forward_levels = [
        jnp.transpose(levels[i], (0, 2, 1, 3)).reshape(4 * rank_size, 4 * rank_size)
        for i in range(local_depth)
    ]
    forward_mats = jnp.stack([spread] + forward_levels)
    adjoint_mats = jnp.stack([w.T for w in reversed(forward_levels)] + [spread.T])
    forward_plan = [chain_sets(part, 1)] + [chain_sets(part, 4**i) for i in range(local_depth)]
    adjoint_plan = [chain_sets(part, 4**i) for i in reversed(range(local_depth))] + [
        chain_sets(part, 1)
    ]
    k0_ref = jnp.reshape(k0, (1,)).astype(jnp.int32)
    piece_shape = jax.ShapeDtypeStruct((part, rank_size, inner_boxes), jnp.bfloat16)
    whole_piece = pl.BlockSpec((part, rank_size, inner_boxes), lambda i, k: (0, 0, 0))

    def in_place(m, f):
        return pl.BlockSpec(
            (None, None, part, rank_size, inner_boxes),
            lambda i, k: (jnp.bitwise_xor(k[0], f), m, 0, 0, 0),
        )

    def local_forward(m, f):
        return chain_call(
            forward_plan, k0_ref, image, forward_mats, in_place(m, f), piece_shape, whole_piece
        )

    def local_adjoint(gradient, piece, m, f):
        return chain_call(
            adjoint_plan,
            k0_ref,
            piece,
            adjoint_mats,
            whole_piece,
            jax.ShapeDtypeStruct(shape5, jnp.bfloat16),
            in_place(m, f),
            target=gradient,
        )

    gradient = None
    for m in range(CHUNKS):
        coef = [local_forward(m, f) for f in range(4)]
        pieces = exchange(coef, *shifts[0])
        cur = mixing(w0, jnp.stack(pieces), "scor,cjrl->sjol")
        pieces = exchange(cur, *shifts[1])
        terms = output_stage(pieces, wave, obs, m, w1_mat, w1_t, ow_mat, ow_t)
        back = exchange(terms, *shifts[1])
        terms = mixing(w0, jnp.stack(back), "scor,sjol->cjrl")
        back = exchange(terms, *shifts[0])
        for f in range(4):
            gradient = local_adjoint(gradient, back[f], m, f)
    return gradient.reshape(groups, rank_size, inner_boxes)[None, None]


def solution(mesh):
    placed = (
        P("qx", "qy", None, None, None),
        P("qx", "qy", None, None, None),
        P("qx", "qy", None, None, None),
        P(),
        P("qx", "qy", None, None, None, None, None),
        P("qx", "qy", None, None, None, None, None),
        P(),
    )
    return jax.shard_map(
        local,
        mesh=mesh,
        in_specs=placed,
        out_specs=P("qx", "qy", None, None, None),
        check_vma=False,
    )
```

```python
import functools
import math

import jax
import jax.numpy as jnp
from jax import lax
from jax.experimental import pallas as pl
from jax.experimental.pallas import tpu as pltpu
from jax.sharding import PartitionSpec as P

CHUNKS = 2


def mixing(weight, data, form):
    return jnp.einsum(form, weight, data, preferred_element_type=jnp.float32).astype(jnp.bfloat16)


def level_bit(axis_count, level_index, depth):
    total_bits = axis_count.bit_length() - 1
    return level_index * (total_bits - 1) // max(depth - 1, 1)


def xor_order(x, axis, x_bit, y_bit):
    moved = jnp.moveaxis(x, axis, 0)
    shape = moved.shape
    pairs = moved.reshape((2, 2) + shape[1:])
    pairs = jnp.where(y_bit == 1, jnp.flip(pairs, 1), pairs)
    pairs = jnp.where(x_bit == 1, jnp.flip(pairs, 0), pairs)
    return jnp.moveaxis(pairs.reshape(shape), 0, axis)


PI_HI = 3.140625
PI_LO = math.pi - 3.140625


def cas(phase):
    x = phase + jnp.float32(math.pi / 4)
    n = jnp.round(x * jnp.float32(1 / math.pi))
    y = (x - n * jnp.float32(PI_HI)) - n * jnp.float32(PI_LO)
    y2 = y * y
    poly = jnp.float32(-1 / 39916800)
    for k in (9, 7, 5, 3):
        poly = poly * y2 + jnp.float32((-1) ** ((k - 1) // 2) / math.factorial(k))
    sine = y + y * y2 * poly
    odd = jnp.abs(n) == 1
    scale = jnp.where(odd, jnp.float32(-math.sqrt(2.0)), jnp.float32(math.sqrt(2.0)))
    return scale * sine


def flip_send(value, flip, x_shift, y_shift):
    n_x = lax.axis_size("qx")
    n_y = lax.axis_size("qy")
    if flip == 2:
        pairs = [(i, i ^ (1 << x_shift)) for i in range(n_x)]
        return lax.ppermute(value, "qx", pairs)
    if flip == 1:
        pairs = [(i, i ^ (1 << y_shift)) for i in range(n_y)]
        return lax.ppermute(value, "qy", pairs)
    pairs = [
        (t * n_y + u, (t ^ (1 << x_shift)) * n_y + (u ^ (1 << y_shift)))
        for t in range(n_x)
        for u in range(n_y)
    ]
    return lax.ppermute(value, ("qx", "qy"), pairs)


def exchange(relative, x_shift, y_shift):
    return [relative[0]] + [flip_send(relative[f], f, x_shift, y_shift) for f in (1, 2, 3)]


def cas_kernel(phase):
    x = phase + jnp.float32(math.pi / 4)
    n = jnp.floor(x * jnp.float32(1 / math.pi) + jnp.float32(0.5))
    y = (x - n * jnp.float32(PI_HI)) - n * jnp.float32(PI_LO)
    y2 = y * y
    poly = jnp.float32(-1 / 39916800)
    for k in (9, 7, 5, 3):
        poly = poly * y2 + jnp.float32((-1) ** ((k - 1) // 2) / math.factorial(k))
    sine = y + y * y2 * poly
    half = n * jnp.float32(0.5)
    odd = half != jnp.floor(half)
    scale = jnp.where(odd, jnp.float32(-math.sqrt(2.0)), jnp.float32(math.sqrt(2.0)))
    return scale * sine


def output_stage_kernel(p0, p1, p2, p3, ph_ref, obs_ref, w_ref, wt_ref, o_ref, ot_ref,
                        t0, t1, t2, t3):
    size = p0.shape[1]
    rows = 4 * size
    step = p0.shape[0]
    pieces = (p0, p1, p2, p3)
    terms = (t0, t1, t2, t3)

    def wide(parts):
        return jnp.concatenate(parts, axis=1)

    stacked = wide([jnp.concatenate([p[j] for p in pieces], axis=0) for j in range(step)])
    merged = jnp.dot(w_ref[...], stacked, preferred_element_type=jnp.float32)
    merged = merged.astype(jnp.bfloat16)
    predicted = jnp.dot(o_ref[...], merged, preferred_element_type=jnp.float32)
    wave = cas_kernel(wide([ph_ref[:, j].reshape(rows, -1) for j in range(step)]))
    seen = wide([obs_ref[:, j].reshape(rows, -1) for j in range(step)]).astype(jnp.float32)
    residual = (wave * predicted - seen).astype(jnp.bfloat16)
    weighted = (wave * residual.astype(jnp.float32)).astype(jnp.bfloat16)
    back = jnp.dot(ot_ref[...], weighted, preferred_element_type=jnp.float32)
    back = back.astype(jnp.bfloat16)
    out = jnp.dot(wt_ref[...], back, preferred_element_type=jnp.float32)
    out = out.astype(jnp.bfloat16)
    lanes = p0.shape[2]
    for f in range(4):
        for j in range(step):
            terms[f][j] = out[f * size:(f + 1) * size, j * lanes:(j + 1) * lanes]


def chain_stage(cur, matrix, sets):
    size = cur[0].shape[0]
    lanes = cur[0].shape[1]
    wide = jnp.concatenate(
        [jnp.concatenate([cur[g] for g in group], axis=0) for group in sets], axis=1
    )
    mixed = jnp.dot(matrix, wide, preferred_element_type=jnp.float32).astype(jnp.bfloat16)
    out = list(cur)
    for b, group in enumerate(sets):
        for c, g in enumerate(group):
            out[g] = mixed[c * size:(c + 1) * size, b * lanes:(b + 1) * lanes]
    return out


def chain_sets(count, stride):
    return [
        [a * 4 * stride + c * stride + e for c in range(4)]
        for a in range(count // (4 * stride))
        for e in range(stride)
    ]


def chain_kernel(plan, k_ref, x_ref, m_ref, *rest):
    o_ref = rest[-1]
    cur = [x_ref[g] for g in range(x_ref.shape[0])]
    for index, sets in enumerate(plan):
        cur = chain_stage(cur, m_ref[index], sets)
    for g in range(len(cur)):
        o_ref[g] = cur[g]


def chain_call(plan, k0, data, mats, data_spec, out_shape, out_spec, target=None):
    in_specs = [data_spec, pl.BlockSpec(mats.shape, lambda i, k: (0, 0, 0))]
    operands = [k0, data, mats]
    aliases = {}
    if target is not None:
        in_specs.append(pl.BlockSpec(memory_space=pl.ANY))
        operands.append(target)
        aliases = {3: 0}
    return pl.pallas_call(
        functools.partial(chain_kernel, plan),
        grid_spec=pltpu.PrefetchScalarGridSpec(
            num_scalar_prefetch=1, grid=(1,), in_specs=in_specs, out_specs=out_spec
        ),
        out_shape=out_shape,
        input_output_aliases=aliases,
    )(*operands)


def output_stage(pieces, wave, obs, chunk, w_mat, w_t, o_mat, o_t, step=16):
    part, rank_size, inner_boxes = pieces[0].shape
    piece_spec = pl.BlockSpec((step, rank_size, inner_boxes), lambda i: (i, 0, 0))
    field_spec = pl.BlockSpec(
        (4, None, step, rank_size, inner_boxes), lambda i: (0, chunk, i, 0, 0)
    )
    square = pl.BlockSpec(w_mat.shape, lambda i: (0, 0))
    flops = 4 * 2 * part * inner_boxes * w_mat.shape[0] * w_mat.shape[1]
    moved = part * rank_size * inner_boxes * 4 * (2 + 4 + 2 + 2)
    return pl.pallas_call(
        output_stage_kernel,
        grid=(part // step,),
        in_specs=[piece_spec] * 4 + [field_spec, field_spec] + [square] * 4,
        out_specs=[piece_spec] * 4,
        out_shape=[jax.ShapeDtypeStruct(pieces[0].shape, jnp.bfloat16)] * 4,
        cost_estimate=pl.CostEstimate(
            flops=flops, bytes_accessed=moved, transcendentals=0
        ),
    )(*pieces, wave, obs, w_mat, w_t, o_mat, o_t)


def local(image_tiles, observed, phases, interpolate, local_weights, merge_weights, output_weight):
    groups = image_tiles.shape[2]
    rank_size = image_tiles.shape[3]
    inner_boxes = image_tiles.shape[4]
    local_depth = local_weights.shape[2]
    quarter = groups // 4
    part = quarter // CHUNKS
    levels = local_weights[0, 0]
    merges = merge_weights[0, 0]
    n_x = lax.axis_size("qx")
    n_y = lax.axis_size("qy")
    t = lax.axis_index("qx")
    u = lax.axis_index("qy")
    shifts = [(level_bit(n_x, j, 2), level_bit(n_y, j, 2)) for j in range(2)]
    bits = [
        (jnp.right_shift(t, xs) & 1, jnp.right_shift(u, ys) & 1) for xs, ys in shifts
    ]

    w0 = xor_order(xor_order(merges[0], 1, *bits[0]), 0, *bits[1])
    w1 = xor_order(merges[1], 1, *bits[1])
    w1_mat = jnp.transpose(w1, (0, 2, 1, 3)).reshape(4 * rank_size, 4 * rank_size)
    w1_t = w1_mat.T
    ow_mat = jnp.einsum("st,or->sotr", jnp.eye(4, dtype=output_weight.dtype), output_weight).reshape(4 * rank_size, 4 * rank_size)
    ow_t = ow_mat.T

    shape5 = (4, CHUNKS, part, rank_size, inner_boxes)
    image = image_tiles[0, 0].reshape(shape5)
    obs = observed[0, 0].reshape(shape5)
    wave = phases[0, 0].reshape(shape5)
    k0 = 2 * bits[0][0] + bits[0][1]

    eye = jnp.eye(4, dtype=interpolate.dtype)
    spread = jnp.einsum("st,op->sotp", eye, interpolate).reshape(4 * rank_size, 4 * rank_size)
    forward_levels = [
        jnp.transpose(levels[i], (0, 2, 1, 3)).reshape(4 * rank_size, 4 * rank_size)
        for i in range(local_depth)
    ]
    forward_mats = jnp.stack([spread] + forward_levels)
    adjoint_mats = jnp.stack([w.T for w in reversed(forward_levels)] + [spread.T])
    forward_plan = [chain_sets(part, 1)] + [chain_sets(part, 4**i) for i in range(local_depth)]
    adjoint_plan = [chain_sets(part, 4**i) for i in reversed(range(local_depth))] + [
        chain_sets(part, 1)
    ]
    k0_ref = jnp.reshape(k0, (1,)).astype(jnp.int32)
    piece_shape = jax.ShapeDtypeStruct((part, rank_size, inner_boxes), jnp.bfloat16)
    whole_piece = pl.BlockSpec((part, rank_size, inner_boxes), lambda i, k: (0, 0, 0))

    def in_place(m, f):
        return pl.BlockSpec(
            (None, None, part, rank_size, inner_boxes),
            lambda i, k: (jnp.bitwise_xor(k[0], f), m, 0, 0, 0),
        )

    def local_forward(m, f):
        return chain_call(
            forward_plan, k0_ref, image, forward_mats, in_place(m, f), piece_shape, whole_piece
        )

    def local_adjoint(gradient, piece, m, f):
        return chain_call(
            adjoint_plan,
            k0_ref,
            piece,
            adjoint_mats,
            whole_piece,
            jax.ShapeDtypeStruct(shape5, jnp.bfloat16),
            in_place(m, f),
            target=gradient,
        )

    gradient = None
    for m in range(CHUNKS):
        coef = [local_forward(m, f) for f in range(4)]
        pieces = exchange(coef, *shifts[0])
        cur = mixing(w0, jnp.stack(pieces), "scor,cjrl->sjol")
        pieces = exchange(cur, *shifts[1])
        terms = output_stage(pieces, wave, obs, m, w1_mat, w1_t, ow_mat, ow_t)
        back = exchange(terms, *shifts[1])
        terms = mixing(w0, jnp.stack(back), "scor,sjol->cjrl")
        back = exchange(terms, *shifts[0])
        for f in range(4):
            gradient = local_adjoint(gradient, back[f], m, f)
    return gradient.reshape(groups, rank_size, inner_boxes)[None, None]


def solution(mesh):
    placed = (
        P("qx", "qy", None, None, None),
        P("qx", "qy", None, None, None),
        P("qx", "qy", None, None, None),
        P(),
        P("qx", "qy", None, None, None, None, None),
        P("qx", "qy", None, None, None, None, None),
        P(),
    )
    return jax.shard_map(
        local,
        mesh=mesh,
        in_specs=placed,
        out_specs=P("qx", "qy", None, None, None),
        check_vma=False,
    )
```

```python
import functools
import math

import jax
import jax.numpy as jnp
from jax import lax
from jax.experimental import pallas as pl
from jax.experimental.pallas import tpu as pltpu
from jax.sharding import PartitionSpec as P

CHUNKS = 2


def mixing(weight, data, form):
    return jnp.einsum(form, weight, data, preferred_element_type=jnp.float32).astype(jnp.bfloat16)


def level_bit(axis_count, level_index, depth):
    total_bits = axis_count.bit_length() - 1
    return level_index * (total_bits - 1) // max(depth - 1, 1)


def xor_order(x, axis, x_bit, y_bit):
    moved = jnp.moveaxis(x, axis, 0)
    shape = moved.shape
    pairs = moved.reshape((2, 2) + shape[1:])
    pairs = jnp.where(y_bit == 1, jnp.flip(pairs, 1), pairs)
    pairs = jnp.where(x_bit == 1, jnp.flip(pairs, 0), pairs)
    return jnp.moveaxis(pairs.reshape(shape), 0, axis)


PI_HI = 3.140625
PI_LO = math.pi - 3.140625


def cas(phase):
    x = phase + jnp.float32(math.pi / 4)
    n = jnp.round(x * jnp.float32(1 / math.pi))
    y = (x - n * jnp.float32(PI_HI)) - n * jnp.float32(PI_LO)
    y2 = y * y
    poly = jnp.float32(-1 / 39916800)
    for k in (9, 7, 5, 3):
        poly = poly * y2 + jnp.float32((-1) ** ((k - 1) // 2) / math.factorial(k))
    sine = y + y * y2 * poly
    odd = jnp.abs(n) == 1
    scale = jnp.where(odd, jnp.float32(-math.sqrt(2.0)), jnp.float32(math.sqrt(2.0)))
    return scale * sine


def flip_send(value, flip, x_shift, y_shift):
    n_x = lax.axis_size("qx")
    n_y = lax.axis_size("qy")
    if flip == 2:
        pairs = [(i, i ^ (1 << x_shift)) for i in range(n_x)]
        return lax.ppermute(value, "qx", pairs)
    if flip == 1:
        pairs = [(i, i ^ (1 << y_shift)) for i in range(n_y)]
        return lax.ppermute(value, "qy", pairs)
    pairs = [
        (t * n_y + u, (t ^ (1 << x_shift)) * n_y + (u ^ (1 << y_shift)))
        for t in range(n_x)
        for u in range(n_y)
    ]
    return lax.ppermute(value, ("qx", "qy"), pairs)


def exchange(relative, x_shift, y_shift):
    return [relative[0]] + [flip_send(relative[f], f, x_shift, y_shift) for f in (1, 2, 3)]


def cas_kernel(phase):
    x = phase + jnp.float32(math.pi / 4)
    n = jnp.floor(x * jnp.float32(1 / math.pi) + jnp.float32(0.5))
    y = (x - n * jnp.float32(PI_HI)) - n * jnp.float32(PI_LO)
    y2 = y * y
    poly = jnp.float32(-1 / 39916800)
    for k in (9, 7, 5, 3):
        poly = poly * y2 + jnp.float32((-1) ** ((k - 1) // 2) / math.factorial(k))
    sine = y + y * y2 * poly
    half = n * jnp.float32(0.5)
    odd = half != jnp.floor(half)
    scale = jnp.where(odd, jnp.float32(-math.sqrt(2.0)), jnp.float32(math.sqrt(2.0)))
    return scale * sine


def output_stage_kernel(p0, p1, p2, p3, ph_ref, obs_ref, w_ref, wt_ref, o_ref, ot_ref,
                        t0, t1, t2, t3):
    size = p0.shape[1]
    rows = 4 * size
    step = p0.shape[0]
    pieces = (p0, p1, p2, p3)
    terms = (t0, t1, t2, t3)

    def wide(parts):
        return jnp.concatenate(parts, axis=1)

    stacked = wide([jnp.concatenate([p[j] for p in pieces], axis=0) for j in range(step)])
    merged = jnp.dot(w_ref[...], stacked, preferred_element_type=jnp.float32)
    merged = merged.astype(jnp.bfloat16)
    predicted = jnp.dot(o_ref[...], merged, preferred_element_type=jnp.float32)
    wave = cas_kernel(wide([ph_ref[:, j].reshape(rows, -1) for j in range(step)]))
    seen = wide([obs_ref[:, j].reshape(rows, -1) for j in range(step)]).astype(jnp.float32)
    residual = (wave * predicted - seen).astype(jnp.bfloat16)
    weighted = (wave * residual.astype(jnp.float32)).astype(jnp.bfloat16)
    back = jnp.dot(ot_ref[...], weighted, preferred_element_type=jnp.float32)
    back = back.astype(jnp.bfloat16)
    out = jnp.dot(wt_ref[...], back, preferred_element_type=jnp.float32)
    out = out.astype(jnp.bfloat16)
    lanes = p0.shape[2]
    for f in range(4):
        for j in range(step):
            terms[f][j] = out[f * size:(f + 1) * size, j * lanes:(j + 1) * lanes]


def chain_stage(cur, matrix, sets):
    size = cur[0].shape[0]
    lanes = cur[0].shape[1]
    wide = jnp.concatenate(
        [jnp.concatenate([cur[g] for g in group], axis=0) for group in sets], axis=1
    )
    mixed = jnp.dot(matrix, wide, preferred_element_type=jnp.float32).astype(jnp.bfloat16)
    out = list(cur)
    for b, group in enumerate(sets):
        for c, g in enumerate(group):
            out[g] = mixed[c * size:(c + 1) * size, b * lanes:(b + 1) * lanes]
    return out


def chain_sets(count, stride):
    return [
        [a * 4 * stride + c * stride + e for c in range(4)]
        for a in range(count // (4 * stride))
        for e in range(stride)
    ]


def chain_kernel(plan, k_ref, x_ref, m_ref, *rest):
    o_ref = rest[-1]
    cur = [x_ref[g] for g in range(x_ref.shape[0])]
    for index, sets in enumerate(plan):
        cur = chain_stage(cur, m_ref[index], sets)
    for g in range(len(cur)):
        o_ref[g] = cur[g]


def chain_call(plan, k0, data, mats, data_spec, out_shape, out_spec, target=None):
    in_specs = [data_spec, pl.BlockSpec(mats.shape, lambda i, k: (0, 0, 0))]
    operands = [k0, data, mats]
    aliases = {}
    if target is not None:
        in_specs.append(pl.BlockSpec(memory_space=pl.ANY))
        operands.append(target)
        aliases = {3: 0}
    return pl.pallas_call(
        functools.partial(chain_kernel, plan),
        grid_spec=pltpu.PrefetchScalarGridSpec(
            num_scalar_prefetch=1, grid=(1,), in_specs=in_specs, out_specs=out_spec
        ),
        out_shape=out_shape,
        input_output_aliases=aliases,
    )(*operands)


def output_stage(pieces, wave, obs, chunk, w_mat, w_t, o_mat, o_t, step=8):
    part, rank_size, inner_boxes = pieces[0].shape
    piece_spec = pl.BlockSpec((step, rank_size, inner_boxes), lambda i: (i, 0, 0))
    field_spec = pl.BlockSpec(
        (4, None, step, rank_size, inner_boxes), lambda i: (0, chunk, i, 0, 0)
    )
    square = pl.BlockSpec(w_mat.shape, lambda i: (0, 0))
    flops = 4 * 2 * part * inner_boxes * w_mat.shape[0] * w_mat.shape[1]
    moved = part * rank_size * inner_boxes * 4 * (2 + 4 + 2 + 2)
    return pl.pallas_call(
        output_stage_kernel,
        grid=(part // step,),
        in_specs=[piece_spec] * 4 + [field_spec, field_spec] + [square] * 4,
        out_specs=[piece_spec] * 4,
        out_shape=[jax.ShapeDtypeStruct(pieces[0].shape, jnp.bfloat16)] * 4,
        cost_estimate=pl.CostEstimate(
            flops=flops, bytes_accessed=moved, transcendentals=0
        ),
    )(*pieces, wave, obs, w_mat, w_t, o_mat, o_t)


def local(image_tiles, observed, phases, interpolate, local_weights, merge_weights, output_weight):
    groups = image_tiles.shape[2]
    rank_size = image_tiles.shape[3]
    inner_boxes = image_tiles.shape[4]
    local_depth = local_weights.shape[2]
    quarter = groups // 4
    part = quarter // CHUNKS
    levels = local_weights[0, 0]
    merges = merge_weights[0, 0]
    n_x = lax.axis_size("qx")
    n_y = lax.axis_size("qy")
    t = lax.axis_index("qx")
    u = lax.axis_index("qy")
    shifts = [(level_bit(n_x, j, 2), level_bit(n_y, j, 2)) for j in range(2)]
    bits = [
        (jnp.right_shift(t, xs) & 1, jnp.right_shift(u, ys) & 1) for xs, ys in shifts
    ]

    w0 = xor_order(xor_order(merges[0], 1, *bits[0]), 0, *bits[1])
    w1 = xor_order(merges[1], 1, *bits[1])
    w1_mat = jnp.transpose(w1, (0, 2, 1, 3)).reshape(4 * rank_size, 4 * rank_size)
    w1_t = w1_mat.T
    ow_mat = jnp.einsum("st,or->sotr", jnp.eye(4, dtype=output_weight.dtype), output_weight).reshape(4 * rank_size, 4 * rank_size)
    ow_t = ow_mat.T

    shape5 = (4, CHUNKS, part, rank_size, inner_boxes)
    image = image_tiles[0, 0].reshape(shape5)
    obs = observed[0, 0].reshape(shape5)
    wave = phases[0, 0].reshape(shape5)
    k0 = 2 * bits[0][0] + bits[0][1]

    eye = jnp.eye(4, dtype=interpolate.dtype)
    spread = jnp.einsum("st,op->sotp", eye, interpolate).reshape(4 * rank_size, 4 * rank_size)
    forward_levels = [
        jnp.transpose(levels[i], (0, 2, 1, 3)).reshape(4 * rank_size, 4 * rank_size)
        for i in range(local_depth)
    ]
    forward_mats = jnp.stack([spread] + forward_levels)
    adjoint_mats = jnp.stack([w.T for w in reversed(forward_levels)] + [spread.T])
    forward_plan = [chain_sets(part, 1)] + [chain_sets(part, 4**i) for i in range(local_depth)]
    adjoint_plan = [chain_sets(part, 4**i) for i in reversed(range(local_depth))] + [
        chain_sets(part, 1)
    ]
    k0_ref = jnp.reshape(k0, (1,)).astype(jnp.int32)
    piece_shape = jax.ShapeDtypeStruct((part, rank_size, inner_boxes), jnp.bfloat16)
    whole_piece = pl.BlockSpec((part, rank_size, inner_boxes), lambda i, k: (0, 0, 0))

    def in_place(m, f):
        return pl.BlockSpec(
            (None, None, part, rank_size, inner_boxes),
            lambda i, k: (jnp.bitwise_xor(k[0], f), m, 0, 0, 0),
        )

    def local_forward(m, f):
        return chain_call(
            forward_plan, k0_ref, image, forward_mats, in_place(m, f), piece_shape, whole_piece
        )

    def local_adjoint(gradient, piece, m, f):
        return chain_call(
            adjoint_plan,
            k0_ref,
            piece,
            adjoint_mats,
            whole_piece,
            jax.ShapeDtypeStruct(shape5, jnp.bfloat16),
            in_place(m, f),
            target=gradient,
        )

    half = part // 2
    half_plan = [chain_sets(half, 4**i) for i in reversed(range(local_depth))] + [
        chain_sets(half, 1)
    ]

    def local_adjoint_half(gradient, piece, m, f, h):
        return chain_call(
            half_plan,
            k0_ref,
            piece,
            adjoint_mats,
            pl.BlockSpec((half, rank_size, inner_boxes), lambda i, k: (0, 0, 0)),
            jax.ShapeDtypeStruct(shape5, jnp.bfloat16),
            pl.BlockSpec(
                (None, None, half, rank_size, inner_boxes),
                lambda i, k: (jnp.bitwise_xor(k[0], f), m, h, 0, 0),
            ),
            target=gradient,
        )

    gradient = None
    for m in range(CHUNKS):
        coef = [local_forward(m, f) for f in range(4)]
        pieces = exchange(coef, *shifts[0])
        cur = mixing(w0, jnp.stack(pieces), "scor,cjrl->sjol")
        pieces = exchange(cur, *shifts[1])
        terms = output_stage(pieces, wave, obs, m, w1_mat, w1_t, ow_mat, ow_t)
        back = exchange(terms, *shifts[1])
        terms = mixing(w0, jnp.stack(back), "scor,sjol->cjrl")
        if m < CHUNKS - 1:
            back = exchange(terms, *shifts[0])
            for f in range(4):
                gradient = local_adjoint(gradient, back[f], m, f)
            continue
        for h in range(2):
            back = exchange(terms[:, h * half:(h + 1) * half], *shifts[0])
            for f in range(4):
                gradient = local_adjoint_half(gradient, back[f], m, f, h)
    return gradient.reshape(groups, rank_size, inner_boxes)[None, None]


def solution(mesh):
    placed = (
        P("qx", "qy", None, None, None),
        P("qx", "qy", None, None, None),
        P("qx", "qy", None, None, None),
        P(),
        P("qx", "qy", None, None, None, None, None),
        P("qx", "qy", None, None, None, None, None),
        P(),
    )
    return jax.shard_map(
        local,
        mesh=mesh,
        in_specs=placed,
        out_specs=P("qx", "qy", None, None, None),
        check_vma=False,
    )
```

```python
import functools
import math

import jax
import jax.numpy as jnp
from jax import lax
from jax.experimental import pallas as pl
from jax.experimental.pallas import tpu as pltpu
from jax.sharding import PartitionSpec as P

CHUNKS = 2


def mixing(weight, data, form):
    return jnp.einsum(form, weight, data, preferred_element_type=jnp.float32).astype(jnp.bfloat16)


def level_bit(axis_count, level_index, depth):
    total_bits = axis_count.bit_length() - 1
    return level_index * (total_bits - 1) // max(depth - 1, 1)


def xor_order(x, axis, x_bit, y_bit):
    moved = jnp.moveaxis(x, axis, 0)
    shape = moved.shape
    pairs = moved.reshape((2, 2) + shape[1:])
    pairs = jnp.where(y_bit == 1, jnp.flip(pairs, 1), pairs)
    pairs = jnp.where(x_bit == 1, jnp.flip(pairs, 0), pairs)
    return jnp.moveaxis(pairs.reshape(shape), 0, axis)


PI_HI = 3.140625
PI_LO = math.pi - 3.140625


def cas(phase):
    x = phase + jnp.float32(math.pi / 4)
    n = jnp.round(x * jnp.float32(1 / math.pi))
    y = (x - n * jnp.float32(PI_HI)) - n * jnp.float32(PI_LO)
    y2 = y * y
    poly = jnp.float32(-1 / 39916800)
    for k in (9, 7, 5, 3):
        poly = poly * y2 + jnp.float32((-1) ** ((k - 1) // 2) / math.factorial(k))
    sine = y + y * y2 * poly
    odd = jnp.abs(n) == 1
    scale = jnp.where(odd, jnp.float32(-math.sqrt(2.0)), jnp.float32(math.sqrt(2.0)))
    return scale * sine


def flip_send(value, flip, x_shift, y_shift):
    n_x = lax.axis_size("qx")
    n_y = lax.axis_size("qy")
    if flip == 2:
        pairs = [(i, i ^ (1 << x_shift)) for i in range(n_x)]
        return lax.ppermute(value, "qx", pairs)
    if flip == 1:
        pairs = [(i, i ^ (1 << y_shift)) for i in range(n_y)]
        return lax.ppermute(value, "qy", pairs)
    pairs = [
        (t * n_y + u, (t ^ (1 << x_shift)) * n_y + (u ^ (1 << y_shift)))
        for t in range(n_x)
        for u in range(n_y)
    ]
    return lax.ppermute(value, ("qx", "qy"), pairs)


def exchange(relative, x_shift, y_shift):
    return [relative[0]] + [flip_send(relative[f], f, x_shift, y_shift) for f in (1, 2, 3)]


def cas_kernel(phase):
    x = phase + jnp.float32(math.pi / 4)
    n = jnp.floor(x * jnp.float32(1 / math.pi) + jnp.float32(0.5))
    y = (x - n * jnp.float32(PI_HI)) - n * jnp.float32(PI_LO)
    y2 = y * y
    poly = jnp.float32(-1 / 39916800)
    for k in (9, 7, 5, 3):
        poly = poly * y2 + jnp.float32((-1) ** ((k - 1) // 2) / math.factorial(k))
    sine = y + y * y2 * poly
    half = n * jnp.float32(0.5)
    odd = half != jnp.floor(half)
    scale = jnp.where(odd, jnp.float32(-math.sqrt(2.0)), jnp.float32(math.sqrt(2.0)))
    return scale * sine


def output_stage_kernel(p0, p1, p2, p3, ph_ref, obs_ref, w_ref, wt_ref, o_ref, ot_ref,
                        t0, t1, t2, t3):
    size = p0.shape[1]
    rows = 4 * size
    step = p0.shape[0]
    pieces = (p0, p1, p2, p3)
    terms = (t0, t1, t2, t3)

    def wide(parts):
        return jnp.concatenate(parts, axis=1)

    stacked = wide([jnp.concatenate([p[j] for p in pieces], axis=0) for j in range(step)])
    merged = jnp.dot(w_ref[...], stacked, preferred_element_type=jnp.float32)
    merged = merged.astype(jnp.bfloat16)
    predicted = jnp.dot(o_ref[...], merged, preferred_element_type=jnp.float32)
    wave = cas_kernel(wide([ph_ref[:, j].reshape(rows, -1) for j in range(step)]))
    seen = wide([obs_ref[:, j].reshape(rows, -1) for j in range(step)]).astype(jnp.float32)
    residual = (wave * predicted - seen).astype(jnp.bfloat16)
    weighted = (wave * residual.astype(jnp.float32)).astype(jnp.bfloat16)
    back = jnp.dot(ot_ref[...], weighted, preferred_element_type=jnp.float32)
    back = back.astype(jnp.bfloat16)
    out = jnp.dot(wt_ref[...], back, preferred_element_type=jnp.float32)
    out = out.astype(jnp.bfloat16)
    lanes = p0.shape[2]
    for f in range(4):
        for j in range(step):
            terms[f][j] = out[f * size:(f + 1) * size, j * lanes:(j + 1) * lanes]


def mix4_kernel(p0, p1, p2, p3, w_ref, t0, t1, t2, t3):
    size = p0.shape[1]
    lanes = p0.shape[2]
    step = p0.shape[0]
    pieces = (p0, p1, p2, p3)
    terms = (t0, t1, t2, t3)
    stacked = jnp.concatenate(
        [jnp.concatenate([p[j] for p in pieces], axis=0) for j in range(step)], axis=1
    )
    out = jnp.dot(w_ref[...], stacked, preferred_element_type=jnp.float32).astype(jnp.bfloat16)
    for f in range(4):
        for j in range(step):
            terms[f][j] = out[f * size:(f + 1) * size, j * lanes:(j + 1) * lanes]


def mix4(pieces, w_mat, step=8):
    part, rank_size, inner_boxes = pieces[0].shape
    piece_spec = pl.BlockSpec((step, rank_size, inner_boxes), lambda i: (i, 0, 0))
    return pl.pallas_call(
        mix4_kernel,
        grid=(part // step,),
        in_specs=[piece_spec] * 4 + [pl.BlockSpec(w_mat.shape, lambda i: (0, 0))],
        out_specs=[piece_spec] * 4,
        out_shape=[jax.ShapeDtypeStruct(pieces[0].shape, jnp.bfloat16)] * 4,
        cost_estimate=pl.CostEstimate(
            flops=2 * part * inner_boxes * w_mat.shape[0] * w_mat.shape[1],
            bytes_accessed=8 * part * rank_size * inner_boxes * 2,
            transcendentals=0,
        ),
    )(*pieces, w_mat)


def chain_stage(cur, matrix, sets):
    size = cur[0].shape[0]
    lanes = cur[0].shape[1]
    wide = jnp.concatenate(
        [jnp.concatenate([cur[g] for g in group], axis=0) for group in sets], axis=1
    )
    mixed = jnp.dot(matrix, wide, preferred_element_type=jnp.float32).astype(jnp.bfloat16)
    out = list(cur)
    for b, group in enumerate(sets):
        for c, g in enumerate(group):
            out[g] = mixed[c * size:(c + 1) * size, b * lanes:(b + 1) * lanes]
    return out


def chain_sets(count, stride):
    return [
        [a * 4 * stride + c * stride + e for c in range(4)]
        for a in range(count // (4 * stride))
        for e in range(stride)
    ]


def chain_kernel(plan, k_ref, x_ref, m_ref, *rest):
    o_ref = rest[-1]
    cur = [x_ref[g] for g in range(x_ref.shape[0])]
    for index, sets in enumerate(plan):
        cur = chain_stage(cur, m_ref[index], sets)
    for g in range(len(cur)):
        o_ref[g] = cur[g]


def chain_call(plan, k0, data, mats, data_spec, out_shape, out_spec, target=None):
    in_specs = [data_spec, pl.BlockSpec(mats.shape, lambda i, k: (0, 0, 0))]
    operands = [k0, data, mats]
    aliases = {}
    if target is not None:
        in_specs.append(pl.BlockSpec(memory_space=pl.ANY))
        operands.append(target)
        aliases = {3: 0}
    return pl.pallas_call(
        functools.partial(chain_kernel, plan),
        grid_spec=pltpu.PrefetchScalarGridSpec(
            num_scalar_prefetch=1, grid=(1,), in_specs=in_specs, out_specs=out_spec
        ),
        out_shape=out_shape,
        input_output_aliases=aliases,
    )(*operands)


def output_stage(pieces, wave, obs, chunk, w_mat, w_t, o_mat, o_t, step=8):
    part, rank_size, inner_boxes = pieces[0].shape
    piece_spec = pl.BlockSpec((step, rank_size, inner_boxes), lambda i: (i, 0, 0))
    field_spec = pl.BlockSpec(
        (4, None, step, rank_size, inner_boxes), lambda i: (0, chunk, i, 0, 0)
    )
    square = pl.BlockSpec(w_mat.shape, lambda i: (0, 0))
    flops = 4 * 2 * part * inner_boxes * w_mat.shape[0] * w_mat.shape[1]
    moved = part * rank_size * inner_boxes * 4 * (2 + 4 + 2 + 2)
    return pl.pallas_call(
        output_stage_kernel,
        grid=(part // step,),
        in_specs=[piece_spec] * 4 + [field_spec, field_spec] + [square] * 4,
        out_specs=[piece_spec] * 4,
        out_shape=[jax.ShapeDtypeStruct(pieces[0].shape, jnp.bfloat16)] * 4,
        cost_estimate=pl.CostEstimate(
            flops=flops, bytes_accessed=moved, transcendentals=0
        ),
    )(*pieces, wave, obs, w_mat, w_t, o_mat, o_t)


def local(image_tiles, observed, phases, interpolate, local_weights, merge_weights, output_weight):
    groups = image_tiles.shape[2]
    rank_size = image_tiles.shape[3]
    inner_boxes = image_tiles.shape[4]
    local_depth = local_weights.shape[2]
    quarter = groups // 4
    part = quarter // CHUNKS
    levels = local_weights[0, 0]
    merges = merge_weights[0, 0]
    n_x = lax.axis_size("qx")
    n_y = lax.axis_size("qy")
    t = lax.axis_index("qx")
    u = lax.axis_index("qy")
    shifts = [(level_bit(n_x, j, 2), level_bit(n_y, j, 2)) for j in range(2)]
    bits = [
        (jnp.right_shift(t, xs) & 1, jnp.right_shift(u, ys) & 1) for xs, ys in shifts
    ]

    w0 = xor_order(xor_order(merges[0], 1, *bits[0]), 0, *bits[1])
    w1 = xor_order(merges[1], 1, *bits[1])
    w1_mat = jnp.transpose(w1, (0, 2, 1, 3)).reshape(4 * rank_size, 4 * rank_size)
    w1_t = w1_mat.T
    w0_mat = jnp.transpose(w0, (0, 2, 1, 3)).reshape(4 * rank_size, 4 * rank_size)
    w0_t = w0_mat.T
    ow_mat = jnp.einsum("st,or->sotr", jnp.eye(4, dtype=output_weight.dtype), output_weight).reshape(4 * rank_size, 4 * rank_size)
    ow_t = ow_mat.T

    shape5 = (4, CHUNKS, part, rank_size, inner_boxes)
    image = image_tiles[0, 0].reshape(shape5)
    obs = observed[0, 0].reshape(shape5)
    wave = phases[0, 0].reshape(shape5)
    k0 = 2 * bits[0][0] + bits[0][1]

    eye = jnp.eye(4, dtype=interpolate.dtype)
    spread = jnp.einsum("st,op->sotp", eye, interpolate).reshape(4 * rank_size, 4 * rank_size)
    forward_levels = [
        jnp.transpose(levels[i], (0, 2, 1, 3)).reshape(4 * rank_size, 4 * rank_size)
        for i in range(local_depth)
    ]
    forward_mats = jnp.stack([spread] + forward_levels)
    adjoint_mats = jnp.stack([w.T for w in reversed(forward_levels)] + [spread.T])
    forward_plan = [chain_sets(part, 1)] + [chain_sets(part, 4**i) for i in range(local_depth)]
    adjoint_plan = [chain_sets(part, 4**i) for i in reversed(range(local_depth))] + [
        chain_sets(part, 1)
    ]
    k0_ref = jnp.reshape(k0, (1,)).astype(jnp.int32)
    piece_shape = jax.ShapeDtypeStruct((part, rank_size, inner_boxes), jnp.bfloat16)
    whole_piece = pl.BlockSpec((part, rank_size, inner_boxes), lambda i, k: (0, 0, 0))

    def in_place(m, f):
        return pl.BlockSpec(
            (None, None, part, rank_size, inner_boxes),
            lambda i, k: (jnp.bitwise_xor(k[0], f), m, 0, 0, 0),
        )

    def local_forward(m, f):
        return chain_call(
            forward_plan, k0_ref, image, forward_mats, in_place(m, f), piece_shape, whole_piece
        )

    def local_adjoint(gradient, piece, m, f):
        return chain_call(
            adjoint_plan,
            k0_ref,
            piece,
            adjoint_mats,
            whole_piece,
            jax.ShapeDtypeStruct(shape5, jnp.bfloat16),
            in_place(m, f),
            target=gradient,
        )

    gradient = None
    for m in range(CHUNKS):
        coef = [local_forward(m, f) for f in range(4)]
        pieces = exchange(coef, *shifts[0])
        cur = mix4(pieces, w0_mat)
        pieces = exchange(cur, *shifts[1])
        terms = output_stage(pieces, wave, obs, m, w1_mat, w1_t, ow_mat, ow_t)
        back = exchange(terms, *shifts[1])
        terms = mix4(back, w0_t)
        back = exchange(terms, *shifts[0])
        for f in range(4):
            gradient = local_adjoint(gradient, back[f], m, f)
    return gradient.reshape(groups, rank_size, inner_boxes)[None, None]


def solution(mesh):
    placed = (
        P("qx", "qy", None, None, None),
        P("qx", "qy", None, None, None),
        P("qx", "qy", None, None, None),
        P(),
        P("qx", "qy", None, None, None, None, None),
        P("qx", "qy", None, None, None, None, None),
        P(),
    )
    return jax.shard_map(
        local,
        mesh=mesh,
        in_specs=placed,
        out_specs=P("qx", "qy", None, None, None),
        check_vma=False,
    )
```
